32 devices in a mesh: grp: 2 (over x), own: 8 (over z, y), shot: 2 (over core).
Axes of the slice: x: 2, y: 2, z: 4, core: 2. Of those that a mesh axis runs over, the one named last changes fastest.
Arguments:
- velocity: bfloat16 [2048, 4, 4, 128], P(('grp', 'own')), parts along dimension 0, may hold values from 1.5 to 4.5
- density: bfloat16 [2048, 4, 4, 128], P(('grp', 'own')), parts along dimension 0, may hold values from 1 to 2.59375
- tile_home: int32 [2048], P('grp'), parts along dimension 0, may hold values from 0 to 1023, as said below
- footprints: int32 [16, 2, 2, 64], P('grp'), parts along dimension 0, may hold values from 0 to 1023, as said below
- source_cell: int32 [16, 2, 2], P(('grp', 'own'), 'shot'), parts along dimension 0, may hold values from 0 to 131071
- source_wave: float32 [16, 2, 2, 2], P(('grp', 'own'), 'shot'), parts along dimension 0, may hold values from -16 to 16
- receivers: int32 [16, 2, 2, 128], P(('grp', 'own'), 'shot'), parts along dimension 0, may hold values from 0 to 131071
- observed: float32 [16, 2, 2, 2, 128], P(('grp', 'own'), 'shot'), parts along dimension 0, may hold values from -6 to 6
- pressure_old: bfloat16 [16, 2, 2, 32, 32, 128], P(('grp', 'own'), 'shot'), parts along dimension 0, may hold values from -6 to 6
- pressure_now: bfloat16 [16, 2, 2, 32, 32, 128], P(('grp', 'own'), 'shot'), parts along dimension 0, may hold values from -6 to 6
- adjoint_next: bfloat16 [16, 2, 2, 32, 32, 128], P(('grp', 'own'), 'shot'), parts along dimension 0, may hold values from -6 to 6
- adjoint_now: bfloat16 [16, 2, 2, 32, 32, 128], P(('grp', 'own'), 'shot'), parts along dimension 0, may hold values from -6 to 6
Outputs:
- velocity_gradient: float32 [2048, 4, 4, 128], P(('grp', 'own'), 'shot'), parts along dimension 0
The draws below stay inside these ranges and needn't reach their ends.
There are 2 independent parts, one for each index of `grp`. The reference program is written for one: setup_inputs(seed, part) draws one part's arguments, and reference() takes and returns one part's arrays. A program takes and returns all parts, laid end to end along the dimension named above; each array names one. Nothing has to cross between parts.
Inputs may be any that keep to these rules, and one draw needn't show every extreme that they name: `tile_home`: a permutation of the rows; a row's owner is row // 128; with tiles numbered row by row over the 32 x 32 grid, every square block of 8 x 8 tiles holds exactly 8 tiles of each owner. `footprints`: each list names the tiles of one square block of 8 x 8 tiles of the grid, row by row.
All inputs are finite; a program needn't handle non-finite values.
Results may differ from the reference program's by a relative error of at most 0.0003.
Values may be sent and summed in bfloat16 or wider, within the bound.
A program may use at most 64 MiB of HBM per device.

```python
import jax
import jax.numpy as jnp
from jax import lax

TX = 4
TY = 4
NZ = 128
GT = 32
FT = 8
SHOTS_DEV = 2
NREC = 128
NTILE = 1024
TPO = 128
FX = 32
FY = 32
CELLS = 131072
N_OWN = 8
N_SHOT = 2


def draw_tile_home(key, part):
    owners = GT * GT // TPO
    exponent = owners.bit_length() - 1
    across = 2 ** ((exponent + 1) // 2)
    along = owners // across
    key_owner, key_local = jax.random.split(jax.random.fold_in(key, 17))
    owner_order = jax.random.permutation(key_owner, owners)
    local_order = jax.random.permutation(key_local, TPO)
    tile_x = jnp.arange(GT)[:, None]
    tile_y = jnp.arange(GT)[None, :]
    owner_of = owner_order[tile_x % across * along + tile_y % along]
    local_of = local_order[tile_x // across * (GT // along) + tile_y // along]
    return (owner_of * TPO + local_of).reshape(-1).astype(jnp.int32)


def draw_footprints(key, part):
    shot_total = N_OWN * N_SHOT * SHOTS_DEV
    key_x, key_y = jax.random.split(jax.random.fold_in(key, 23))
    anchor_x = jax.random.randint(key_x, (shot_total,), 0, GT - FT + 1)
    anchor_y = jax.random.randint(key_y, (shot_total,), 0, GT - FT + 1)
    anchor_x = anchor_x.at[0].set(GT - FT).at[1].set(0)
    anchor_y = anchor_y.at[0].set(GT - FT).at[1].set(0)
    position = jnp.arange(FT * FT)
    tile_lists = (anchor_x[:, None] + position[None, :] // FT) * GT + anchor_y[:, None] + position[None, :] % FT
    return tile_lists.reshape(N_OWN, N_SHOT, SHOTS_DEV, FT * FT).astype(jnp.int32)


def set_ends(entries, key, least, largest):
    longest = entries.shape.index(max(entries.shape))
    spots = []
    for shift in (0, 1):
        where = [jax.random.randint(jax.random.fold_in(key, axis), (), 0, length) for axis, length in enumerate(entries.shape)]
        where[longest] = (where[longest] + shift) % entries.shape[longest]
        spots.append(tuple(where))
    return entries.at[spots[0]].set(least).at[spots[1]].set(largest)


def block_levels(stream_key, extent, cuts, smallest, top_value):
    def one(dim, blocks):
        heights = jax.random.uniform(jax.random.fold_in(jax.random.fold_in(stream_key, 6), dim), (blocks,), jnp.float32, smallest / len(cuts), top_value / len(cuts))
        return jnp.repeat(jnp.exp(heights), extent[dim] // blocks).reshape((-1,) + (1,) * (len(extent) - dim - 1))

    factor_of = one(*cuts[0])
    for cut in cuts[1:]:
        factor_of = factor_of * one(*cut)
    return factor_of


def noise(own_key, extent, scale, most, cuts=(), kind=jnp.bfloat16):
    drawn = scale * jax.random.normal(own_key, extent, jnp.float32)
    if cuts:
        drawn = drawn * block_levels(own_key, extent, cuts, -0.22, 0.18)
    return jnp.clip(drawn, -most, most).astype(kind)


def setup_inputs(seed: int = 0, part: int = 0) -> dict:
    key_list = jax.random.split(jax.random.key(seed), 13)
    part_keys = jax.random.split(jax.random.fold_in(key_list[12], part), 13)
    return {
        "velocity": jnp.clip(1.5 + 3.0 * jax.random.uniform(part_keys[0], (NTILE, TX, TY, NZ), jnp.float32) ** block_levels(part_keys[0], (NTILE, TX, TY, NZ), ((0, 8),), -0.2, 0.2), 1.5, 4.5).astype(jnp.bfloat16),
        "density": jnp.clip(1.0 + 1.59375 * jax.random.uniform(part_keys[1], (NTILE, TX, TY, NZ), jnp.float32) ** block_levels(part_keys[1], (NTILE, TX, TY, NZ), ((0, 8),), -0.2, 0.2), 1.0, 2.59375).astype(jnp.bfloat16),
        "tile_home": draw_tile_home(jax.random.fold_in(jax.random.fold_in(key_list[12], part), 71), part),
        "footprints": draw_footprints(jax.random.fold_in(jax.random.fold_in(key_list[12], part), 71), part),
        "source_cell": set_ends(jax.random.randint(part_keys[4], (N_OWN, N_SHOT, SHOTS_DEV), 0, CELLS), jax.random.fold_in(part_keys[4], 1), 0, CELLS - 1).astype(jnp.int32),
        "source_wave": noise(part_keys[5], (N_OWN, N_SHOT, SHOTS_DEV, 2), 4.0, 16.0, ((0, 8), (1, 2)), jnp.float32),
        "receivers": set_ends(jax.random.randint(part_keys[6], (N_OWN, N_SHOT, SHOTS_DEV, NREC), 0, CELLS), jax.random.fold_in(part_keys[6], 1), 0, CELLS - 1).astype(jnp.int32),
        "observed": noise(part_keys[7], (N_OWN, N_SHOT, SHOTS_DEV, 2, NREC), 1.0, 6.0, ((0, 8), (1, 2)), jnp.float32),
        "pressure_old": noise(part_keys[8], (N_OWN, N_SHOT, SHOTS_DEV, FX, FY, NZ), 1.0, 6.0, ((0, 8), (1, 2))),
        "pressure_now": noise(part_keys[9], (N_OWN, N_SHOT, SHOTS_DEV, FX, FY, NZ), 1.0, 6.0, ((0, 8), (1, 2))),
        "adjoint_next": noise(part_keys[10], (N_OWN, N_SHOT, SHOTS_DEV, FX, FY, NZ), 1.0, 6.0, ((0, 8), (1, 2))),
        "adjoint_now": noise(part_keys[11], (N_OWN, N_SHOT, SHOTS_DEV, FX, FY, NZ), 1.0, 6.0, ((0, 8), (1, 2))),
    }


STENCIL = (1225.0 / 1024.0, -245.0 / 3072.0, 49.0 / 5120.0, -5.0 / 7168.0)
COURANT = 0.09


def take_cells(wavefield, dimension, first_cell, length):
    return lax.slice_in_dim(wavefield, first_cell, first_cell + length, axis=dimension)


def half_buoyancy(buoyancy, dimension):
    length = buoyancy.shape[dimension]
    following = jnp.concatenate([take_cells(buoyancy, dimension, 1, length - 1), take_cells(buoyancy, dimension, length - 1, 1)], axis=dimension)
    return 0.5 * (buoyancy + following)


def pad_along(wavefield, dimension):
    widths = [(4, 4) if index_dim == dimension else (0, 0) for index_dim in range(3)]
    return jnp.pad(wavefield, widths)


def apply_operator(wavefield, half_buoys):
    summed = jnp.zeros_like(wavefield)
    for dimension in range(3):
        length = wavefield.shape[dimension]
        padded = pad_along(wavefield, dimension)
        gradient = jnp.zeros_like(wavefield)
        for position, weight in enumerate(STENCIL):
            distance = position + 1
            gradient = gradient + weight * (take_cells(padded, dimension, 4 + distance, length) - take_cells(padded, dimension, 5 - distance, length))
        flux_pad = pad_along(half_buoys[dimension] * gradient, dimension)
        for position, weight in enumerate(STENCIL):
            distance = position + 1
            summed = summed + weight * (take_cells(flux_pad, dimension, 3 + distance, length) - take_cells(flux_pad, dimension, 4 - distance, length))
    return summed


def inject(wavefield, cell_index, amounts):
    return wavefield.reshape(-1).at[cell_index].add(amounts).reshape(wavefield.shape)


def record(wavefield, cell_index):
    return wavefield.reshape(-1)[cell_index]


def run_shot(velocity, density, pressure_old, pressure_now, adjoint_next, adjoint_now, source_cell, source_wave, receivers, observed):
    coupling = (COURANT * velocity) ** 2 * density
    buoyancy = 1.0 / density
    half_buoys = tuple(half_buoyancy(buoyancy, dimension) for dimension in range(3))
    image_one = apply_operator(pressure_now, half_buoys)
    pressure_two = inject(2.0 * pressure_now - pressure_old + coupling * image_one, source_cell, source_wave[0])
    image_two = apply_operator(pressure_two, half_buoys)
    pressure_three = inject(2.0 * pressure_two - pressure_now + coupling * image_two, source_cell, source_wave[1])
    misfit_one = record(pressure_two, receivers) - observed[0]
    misfit_two = record(pressure_three, receivers) - observed[1]
    adjoint_one = inject(2.0 * adjoint_now - adjoint_next + coupling * apply_operator(adjoint_now, half_buoys), receivers, misfit_two)
    adjoint_zero = inject(2.0 * adjoint_one - adjoint_now + coupling * apply_operator(adjoint_one, half_buoys), receivers, misfit_one)
    return 2.0 * COURANT * COURANT * velocity * density * (adjoint_one * image_two + adjoint_zero * image_one)


def tiles_to_field(tiles, per_side):
    tile_x, tile_y, depth = tiles.shape[1], tiles.shape[2], tiles.shape[3]
    grid = tiles.reshape(per_side, per_side, tile_x, tile_y, depth).transpose(0, 2, 1, 3, 4)
    return grid.reshape(per_side * tile_x, per_side * tile_y, depth)


def field_to_tiles(wavefield, per_side):
    tile_x = wavefield.shape[0] // per_side
    tile_y = wavefield.shape[1] // per_side
    depth = wavefield.shape[2]
    grid = wavefield.reshape(per_side, tile_x, per_side, tile_y, depth).transpose(0, 2, 1, 3, 4)
    return grid.reshape(per_side * per_side, tile_x, tile_y, depth)


def reference(velocity, density, tile_home, footprints, source_cell, source_wave, receivers, observed, pressure_old, pressure_now, adjoint_next, adjoint_now):
    shot_total = N_OWN * N_SHOT * SHOTS_DEV
    field_shape = (shot_total, FT * TX, FT * TY, NZ)
    inputs = (footprints.reshape(shot_total, FT * FT), source_cell.reshape(shot_total), source_wave.reshape(shot_total, 2), receivers.reshape(shot_total, NREC), observed.reshape(shot_total, 2, NREC), pressure_old.reshape(field_shape), pressure_now.reshape(field_shape), adjoint_next.reshape(field_shape), adjoint_now.reshape(field_shape))

    def accumulate(gradient_sum, shot_inputs):
        tile_list, cell_one, wave_one, receiver_list, observed_one, field_old, field_now, field_next, field_adj = shot_inputs
        home_rows = tile_home[tile_list]
        shot_velocity = tiles_to_field(velocity[home_rows], FT).astype(jnp.float32)
        shot_density = tiles_to_field(density[home_rows], FT).astype(jnp.float32)
        shot_gradient = run_shot(shot_velocity, shot_density, field_old.astype(jnp.float32), field_now.astype(jnp.float32), field_next.astype(jnp.float32), field_adj.astype(jnp.float32), cell_one, wave_one, receiver_list, observed_one)
        return gradient_sum.at[home_rows].add(field_to_tiles(shot_gradient, FT)), None

    initial = jnp.zeros((GT * GT, TX, TY, NZ), jnp.float32)
    velocity_gradient, unused = lax.scan(accumulate, initial, inputs)
    return velocity_gradient
```

```python
import functools

import jax
import jax.numpy as jnp
import numpy as np
from jax import lax
from jax.experimental import pallas as pl
from jax.experimental.pallas import tpu as pltpu
from jax.sharding import PartitionSpec as P

COURANT = 0.09
LEAD = 1225.0 / 1024.0
RATIOS = (1.0, -1.0 / 15.0, 1.0 / 125.0, -1.0 / 1715.0)
BAND = 105.0
GROUP = 8
MESH = pl.DeviceIdType.MESH


def difference_matrices(length):
    grad = np.zeros((length, length), np.float32)
    div = np.zeros((length, length), np.float32)
    for i in range(length):
        for m, ratio in enumerate(RATIOS, start=1):
            if i + m < length:
                grad[i, i + m] += BAND * ratio
            if i + 1 - m >= 0:
                grad[i, i + 1 - m] -= BAND * ratio
            if i + m - 1 < length:
                div[i, i + m - 1] += BAND * ratio
            if i - m >= 0:
                div[i, i - m] -= BAND * ratio
    return grad, div


def depth_bands(depth):
    grad, div = difference_matrices(depth)
    return jnp.asarray(np.stack([np.concatenate([a.T, a.T], axis=0) for a in (grad, div)]), jnp.bfloat16)


def line_bands(length):
    return jnp.asarray(np.stack([np.kron(np.eye(GROUP, dtype=np.float32), a) for a in difference_matrices(length)]), jnp.bfloat16)


def scatter_kernel(rows_ref, *refs):
    arrived, out = refs[:-1], refs[-1]
    out[...] = jnp.zeros_like(out)
    for member, ref in enumerate(arrived):
        sources, cap = ref.shape[:2]

        def body(src, carry):
            for j in range(cap):
                row = rows_ref[(member * sources + src) * cap + j]
                out[row] = out[row] + ref[src, j]
            return carry

        lax.fori_loop(0, sources, body, 0)


def lookup(tile_home, footprints):
    side = int(round(tile_home.shape[0] ** 0.5))
    foot = int(round(footprints.shape[-1] ** 0.5))
    first = footprints[..., 0].reshape(-1)
    spot = jnp.arange(foot, dtype=jnp.int32)
    along = jnp.arange(side, dtype=jnp.int32)
    pick_x = ((first // side)[:, None] + spot)[..., None] == along
    pick_y = ((first % side)[:, None] + spot)[..., None] == along
    grid = tile_home.reshape(side, side).astype(jnp.float32)
    lines = jnp.dot(pick_x.astype(jnp.float32).reshape(-1, side), grid, precision=lax.Precision.HIGHEST)
    lines = lines.reshape(first.shape[0], foot, 1, side)
    home = jnp.sum(jnp.where(pick_y[:, None], lines, 0.0), axis=-1)
    return home.astype(jnp.int32).reshape(footprints.shape)


def taps(at, low):
    total = None
    for m, ratio in enumerate(RATIOS, start=1):
        up, down = (at(m), at(1 - m)) if low else (at(m - 1), at(-m))
        if up is None and down is None:
            continue
        diff = up - down if up is not None and down is not None else (up if down is None else -down)
        term = diff if m == 1 else ratio * diff
        total = term if total is None else total + term
    return total


def halves(value):
    high = value.astype(jnp.bfloat16)
    return high, (value - high.astype(jnp.float32)).astype(jnp.bfloat16)


def dot(a, b):
    return jnp.dot(a, b, preferred_element_type=jnp.float32)


def shots_kernel(
    rows_ref, slots_ref, spots_ref, source_ref, cells_ref, wave_ref, obs_ref, lanes_ref,
    vel_hbm, rho_hbm, zband_hbm, yband_hbm, old_hbm, now_hbm, next_hbm, adj_hbm,
    *rest,
):
    members = slots_ref.shape[0]
    arrived, rest = rest[:members], rest[members:]
    models, rest = rest[: 2 * members], rest[2 * members :]
    leaving, rest = rest[: 2 * members], rest[2 * members :]
    outgoing, rest = rest[:members], rest[members:]
    (
        vel_tab, rho_tab, zband, yband, old_ref, now_ref, next_ref, adj_ref,
        rho, vel, buoy, hx, hy, hz, sum_p, sum_q, image_one, adj_one, second, third, image_two, mixed, wide_p, wide_q, tiles,
        misfit,
        load_sems, keep_sems, model_send, model_recv, grad_send, grad_recv,
    ) = rest
    owners, cap = models[0].shape[:2]
    cores = arrived[0].shape[0] // owners
    nx, ny, nz = now_ref.shape[1:]
    grid_y = ny // 4
    tiles_y = ny // 8
    rows = GROUP * ny
    me = lax.axis_index("own")
    whole_me = me * cores + lax.axis_index("shot")
    peers = owners * cores
    lane = lax.broadcasted_iota(jnp.int32, (1, nz), 1)

    loads = [
        pltpu.make_async_copy(src, dst, load_sems.at[i])
        for i, (src, dst) in enumerate((
            (rho_hbm, rho_tab), (vel_hbm, vel_tab), (zband_hbm, zband), (yband_hbm, yband),
            (now_hbm.at[0, 0], now_ref), (adj_hbm.at[0, 0], adj_ref), (old_hbm.at[0, 0], old_ref), (next_hbm.at[0, 0], next_ref),
        ))
    ]
    for load in loads:
        load.start()
    barrier = pltpu.get_barrier_semaphore()

    def device(peer):
        return {"own": peer // cores, "shot": peer % cores}

    def greet(d, carry):
        pl.semaphore_signal(barrier, inc=1, device_id=device((whole_me + d) % peers), device_id_type=MESH)
        return carry

    lax.fori_loop(1, peers, greet, 0)

    def model_copy(phase, d):
        peer = (me + d) % owners
        return pltpu.make_async_remote_copy(
            src_ref=leaving[phase].at[peer], dst_ref=models[phase].at[me],
            send_sem=model_send.at[phase, d], recv_sem=model_recv.at[phase, d],
            device_id={"own": peer}, device_id_type=MESH,
        )

    def grad_copy(member, d):
        peer = (whole_me + d) % peers
        return pltpu.make_async_remote_copy(
            src_ref=outgoing[member].at[peer], dst_ref=arrived[member].at[whole_me],
            send_sem=grad_send.at[member, d], recv_sem=grad_recv.at[member, d],
            device_id=device(peer), device_id_type=MESH,
        )

    def each(count, act):
        def body(d, carry):
            act(d)
            return carry

        lax.fori_loop(1, count, body, 0)

    def collect(table, member, peer, out):
        for j in range(cap):
            out[peer, j] = table[rows_ref[(member * owners + peer) * cap + j]]

    loads[0].wait()
    for phase in range(2 * members):
        member, table = phase // 2, (rho_tab, vel_tab)[phase % 2]
        if phase == 1:
            loads[1].wait()
        if phase == 0:
            each(owners, lambda d: collect(table, member, (me + d) % owners, leaving[phase]))
            pl.semaphore_wait(barrier, peers - 1)
            each(owners, lambda d: model_copy(phase, d).start())
        else:
            def send(d):
                collect(table, member, (me + d) % owners, leaving[phase])
                model_copy(phase, d).start()

            each(owners, send)
        collect(table, member, me, models[phase])

    def unpack(member, arrival, field):
        def body(kx, carry):
            for ky in range(grid_y):
                slot = slots_ref[member, kx * grid_y + ky]
                tile = arrival[slot // cap, slot % cap].astype(jnp.float32)
                for i in range(4):
                    field[kx * 4 + i, pl.ds(ky * 4, 4), :] = tile[4 * i : 4 * i + 4]
            return carry

        lax.fori_loop(0, nx // 4, body, 0)

    def divergence(value, half, transposed):
        high, low = halves(half * value)
        if transposed:
            return dot(jnp.concatenate([yband[1], yband[1]], axis=1), jnp.concatenate([high, low], axis=0))
        return dot(jnp.concatenate([high, low], axis=1), zband[1])

    def planes(ref, g, *lead):
        return ref[(*lead, pl.ds(pl.multiple_of(g * GROUP, GROUP), GROUP))].reshape(rows, nz)

    def lines(first, second_block, first_half, second_half, exact):
        pair = lambda a, b: jnp.concatenate([a, b], axis=1)
        stack = lambda a, b: jnp.concatenate([a, b], axis=0)
        if exact:
            grad_z = dot(stack(first, second_block), zband[0, :nz])
            grad_y = dot(yband[0], pair(first, second_block))
        else:
            (high_a, low_a), (high_b, low_b) = halves(first), halves(second_block)
            grad_z = dot(stack(pair(high_a, low_a), pair(high_b, low_b)), zband[0])
            grad_y = dot(pair(yband[0], yband[0]), stack(pair(high_a, high_b), pair(low_a, low_b)))
        (hy_a, hz_a), (hy_b, hz_b) = first_half, second_half
        div_z = divergence(grad_z, stack(hz_a, hz_b), False)
        div_y = divergence(grad_y, pair(hy_a, hy_b), True)
        return div_z[:rows] + div_y[:, :nz], div_z[rows:] + div_y[:, nz:]

    def cut(g):
        return planes(hy, g), planes(hz, g)

    def put(ref, g, block):
        ref[pl.ds(pl.multiple_of(g * GROUP, GROUP), GROUP)] = block.reshape(GROUP, ny, nz)

    def columns(jobs):
        def body(ty, carry):
            start = pl.multiple_of(ty * 8, 8)
            here = pl.ds(start, 8)
            for load, rest_sum, finish in jobs:
                values, fluxes = {}, {}

                def value_at(x):
                    if x < 0 or x >= nx:
                        return None
                    if x not in values:
                        values[x] = load(x, here)
                    return values[x]

                def flux_at(x):
                    if x < 0 or x >= nx:
                        return None
                    if x not in fluxes:
                        fluxes[x] = hx[x, here, :] * taps(lambda shift: value_at(x + shift), True)
                    return fluxes[x]

                for x in range(nx):
                    total = rest_sum[x, here, :] + taps(lambda shift: flux_at(x + shift), False)
                    finish(x, ty, here, value_at(x), total)
            return carry

        lax.fori_loop(0, tiles_y, body, 0)

    def single(field):
        def body(pair_index, carry):
            g = pair_index * 2
            one, two = lines(planes(field, g), planes(field, g + 1), cut(g), cut(g + 1), False)
            put(sum_p, g, one)
            put(sum_p, g + 1, two)
            return carry

        lax.fori_loop(0, nx // GROUP // 2, body, 0)

    def source_term(member, step, base, shape):
        local = lax.broadcasted_iota(jnp.int32, shape, 0) * nz + lax.broadcasted_iota(jnp.int32, shape, 1)
        return jnp.where(local == source_ref[0, 0, member] - base, wave_ref[0, 0, member, step], 0.0)

    def first_half(member):
        each(owners, lambda d: model_copy(2 * member, d).wait())
        unpack(member, models[2 * member], rho)

        def prepare(x, carry):
            value = (0.5 * LEAD * LEAD) / rho[x]
            buoy[x, pl.ds(0, ny), :] = value
            buoy[x, pl.ds(ny, 1), :] = value[ny - 1 :]
            return carry

        lax.fori_loop(0, nx, prepare, 0, unroll=2)

        def between(x, carry):
            here = buoy[x, pl.ds(0, ny), :]
            hx[x] = here + buoy[jnp.minimum(x + 1, nx - 1), pl.ds(0, ny), :]
            hy[x] = (here + buoy[x, pl.ds(1, ny), :]) * (1.0 / (BAND * BAND))
            shifted = jnp.where(lane == nz - 1, here, pltpu.roll(here, nz - 1, 1))
            hz[x] = (here + shifted) * (1.0 / (BAND * BAND))
            return carry

        lax.fori_loop(0, nx, between, 0, unroll=2)
        if member == 0:
            for load in loads[2:6]:
                load.wait()

        def both(g, carry):
            first, other = planes(now_ref, g, member), planes(adj_ref, g, member)
            put(wide_p, g, first.astype(jnp.float32))
            put(wide_q, g, other.astype(jnp.float32))
            one, two = lines(first, other, cut(g), cut(g), True)
            put(sum_p, g, one)
            put(sum_q, g, two)
            return carry

        lax.fori_loop(0, nx // GROUP, both, 0)

        def keep_p(x, ty, here, value, total):
            image_one[x, here, :] = total

        def keep_q(x, ty, here, value, total):
            adj_one[x, here, :] = total

        columns((
            (lambda x, here: wide_p[x, here, :], sum_p, keep_p),
            (lambda x, here: wide_q[x, here, :], sum_q, keep_q),
        ))

    def second_half(member):
        unpack(member, models[2 * member + 1], vel)
        if member == 0:
            for load in loads[6:]:
                load.wait()
        coupling, weight = vel, rho

        def advance(x, carry):
            velocity, density = vel[x], rho[x]
            scale = (COURANT * velocity) * (COURANT * velocity) * density
            coupling[x] = scale
            weight[x] = (2.0 * COURANT * COURANT) * velocity * density
            wide = lambda ref: ref[member, x].astype(jnp.float32)
            second[x] = 2.0 * wide_p[x] - wide(old_ref) + scale * image_one[x] + source_term(member, 0, x * (ny * nz), (ny, nz))
            adj_one[x] = 2.0 * wide_q[x] - wide(next_ref) + scale * adj_one[x]
            return carry

        lax.fori_loop(0, nx, advance, 0, unroll=2)
        single(second)

        def finish_two(x, ty, here, value, total):
            image_two[x, here, :] = total
            third[x, here, :] = 2.0 * value - wide_p[x, here, :] + coupling[x, here, :] * total + source_term(member, 1, (x * ny + ty * 8) * nz, (8, nz))

        columns(((lambda x, here: second[x, here, :], sum_p, finish_two),))
        count = cells_ref.shape[-1]

        def receive(step, carry):
            for sub in range(8):
                n = step * 8 + sub
                cell = cells_ref[0, 0, member, n]
                row, z = cell // nz, cell % nz
                x, y = row // ny, row % ny
                spot = pl.ds(y, 1)
                pick = lane == z
                misfit[0, pl.ds(n, 1), :] = jnp.where(pick, third[x, spot, :] - obs_ref[0, 0, member, 1, n], 0.0)
                misfit[1, pl.ds(n, 1), :] = jnp.where(pick, second[x, spot, :] - obs_ref[0, 0, member, 0, n], 0.0)
            return carry

        lax.fori_loop(0, count // 8, receive, 0)
        line_of = lanes_ref[0, 0, pl.ds(member, 1), :] // nz
        amounts = jnp.concatenate(halves(jnp.concatenate([misfit[0], misfit[1]], axis=1)), axis=0)

        def deliver(g, carry):
            pick = (lax.broadcasted_iota(jnp.int32, (rows, count), 0) + g * rows == line_of).astype(jnp.float32).astype(jnp.bfloat16)
            added = dot(jnp.concatenate([pick, pick], axis=1), amounts)
            put(adj_one, g, planes(adj_one, g) + added[:, :nz])
            put(mixed, g, added[:, nz:] - planes(wide_q, g))
            return carry

        lax.fori_loop(0, nx // GROUP, deliver, 0)
        single(adj_one)

        def finish_four(x, ty, here, value, total):
            q0 = 2.0 * value + mixed[x, here, :] + coupling[x, here, :] * total
            result = weight[x, here, :] * (value * image_two[x, here, :] + q0 * image_one[x, here, :])
            for half in range(2):
                spot = (x // 4) * grid_y + ty * 2 + half
                tiles[spot, (x % 4) // 2, pl.ds((x % 2) * 4, 4), :] = result[4 * half : 4 * half + 4]

        columns(((lambda x, here: adj_one[x, here, :], sum_p, finish_four),))

        def pack(owner, carry):
            for j in range(cap):
                spot = spots_ref[member, owner * cap + j]
                for core in range(cores):
                    outgoing[member][owner * cores + core, j] = tiles[spot, core]
            return carry

        lax.fori_loop(0, owners, pack, 0)

    keeps = [
        pltpu.make_async_copy(outgoing[member].at[whole_me], arrived[member].at[whole_me], keep_sems.at[member])
        for member in range(members)
    ]

    def dispatch(member):
        each(peers, lambda d: grad_copy(member, d).start())
        keeps[member].start()

    for member in range(members):
        first_half(member)
        each(owners, lambda d: model_copy(2 * member + 1, d).wait())
        if member == members - 1:
            for done in range(members - 1):
                dispatch(done)
        second_half(member)
    dispatch(members - 1)
    for member in range(members):
        each(peers, lambda d: grad_copy(member, d).wait())
        keeps[member].wait()


def per_device(
    velocity, density, tile_home, footprints, source_cell, source_wave, receivers, observed,
    pressure_old, pressure_now, adjoint_next, adjoint_now,
):
    owners = lax.axis_size("own")
    cores = lax.axis_size("shot")
    me = lax.axis_index("own")
    my_core = lax.axis_index("shot")
    held = velocity.shape[0]
    members, foot = footprints.shape[2:]
    cap = foot // owners
    nx, ny, nz = pressure_now.shape[-3:]
    home = lookup(tile_home, footprints)
    slots = jnp.sum((home[..., None, :] < home[..., :, None]).astype(jnp.int32), axis=-1)
    wanted = me * cap + jnp.arange(cap, dtype=jnp.int32)
    row_all = jnp.sum(
        jnp.where(slots[..., None, :] == wanted[:, None], home[..., None, :] - me * held, 0), axis=-1
    )
    row_all = row_all.transpose(2, 0, 1, 3)
    row_mine = lax.dynamic_index_in_dim(row_all, my_core, 2, keepdims=False)
    my_slots = lax.dynamic_index_in_dim(
        lax.dynamic_index_in_dim(slots, me, 0, keepdims=False), my_core, 0, keepdims=False
    )
    every = jnp.arange(foot, dtype=jnp.int32)
    my_spots = jnp.sum(jnp.where(my_slots[:, None, :] == every[:, None], every, 0), axis=-1)
    vmem = pl.BlockSpec(memory_space=pltpu.VMEM)
    smem = pl.BlockSpec(memory_space=pltpu.SMEM)
    hbm = pl.BlockSpec(memory_space=pl.ANY)
    field = pltpu.VMEM((nx, ny, nz), jnp.float32)
    stored = pltpu.VMEM((members, nx, ny, nz), jnp.bfloat16)
    table = pltpu.VMEM((held, 16, nz), jnp.bfloat16)
    model = pltpu.VMEM((owners, cap, 16, nz), jnp.bfloat16)
    grads = (owners * cores, cap, 8, nz)
    zband, yband = depth_bands(nz), line_bands(ny)
    count = receivers.shape[-1]
    dma = pltpu.SemaphoreType.DMA
    arrived = pl.pallas_call(
        shots_kernel,
        out_shape=[jax.ShapeDtypeStruct(grads, jnp.float32)] * members,
        in_specs=[smem] * 7 + [vmem] + [hbm] * 8,
        out_specs=[vmem] * members,
        scratch_shapes=[model] * (4 * members) + [pltpu.VMEM(grads, jnp.float32)] * members + [
            table, table, pltpu.VMEM(zband.shape, jnp.bfloat16), pltpu.VMEM(yband.shape, jnp.bfloat16),
            stored, stored, stored, stored,
            field, field, pltpu.VMEM((nx, ny + 8, nz), jnp.float32)] + [field] * 13 + [
            pltpu.VMEM((foot, 2, 8, nz), jnp.float32), pltpu.VMEM((2, count, nz), jnp.float32),
            dma((8,)), dma((members,)), dma((2 * members, owners)), dma((2 * members, owners)),
            dma((members, owners * cores)), dma((members, owners * cores)),
        ],
        compiler_params=pltpu.CompilerParams(collective_id=0, has_side_effects=True, vmem_limit_bytes=56 * 1024 * 1024),
        cost_estimate=pl.CostEstimate(flops=200_000_000, bytes_accessed=6_000_000, transcendentals=0),
    )(
        row_mine.reshape(-1), my_slots, my_spots, source_cell, receivers, source_wave, observed, receivers,
        velocity.reshape(held, 16, nz), density.reshape(held, 16, nz), zband, yband,
        pressure_old, pressure_now, adjoint_next, adjoint_now,
    )
    gradient = pl.pallas_call(
        scatter_kernel,
        out_shape=jax.ShapeDtypeStruct((held, 8, nz), jnp.float32),
        in_specs=[smem] + [vmem] * members,
        out_specs=vmem,
    )(row_all.reshape(-1), *arrived)
    return gradient.reshape(held, 4 // cores, 4, nz)


def solution(mesh):
    whole = P(("grp", "own"), None, None, None)
    fields = P(("grp", "own"), "shot", None, None, None, None)
    in_specs = (
        whole, whole, P("grp"), P("grp", None, None, None),
        P(("grp", "own"), "shot", None),
        P(("grp", "own"), "shot", None, None),
        P(("grp", "own"), "shot", None, None),
        P(("grp", "own"), "shot", None, None, None),
        fields, fields, fields, fields,
    )
    return jax.shard_map(
        per_device, mesh=mesh, in_specs=in_specs,
        out_specs=P(("grp", "own"), "shot", None, None), check_vma=False,
    )
```

```python
import functools

import jax
import jax.numpy as jnp
import numpy as np
from jax import lax
from jax.experimental import pallas as pl
from jax.experimental.pallas import tpu as pltpu
from jax.sharding import PartitionSpec as P

COURANT = 0.09
LEAD = 1225.0 / 1024.0
RATIOS = (1.0, -1.0 / 15.0, 1.0 / 125.0, -1.0 / 1715.0)
BAND = 105.0
GROUP = 8
CODES = 32760.0
SMALL = 1e-30
MESH = pl.DeviceIdType.MESH


def difference_matrices(length):
    grad = np.zeros((length, length), np.float32)
    div = np.zeros((length, length), np.float32)
    for i in range(length):
        for m, ratio in enumerate(RATIOS, start=1):
            if i + m < length:
                grad[i, i + m] += BAND * ratio
            if i + 1 - m >= 0:
                grad[i, i + 1 - m] -= BAND * ratio
            if i + m - 1 < length:
                div[i, i + m - 1] += BAND * ratio
            if i - m >= 0:
                div[i, i - m] -= BAND * ratio
    return grad, div


def depth_bands(depth):
    grad, div = difference_matrices(depth)
    return jnp.asarray(np.stack([np.concatenate([a.T, a.T], axis=0) for a in (grad, div)]), jnp.bfloat16)


def line_bands(length):
    return jnp.asarray(np.stack([np.kron(np.eye(GROUP, dtype=np.float32), a) for a in difference_matrices(length)]), jnp.bfloat16)


def lookup(tile_home, footprints):
    side = int(round(tile_home.shape[0] ** 0.5))
    foot = int(round(footprints.shape[-1] ** 0.5))
    first = footprints[..., 0].reshape(-1)
    spot = jnp.arange(foot, dtype=jnp.int32)
    along = jnp.arange(side, dtype=jnp.int32)
    pick_x = ((first // side)[:, None] + spot)[..., None] == along
    pick_y = ((first % side)[:, None] + spot)[..., None] == along
    grid = tile_home.reshape(side, side).astype(jnp.float32)
    lines = jnp.dot(pick_x.astype(jnp.float32).reshape(-1, side), grid, precision=lax.Precision.HIGHEST)
    lines = lines.reshape(first.shape[0], foot, 1, side)
    home = jnp.sum(jnp.where(pick_y[:, None], lines, 0.0), axis=-1)
    return home.astype(jnp.int32).reshape(footprints.shape)


def taps(at, low):
    total = None
    for m, ratio in enumerate(RATIOS, start=1):
        up, down = (at(m), at(1 - m)) if low else (at(m - 1), at(-m))
        if up is None and down is None:
            continue
        diff = up - down if up is not None and down is not None else (up if down is None else -down)
        term = diff if m == 1 else ratio * diff
        total = term if total is None else total + term
    return total


def halves(value):
    high = value.astype(jnp.bfloat16)
    return high, (value - high.astype(jnp.float32)).astype(jnp.bfloat16)


def dot(a, b):
    return jnp.dot(a, b, preferred_element_type=jnp.float32)


def shots_kernel(
    rows_ref, slots_ref, spots_ref, source_ref, cells_ref, wave_ref, obs_ref, lanes_ref, homes_ref,
    vel_hbm, rho_hbm, zband_hbm, yband_hbm, old_hbm, now_hbm, next_hbm, adj_hbm,
    out_ref, *rest,
):
    members = slots_ref.shape[0]
    models, rest = rest[: 2 * members], rest[2 * members :]
    leaving, rest = rest[: 2 * members], rest[2 * members :]
    outgoing, rest = rest[:members], rest[members:]
    arrived, rest = rest[:members], rest[members:]
    (
        vel_tab, rho_tab, zband, yband, old_ref, now_ref, next_ref, adj_ref,
        rho, vel, buoy, hx, hy, hz, sum_p, sum_q, image_one, adj_one, second, third, image_two, mixed, wide_p, wide_q, tiles,
        misfit, decoded, scale_out, scale_in,
        load_sems, keep_sems, model_send, model_recv, grad_send, grad_recv, scale_send, scale_recv,
    ) = rest
    owners, cap = models[0].shape[:2]
    cores = lax.axis_size("shot")
    nx, ny, nz = now_ref.shape[1:]
    grid_y = ny // 4
    tiles_y = ny // 8
    rows = GROUP * ny
    me = lax.axis_index("own")
    whole_me = me * cores + lax.axis_index("shot")
    peers = owners * cores
    lane = lax.broadcasted_iota(jnp.int32, (1, nz), 1)

    loads = [
        pltpu.make_async_copy(src, dst, load_sems.at[i])
        for i, (src, dst) in enumerate((
            (rho_hbm, rho_tab), (vel_hbm, vel_tab), (zband_hbm, zband), (yband_hbm, yband),
            (now_hbm.at[0, 0], now_ref), (adj_hbm.at[0, 0], adj_ref), (old_hbm.at[0, 0], old_ref), (next_hbm.at[0, 0], next_ref),
        ))
    ]
    for load in loads:
        load.start()
    barrier = pltpu.get_barrier_semaphore()

    def device(peer):
        return {"own": peer // cores, "shot": peer % cores}

    def greet(d, carry):
        pl.semaphore_signal(barrier, inc=1, device_id=device((whole_me + d) % peers), device_id_type=MESH)
        return carry

    lax.fori_loop(1, peers, greet, 0)

    def model_copy(phase, d):
        peer = (me + d) % owners
        return pltpu.make_async_remote_copy(
            src_ref=leaving[phase].at[peer], dst_ref=models[phase].at[me],
            send_sem=model_send.at[phase, d], recv_sem=model_recv.at[phase, d],
            device_id={"own": peer}, device_id_type=MESH,
        )

    def grad_copy(member, d):
        peer = (whole_me + d) % peers
        return pltpu.make_async_remote_copy(
            src_ref=outgoing[member].at[peer], dst_ref=arrived[member].at[whole_me],
            send_sem=grad_send.at[member, d], recv_sem=grad_recv.at[member, d],
            device_id=device(peer), device_id_type=MESH,
        )

    def scale_copy(member, d):
        peer = (whole_me + d) % peers
        return pltpu.make_async_remote_copy(
            src_ref=scale_out.at[member], dst_ref=scale_in.at[member, whole_me],
            send_sem=scale_send.at[member, d], recv_sem=scale_recv.at[member, d],
            device_id=device(peer), device_id_type=MESH,
        )

    def each(count, act):
        def body(d, carry):
            act(d)
            return carry

        lax.fori_loop(1, count, body, 0)

    def collect(table, member, peer, out):
        for j in range(cap):
            out[peer, j] = table[rows_ref[(member * owners + peer) * cap + j]]

    loads[0].wait()
    for phase in range(2 * members):
        member, table = phase // 2, (rho_tab, vel_tab)[phase % 2]
        if phase == 1:
            loads[1].wait()
        if phase == 0:
            each(owners, lambda d: collect(table, member, (me + d) % owners, leaving[phase]))
            pl.semaphore_wait(barrier, peers - 1)
            each(owners, lambda d: model_copy(phase, d).start())
        else:
            def send(d):
                collect(table, member, (me + d) % owners, leaving[phase])
                model_copy(phase, d).start()

            each(owners, send)
        collect(table, member, me, models[phase])

    def unpack(member, arrival, field):
        def body(kx, carry):
            for ky in range(grid_y):
                slot = slots_ref[member, kx * grid_y + ky]
                tile = arrival[slot // cap, slot % cap].astype(jnp.float32)
                for i in range(4):
                    field[kx * 4 + i, pl.ds(ky * 4, 4), :] = tile[4 * i : 4 * i + 4]
            return carry

        lax.fori_loop(0, nx // 4, body, 0)

    def divergence(value, half, transposed):
        high, low = halves(half * value)
        if transposed:
            return dot(jnp.concatenate([yband[1], yband[1]], axis=1), jnp.concatenate([high, low], axis=0))
        return dot(jnp.concatenate([high, low], axis=1), zband[1])

    def planes(ref, g, *lead):
        return ref[(*lead, pl.ds(pl.multiple_of(g * GROUP, GROUP), GROUP))].reshape(rows, nz)

    def lines(first, second_block, first_half, second_half, exact):
        pair = lambda a, b: jnp.concatenate([a, b], axis=1)
        stack = lambda a, b: jnp.concatenate([a, b], axis=0)
        if exact:
            grad_z = dot(stack(first, second_block), zband[0, :nz])
            grad_y = dot(yband[0], pair(first, second_block))
        else:
            (high_a, low_a), (high_b, low_b) = halves(first), halves(second_block)
            grad_z = dot(stack(pair(high_a, low_a), pair(high_b, low_b)), zband[0])
            grad_y = dot(pair(yband[0], yband[0]), stack(pair(high_a, high_b), pair(low_a, low_b)))
        (hy_a, hz_a), (hy_b, hz_b) = first_half, second_half
        div_z = divergence(grad_z, stack(hz_a, hz_b), False)
        div_y = divergence(grad_y, pair(hy_a, hy_b), True)
        return div_z[:rows] + div_y[:, :nz], div_z[rows:] + div_y[:, nz:]

    def cut(g):
        return planes(hy, g), planes(hz, g)

    def put(ref, g, block):
        ref[pl.ds(pl.multiple_of(g * GROUP, GROUP), GROUP)] = block.reshape(GROUP, ny, nz)

    def columns(jobs):
        def body(ty, peak):
            start = pl.multiple_of(ty * 8, 8)
            here = pl.ds(start, 8)
            for load, rest_sum, finish in jobs:
                values, fluxes = {}, {}

                def value_at(x):
                    if x < 0 or x >= nx:
                        return None
                    if x not in values:
                        values[x] = load(x, here)
                    return values[x]

                def flux_at(x):
                    if x < 0 or x >= nx:
                        return None
                    if x not in fluxes:
                        fluxes[x] = hx[x, here, :] * taps(lambda shift: value_at(x + shift), True)
                    return fluxes[x]

                for x in range(nx):
                    total = rest_sum[x, here, :] + taps(lambda shift: flux_at(x + shift), False)
                    size = finish(x, ty, here, value_at(x), total)
                    if size is not None:
                        peak = jnp.maximum(peak, size)
            return peak

        return lax.fori_loop(0, tiles_y, body, jnp.zeros((8, nz), jnp.float32))

    def single(field):
        def body(pair_index, carry):
            g = pair_index * 2
            one, two = lines(planes(field, g), planes(field, g + 1), cut(g), cut(g + 1), False)
            put(sum_p, g, one)
            put(sum_p, g + 1, two)
            return carry

        lax.fori_loop(0, nx // GROUP // 2, body, 0)

    def source_term(member, step, base, shape):
        local = lax.broadcasted_iota(jnp.int32, shape, 0) * nz + lax.broadcasted_iota(jnp.int32, shape, 1)
        return jnp.where(local == source_ref[0, 0, member] - base, wave_ref[0, 0, member, step], 0.0)

    def first_half(member):
        each(owners, lambda d: model_copy(2 * member, d).wait())
        unpack(member, models[2 * member], rho)

        def prepare(x, carry):
            value = (0.5 * LEAD * LEAD) / rho[x]
            buoy[x, pl.ds(0, ny), :] = value
            buoy[x, pl.ds(ny, 1), :] = value[ny - 1 :]
            return carry

        lax.fori_loop(0, nx, prepare, 0, unroll=2)

        def between(x, carry):
            here = buoy[x, pl.ds(0, ny), :]
            hx[x] = here + buoy[jnp.minimum(x + 1, nx - 1), pl.ds(0, ny), :]
            hy[x] = (here + buoy[x, pl.ds(1, ny), :]) * (1.0 / (BAND * BAND))
            shifted = jnp.where(lane == nz - 1, here, pltpu.roll(here, nz - 1, 1))
            hz[x] = (here + shifted) * (1.0 / (BAND * BAND))
            return carry

        lax.fori_loop(0, nx, between, 0, unroll=2)
        if member == 0:
            for load in loads[2:6]:
                load.wait()

        def both(g, carry):
            first, other = planes(now_ref, g, member), planes(adj_ref, g, member)
            put(wide_p, g, first.astype(jnp.float32))
            put(wide_q, g, other.astype(jnp.float32))
            one, two = lines(first, other, cut(g), cut(g), True)
            put(sum_p, g, one)
            put(sum_q, g, two)
            return carry

        lax.fori_loop(0, nx // GROUP, both, 0)

        def keep_p(x, ty, here, value, total):
            image_one[x, here, :] = total

        def keep_q(x, ty, here, value, total):
            adj_one[x, here, :] = total

        columns((
            (lambda x, here: wide_p[x, here, :], sum_p, keep_p),
            (lambda x, here: wide_q[x, here, :], sum_q, keep_q),
        ))

    def second_half(member):
        unpack(member, models[2 * member + 1], vel)
        if member == 0:
            for load in loads[6:]:
                load.wait()
        coupling, weight = vel, rho

        def advance(x, carry):
            velocity, density = vel[x], rho[x]
            scale = (COURANT * velocity) * (COURANT * velocity) * density
            coupling[x] = scale
            weight[x] = (2.0 * COURANT * COURANT) * velocity * density
            wide = lambda ref: ref[member, x].astype(jnp.float32)
            second[x] = 2.0 * wide_p[x] - wide(old_ref) + scale * image_one[x] + source_term(member, 0, x * (ny * nz), (ny, nz))
            adj_one[x] = 2.0 * wide_q[x] - wide(next_ref) + scale * adj_one[x]
            return carry

        lax.fori_loop(0, nx, advance, 0, unroll=2)
        single(second)

        def finish_two(x, ty, here, value, total):
            image_two[x, here, :] = total
            third[x, here, :] = 2.0 * value - wide_p[x, here, :] + coupling[x, here, :] * total + source_term(member, 1, (x * ny + ty * 8) * nz, (8, nz))

        columns(((lambda x, here: second[x, here, :], sum_p, finish_two),))
        count = cells_ref.shape[-1]

        def receive(step, carry):
            for sub in range(8):
                n = step * 8 + sub
                cell = cells_ref[0, 0, member, n]
                row, z = cell // nz, cell % nz
                x, y = row // ny, row % ny
                spot = pl.ds(y, 1)
                pick = lane == z
                misfit[0, pl.ds(n, 1), :] = jnp.where(pick, third[x, spot, :] - obs_ref[0, 0, member, 1, n], 0.0)
                misfit[1, pl.ds(n, 1), :] = jnp.where(pick, second[x, spot, :] - obs_ref[0, 0, member, 0, n], 0.0)
            return carry

        lax.fori_loop(0, count // 8, receive, 0)
        line_of = lanes_ref[0, 0, pl.ds(member, 1), :] // nz
        amounts = jnp.concatenate(halves(jnp.concatenate([misfit[0], misfit[1]], axis=1)), axis=0)

        def deliver(g, carry):
            pick = (lax.broadcasted_iota(jnp.int32, (rows, count), 0) + g * rows == line_of).astype(jnp.float32).astype(jnp.bfloat16)
            added = dot(jnp.concatenate([pick, pick], axis=1), amounts)
            put(adj_one, g, planes(adj_one, g) + added[:, :nz])
            put(mixed, g, added[:, nz:] - planes(wide_q, g))
            return carry

        lax.fori_loop(0, nx // GROUP, deliver, 0)
        single(adj_one)

        def finish_four(x, ty, here, value, total):
            q0 = 2.0 * value + mixed[x, here, :] + coupling[x, here, :] * total
            result = weight[x, here, :] * (value * image_two[x, here, :] + q0 * image_one[x, here, :])
            size = jnp.abs(result)
            root = result * lax.rsqrt(jnp.maximum(size, SMALL))
            for half in range(2):
                spot = (x // 4) * grid_y + ty * 2 + half
                tiles[spot, (x % 4) // 2, pl.ds((x % 2) * 4, 4), :] = root[4 * half : 4 * half + 4]
            return size

        peak = columns(((lambda x, here: adj_one[x, here, :], sum_p, finish_four),))
        top = jnp.maximum(jnp.max(peak, axis=(0, 1), keepdims=True), SMALL)
        factor = jnp.broadcast_to(CODES * lax.rsqrt(top), (8, nz))
        scale = jnp.broadcast_to(top * (1.0 / (CODES * CODES)), (1, nz))
        scale_out[member] = scale
        scale_in[member, whole_me] = scale

        def pack(owner, carry):
            for core in range(cores):
                parts = []
                for j in range(0, cap):
                    parts.append(jnp.round(tiles[spots_ref[member, owner * cap + j], core] * factor))
                if cap % 2:
                    parts.append(jnp.zeros((8, nz), jnp.float32))
                for j in range(0, len(parts), 2):
                    code = jnp.concatenate(parts[j : j + 2], axis=0).astype(jnp.int32).astype(jnp.int16)
                    outgoing[member][owner * cores + core, pl.ds(8 * j, 16), :] = code
            return carry

        lax.fori_loop(0, owners, pack, 0)

    keeps = [
        pltpu.make_async_copy(outgoing[member].at[whole_me], arrived[member].at[whole_me], keep_sems.at[member])
        for member in range(members)
    ]

    def dispatch(member):
        each(peers, lambda d: scale_copy(member, d).start())
        each(peers, lambda d: grad_copy(member, d).start())
        keeps[member].start()

    def add_up(member):
        each(peers, lambda d: scale_copy(member, d).wait())
        each(peers, lambda d: grad_copy(member, d).wait())
        keeps[member].wait()
        per = cap * 8

        def decode(source, carry):
            code = arrived[member][source].astype(jnp.int32).astype(jnp.float32)[:per]
            decoded[pl.ds(pl.multiple_of(source * per, per), per), :] = code * jnp.abs(code) * scale_in[member, source]
            return carry

        lax.fori_loop(0, peers, decode, 0, unroll=2)
        held = out_ref.shape[0] // 8
        total = peers * cap
        pick = (lax.broadcasted_iota(jnp.int32, (held, total), 0) == homes_ref[pl.ds(member, 1), :]).astype(jnp.float32).astype(jnp.bfloat16)
        pick = jnp.concatenate([pick, pick], axis=1)
        for i in range(8):
            part = dot(pick, jnp.concatenate(halves(decoded[pl.ds(i, total, stride=8), :]), axis=0))
            mine = pl.ds(i, held, stride=8)
            out_ref[mine, :] = part if member == 0 else out_ref[mine, :] + part

    for member in range(members):
        first_half(member)
        each(owners, lambda d: model_copy(2 * member + 1, d).wait())
        if member == members - 1:
            for done in range(members - 1):
                dispatch(done)
        second_half(member)
    dispatch(members - 1)
    for member in range(members):
        add_up(member)


def per_device(
    velocity, density, tile_home, footprints, source_cell, source_wave, receivers, observed,
    pressure_old, pressure_now, adjoint_next, adjoint_now,
):
    owners = lax.axis_size("own")
    cores = lax.axis_size("shot")
    me = lax.axis_index("own")
    my_core = lax.axis_index("shot")
    held = velocity.shape[0]
    members, foot = footprints.shape[2:]
    cap = foot // owners
    nx, ny, nz = pressure_now.shape[-3:]
    home = lookup(tile_home, footprints)
    slots = jnp.sum((home[..., None, :] < home[..., :, None]).astype(jnp.int32), axis=-1)
    wanted = me * cap + jnp.arange(cap, dtype=jnp.int32)
    row_all = jnp.sum(
        jnp.where(slots[..., None, :] == wanted[:, None], home[..., None, :] - me * held, 0), axis=-1
    )
    row_all = row_all.transpose(2, 0, 1, 3)
    row_mine = lax.dynamic_index_in_dim(row_all, my_core, 2, keepdims=False)
    my_slots = lax.dynamic_index_in_dim(
        lax.dynamic_index_in_dim(slots, me, 0, keepdims=False), my_core, 0, keepdims=False
    )
    every = jnp.arange(foot, dtype=jnp.int32)
    my_spots = jnp.sum(jnp.where(my_slots[:, None, :] == every[:, None], every, 0), axis=-1)
    vmem = pl.BlockSpec(memory_space=pltpu.VMEM)
    smem = pl.BlockSpec(memory_space=pltpu.SMEM)
    hbm = pl.BlockSpec(memory_space=pl.ANY)
    field = pltpu.VMEM((nx, ny, nz), jnp.float32)
    stored = pltpu.VMEM((members, nx, ny, nz), jnp.bfloat16)
    table = pltpu.VMEM((held, 16, nz), jnp.bfloat16)
    model = pltpu.VMEM((owners, cap, 16, nz), jnp.bfloat16)
    peers = owners * cores
    grads = pltpu.VMEM((peers, (cap * 8 + 15) // 16 * 16, nz), jnp.int16)
    zband, yband = depth_bands(nz), line_bands(ny)
    count = receivers.shape[-1]
    dma = pltpu.SemaphoreType.DMA
    gradient = pl.pallas_call(
        shots_kernel,
        out_shape=jax.ShapeDtypeStruct((held * 8, nz), jnp.float32),
        in_specs=[smem] * 7 + [vmem] * 2 + [hbm] * 8,
        out_specs=vmem,
        scratch_shapes=[model] * (4 * members) + [grads] * (2 * members) + [
            table, table, pltpu.VMEM(zband.shape, jnp.bfloat16), pltpu.VMEM(yband.shape, jnp.bfloat16),
            stored, stored, stored, stored,
            field, field, pltpu.VMEM((nx, ny + 8, nz), jnp.float32)] + [field] * 13 + [
            pltpu.VMEM((foot, 2, 8, nz), jnp.float32), pltpu.VMEM((2, count, nz), jnp.float32),
            pltpu.VMEM((peers * cap * 8, nz), jnp.float32), pltpu.VMEM((members, 1, nz), jnp.float32), pltpu.VMEM((members, peers, 1, nz), jnp.float32),
            dma((8,)), dma((members,)), dma((2 * members, owners)), dma((2 * members, owners)),
            dma((members, peers)), dma((members, peers)), dma((members, peers)), dma((members, peers)),
        ],
        compiler_params=pltpu.CompilerParams(collective_id=0, has_side_effects=True, vmem_limit_bytes=56 * 1024 * 1024),
        cost_estimate=pl.CostEstimate(flops=200_000_000, bytes_accessed=6_000_000, transcendentals=0),
    )(
        row_mine.reshape(-1), my_slots, my_spots, source_cell, receivers, source_wave, observed, receivers, row_all.reshape(members, -1),
        velocity.reshape(held, 16, nz), density.reshape(held, 16, nz), zband, yband,
        pressure_old, pressure_now, adjoint_next, adjoint_now,
    )
    return gradient.reshape(held, 4 // cores, 4, nz)


def solution(mesh):
    whole = P(("grp", "own"), None, None, None)
    fields = P(("grp", "own"), "shot", None, None, None, None)
    in_specs = (
        whole, whole, P("grp"), P("grp", None, None, None),
        P(("grp", "own"), "shot", None),
        P(("grp", "own"), "shot", None, None),
        P(("grp", "own"), "shot", None, None),
        P(("grp", "own"), "shot", None, None, None),
        fields, fields, fields, fields,
    )
    return jax.shard_map(
        per_device, mesh=mesh, in_specs=in_specs,
        out_specs=P(("grp", "own"), "shot", None, None), check_vma=False,
    )
```

```python
import functools

import jax
import jax.numpy as jnp
import numpy as np
from jax import lax
from jax.experimental import pallas as pl
from jax.experimental.pallas import tpu as pltpu
from jax.sharding import PartitionSpec as P

COURANT = 0.09
LEAD = 1225.0 / 1024.0
RATIOS = (1.0, -1.0 / 15.0, 1.0 / 125.0, -1.0 / 1715.0)
BAND = 105.0
GROUP = 8
LANE_BITS = 7
CODES = 32760.0
SMALL = 1e-30
MESH = pl.DeviceIdType.MESH


def difference_matrices(length):
    grad = np.zeros((length, length), np.float32)
    div = np.zeros((length, length), np.float32)
    for i in range(length):
        for m, ratio in enumerate(RATIOS, start=1):
            if i + m < length:
                grad[i, i + m] += BAND * ratio
            if i + 1 - m >= 0:
                grad[i, i + 1 - m] -= BAND * ratio
            if i + m - 1 < length:
                div[i, i + m - 1] += BAND * ratio
            if i - m >= 0:
                div[i, i - m] -= BAND * ratio
    return grad, div


def depth_bands(depth):
    grad, div = difference_matrices(depth)
    return jnp.asarray(np.stack([np.concatenate([a.T, a.T], axis=0) for a in (grad, div)]), jnp.bfloat16)


def line_bands(length):
    return jnp.asarray(np.stack([np.kron(np.eye(GROUP, dtype=np.float32), a) for a in difference_matrices(length)]), jnp.bfloat16)


def lookup(tile_home, footprints):
    side = int(round(tile_home.shape[0] ** 0.5))
    foot = int(round(footprints.shape[-1] ** 0.5))
    first = footprints[..., 0].reshape(-1)
    spot = jnp.arange(foot, dtype=jnp.int32)
    along = jnp.arange(side, dtype=jnp.int32)
    pick_x = ((first // side)[:, None] + spot)[..., None] == along
    pick_y = ((first % side)[:, None] + spot)[..., None] == along
    grid = tile_home.reshape(side, side).astype(jnp.float32)
    lines = jnp.dot(pick_x.astype(jnp.float32).reshape(-1, side), grid, precision=lax.Precision.HIGHEST)
    lines = lines.reshape(first.shape[0], foot, 1, side)
    home = jnp.sum(jnp.where(pick_y[:, None], lines, 0.0), axis=-1)
    return home.astype(jnp.int32).reshape(footprints.shape)


def taps(at, low):
    total = None
    for m, ratio in enumerate(RATIOS, start=1):
        up, down = (at(m), at(1 - m)) if low else (at(m - 1), at(-m))
        if up is None and down is None:
            continue
        diff = up - down if up is not None and down is not None else (up if down is None else -down)
        term = diff if m == 1 else ratio * diff
        total = term if total is None else total + term
    return total


def halves(value):
    high = value.astype(jnp.bfloat16)
    return high, (value - high.astype(jnp.float32)).astype(jnp.bfloat16)


def dot(a, b):
    return jnp.dot(a, b, preferred_element_type=jnp.float32)


def shots_kernel(
    rows_ref, slots_ref, spots_ref, source_ref, cells_ref, wave_ref, obs_ref, lanes_ref, homes_ref,
    vel_hbm, rho_hbm, zband_hbm, yband_hbm, old_hbm, now_hbm, next_hbm, adj_hbm,
    out_ref, *rest,
):
    members = slots_ref.shape[0]
    models, rest = rest[: 2 * members], rest[2 * members :]
    leaving, rest = rest[: 2 * members], rest[2 * members :]
    outgoing, rest = rest[:members], rest[members:]
    arrived, rest = rest[:members], rest[members:]
    (
        vel_tab, rho_tab, zband, yband, old_ref, now_ref, next_ref, adj_ref,
        rho, vel, buoy, hx, hy, hz, sum_p, sum_q, image_one, adj_one, second, third, image_two, mixed, wide_p, wide_q, tiles,
        misfit, decoded, scale_out, scale_in,
        load_sems, keep_sems, model_send, model_recv, grad_send, grad_recv, scale_send, scale_recv,
    ) = rest
    owners, cap = leaving[0].shape[:2]
    cores = lax.axis_size("shot")
    nx, ny, nz = now_ref.shape[1:]
    grid_y = ny // 4
    tiles_y = ny // 8
    rows = GROUP * ny
    me = lax.axis_index("own")
    whole_me = me * cores + lax.axis_index("shot")
    peers = owners * cores
    lane = lax.broadcasted_iota(jnp.int32, (1, nz), 1)

    loads = [
        pltpu.make_async_copy(src, dst, load_sems.at[i])
        for i, (src, dst) in enumerate((
            (rho_hbm, rho_tab), (vel_hbm, vel_tab), (zband_hbm, zband), (yband_hbm, yband),
            (now_hbm.at[0, 0], now_ref), (adj_hbm.at[0, 0], adj_ref), (old_hbm.at[0, 0], old_ref), (next_hbm.at[0, 0], next_ref),
        ))
    ]
    for load in loads:
        load.start()
    barrier = pltpu.get_barrier_semaphore()

    def device(peer):
        return {"own": peer // cores, "shot": peer % cores}

    def greet(d, carry):
        pl.semaphore_signal(barrier, inc=1, device_id=device((whole_me + d) % peers), device_id_type=MESH)
        return carry

    lax.fori_loop(1, peers, greet, 0)

    def model_copy(phase, d):
        peer = (me + d) % owners
        return pltpu.make_async_remote_copy(
            src_ref=leaving[phase].at[peer], dst_ref=models[phase].at[pl.ds(me * cap, cap)],
            send_sem=model_send.at[phase, d], recv_sem=model_recv.at[phase, d],
            device_id={"own": peer}, device_id_type=MESH,
        )

    def grad_copy(member, d):
        peer = (whole_me + d) % peers
        return pltpu.make_async_remote_copy(
            src_ref=outgoing[member].at[peer], dst_ref=arrived[member].at[whole_me],
            send_sem=grad_send.at[member, d], recv_sem=grad_recv.at[member, d],
            device_id=device(peer), device_id_type=MESH,
        )

    def scale_copy(member, d):
        peer = (whole_me + d) % peers
        return pltpu.make_async_remote_copy(
            src_ref=scale_out.at[member], dst_ref=scale_in.at[member, whole_me],
            send_sem=scale_send.at[member, d], recv_sem=scale_recv.at[member, d],
            device_id=device(peer), device_id_type=MESH,
        )

    def each(count, act):
        def body(d, carry):
            act(d)
            return carry

        lax.fori_loop(1, count, body, 0)

    def collect(table, member, peer, out):
        for j in range(cap):
            tile = table[rows_ref[(member * owners + peer) * cap + j]]
            if len(out.shape) == 4:
                out[peer, j] = tile
            else:
                out[peer * cap + j] = tile

    loads[0].wait()
    for phase in range(2 * members):
        member, table = phase // 2, (rho_tab, vel_tab)[phase % 2]
        if phase == 1:
            loads[1].wait()
        if phase == 0:
            each(owners, lambda d: collect(table, member, (me + d) % owners, leaving[phase]))
            pl.semaphore_wait(barrier, peers - 1)
            each(owners, lambda d: model_copy(phase, d).start())
        else:
            def send(d):
                collect(table, member, (me + d) % owners, leaving[phase])
                model_copy(phase, d).start()

            each(owners, send)
        collect(table, member, me, models[phase])

    def unpack(member, arrival, field):
        def body(kx, carry):
            for ky in range(grid_y):
                slot = slots_ref[member, kx * grid_y + ky]
                tile = arrival[slot].astype(jnp.float32)
                for i in range(4):
                    field[kx * 4 + i, pl.ds(ky * 4, 4), :] = tile[4 * i : 4 * i + 4]
            return carry

        lax.fori_loop(0, nx // 4, body, 0, unroll=2)

    def divergence(value, half, transposed):
        high, low = halves(half * value)
        if transposed:
            return dot(jnp.concatenate([yband[1], yband[1]], axis=1), jnp.concatenate([high, low], axis=0))
        return dot(jnp.concatenate([high, low], axis=1), zband[1])

    def planes(ref, g, *lead):
        return ref[(*lead, pl.ds(pl.multiple_of(g * GROUP, GROUP), GROUP))].reshape(rows, nz)

    def lines(first, second_block, first_half, second_half, exact):
        pair = lambda a, b: jnp.concatenate([a, b], axis=1)
        stack = lambda a, b: jnp.concatenate([a, b], axis=0)
        if exact:
            grad_z = dot(stack(first, second_block), zband[0, :nz])
            grad_y = dot(yband[0], pair(first, second_block))
        else:
            (high_a, low_a), (high_b, low_b) = halves(first), halves(second_block)
            grad_z = dot(stack(pair(high_a, low_a), pair(high_b, low_b)), zband[0])
            grad_y = dot(pair(yband[0], yband[0]), stack(pair(high_a, high_b), pair(low_a, low_b)))
        (hy_a, hz_a), (hy_b, hz_b) = first_half, second_half
        div_z = divergence(grad_z, stack(hz_a, hz_b), False)
        div_y = divergence(grad_y, pair(hy_a, hy_b), True)
        return div_z[:rows] + div_y[:, :nz], div_z[rows:] + div_y[:, nz:]

    def cut(g):
        return planes(hy, g), planes(hz, g)

    def put(ref, g, block):
        ref[pl.ds(pl.multiple_of(g * GROUP, GROUP), GROUP)] = block.reshape(GROUP, ny, nz)

    def columns(jobs):
        def body(ty, peak):
            start = pl.multiple_of(ty * 8, 8)
            here = pl.ds(start, 8)
            for load, rest_sum, finish in jobs:
                values, fluxes = {}, {}

                def value_at(x):
                    if x < 0 or x >= nx:
                        return None
                    if x not in values:
                        values[x] = load(x, here)
                    return values[x]

                def flux_at(x):
                    if x < 0 or x >= nx:
                        return None
                    if x not in fluxes:
                        fluxes[x] = hx[x, here, :] * taps(lambda shift: value_at(x + shift), True)
                    return fluxes[x]

                for x in range(nx):
                    total = rest_sum[x, here, :] + taps(lambda shift: flux_at(x + shift), False)
                    size = finish(x, ty, here, value_at(x), total)
                    if size is not None:
                        peak = jnp.maximum(peak, size)
            return peak

        return lax.fori_loop(0, tiles_y, body, jnp.zeros((8, nz), jnp.float32))

    def single(field):
        def body(pair_index, carry):
            g = pair_index * 2
            one, two = lines(planes(field, g), planes(field, g + 1), cut(g), cut(g + 1), False)
            put(sum_p, g, one)
            put(sum_p, g + 1, two)
            return carry

        lax.fori_loop(0, nx // GROUP // 2, body, 0, unroll=True)

    def source_term(member, step, base, shape):
        local = lax.broadcasted_iota(jnp.int32, shape, 0) * nz + lax.broadcasted_iota(jnp.int32, shape, 1)
        return jnp.where(local == source_ref[0, 0, member] - base, wave_ref[0, 0, member, step], 0.0)

    def first_half(member):
        each(owners, lambda d: model_copy(2 * member, d).wait())
        unpack(member, models[2 * member], rho)

        def prepare(x, carry):
            value = (0.5 * LEAD * LEAD) / rho[x]
            buoy[x, pl.ds(0, ny), :] = value
            buoy[x, pl.ds(ny, 1), :] = value[ny - 1 :]
            return carry

        lax.fori_loop(0, nx, prepare, 0, unroll=4)

        def between(x, carry):
            here = buoy[x, pl.ds(0, ny), :]
            hx[x] = here + buoy[jnp.minimum(x + 1, nx - 1), pl.ds(0, ny), :]
            hy[x] = (here + buoy[x, pl.ds(1, ny), :]) * (1.0 / (BAND * BAND))
            shifted = jnp.where(lane == nz - 1, here, pltpu.roll(here, nz - 1, 1))
            hz[x] = (here + shifted) * (1.0 / (BAND * BAND))
            return carry

        lax.fori_loop(0, nx, between, 0, unroll=8)
        if member == 0:
            for load in loads[2:6]:
                load.wait()

        def both(g, carry):
            first, other = planes(now_ref, g, member), planes(adj_ref, g, member)
            put(wide_p, g, first.astype(jnp.float32))
            put(wide_q, g, other.astype(jnp.float32))
            one, two = lines(first, other, cut(g), cut(g), True)
            put(sum_p, g, one)
            put(sum_q, g, two)
            return carry

        lax.fori_loop(0, nx // GROUP, both, 0, unroll=True)

        def keep_p(x, ty, here, value, total):
            image_one[x, here, :] = total

        def keep_q(x, ty, here, value, total):
            adj_one[x, here, :] = total

        columns((
            (lambda x, here: wide_p[x, here, :], sum_p, keep_p),
            (lambda x, here: wide_q[x, here, :], sum_q, keep_q),
        ))

    def second_half(member):
        unpack(member, models[2 * member + 1], vel)
        if member == 0:
            for load in loads[6:]:
                load.wait()
        coupling, weight = vel, rho

        def advance(x, carry):
            velocity, density = vel[x], rho[x]
            scale = (COURANT * velocity) * (COURANT * velocity) * density
            coupling[x] = scale
            weight[x] = velocity * density
            wide = lambda ref: ref[member, x].astype(jnp.float32)
            second[x] = 2.0 * wide_p[x] - wide(old_ref) + scale * image_one[x] + source_term(member, 0, x * (ny * nz), (ny, nz))
            adj_one[x] = 2.0 * wide_q[x] - wide(next_ref) + scale * adj_one[x]
            return carry

        lax.fori_loop(0, nx, advance, 0, unroll=2)
        single(second)

        def finish_two(x, ty, here, value, total):
            image_two[x, here, :] = total
            third[x, here, :] = 2.0 * value - wide_p[x, here, :] + coupling[x, here, :] * total + source_term(member, 1, (x * ny + ty * 8) * nz, (8, nz))

        columns(((lambda x, here: second[x, here, :], sum_p, finish_two),))
        count = cells_ref.shape[-1]

        def receive(step, carry):
            for sub in range(16):
                n = step * 16 + sub
                line = lax.shift_right_logical(cells_ref[0, 0, member, n], LANE_BITS)
                spot = pl.ds(lax.bitwise_and(line, ny - 1), 1)
                x = lax.shift_right_logical(line, ny.bit_length() - 1)
                misfit[0, pl.ds(n, 1), :] = third[x, spot, :]
                misfit[1, pl.ds(n, 1), :] = second[x, spot, :]
            return carry

        lax.fori_loop(0, count // 16, receive, 0)
        upright = lambda row: jnp.broadcast_to(row, (nz, count)).T
        cells = lanes_ref[0, 0, pl.ds(member, 1), :]
        pick_z = upright((cells & (nz - 1)).astype(jnp.float32)) == lax.broadcasted_iota(jnp.int32, (count, nz), 1).astype(jnp.float32)
        amounts = [
            jnp.where(pick_z, misfit[step] - upright(obs_ref[0, 0, member, pl.ds(1 - step, 1), :]), 0.0) for step in range(2)
        ]
        amounts = jnp.concatenate(halves(jnp.concatenate(amounts, axis=1)), axis=0)
        line_of = lax.shift_right_logical(cells, LANE_BITS)

        def deliver(g, carry):
            pick = (lax.broadcasted_iota(jnp.int32, (rows, count), 0) + g * rows == line_of).astype(jnp.float32).astype(jnp.bfloat16)
            added = dot(jnp.concatenate([pick, pick], axis=1), amounts)
            put(adj_one, g, planes(adj_one, g) + added[:, :nz])
            put(mixed, g, added[:, nz:] - planes(wide_q, g))
            return carry

        lax.fori_loop(0, nx // GROUP, deliver, 0, unroll=True)
        single(adj_one)

        def finish_four(x, ty, here, value, total):
            q0 = 2.0 * value + mixed[x, here, :] + coupling[x, here, :] * total
            result = weight[x, here, :] * (value * image_two[x, here, :] + q0 * image_one[x, here, :])
            size = jnp.abs(result)
            root = result * lax.rsqrt(jnp.maximum(size, SMALL))
            for half in range(2):
                spot = (x // 4) * grid_y + ty * 2 + half
                tiles[spot, (x % 4) // 2, pl.ds((x % 2) * 4, 4), :] = root[4 * half : 4 * half + 4]
            return size

        peak = columns(((lambda x, here: adj_one[x, here, :], sum_p, finish_four),))
        top = jnp.maximum(jnp.max(peak, axis=(0, 1), keepdims=True), SMALL)
        factor = jnp.broadcast_to(CODES * lax.rsqrt(top), (8, nz))
        scale = jnp.broadcast_to(top * (1.0 / (CODES * CODES)), (1, nz))
        scale_out[member] = scale
        scale_in[member, whole_me] = scale

        def pack(owner, carry):
            for core in range(cores):
                parts = []
                for j in range(0, cap):
                    parts.append(jnp.round(tiles[spots_ref[member, owner * cap + j], core] * factor))
                if cap % 2:
                    parts.append(jnp.zeros((8, nz), jnp.float32))
                for j in range(0, len(parts), 2):
                    code = jnp.concatenate(parts[j : j + 2], axis=0).astype(jnp.int32).astype(jnp.int16)
                    outgoing[member][owner * cores + core, pl.ds(8 * j, 16), :] = code
            return carry

        lax.fori_loop(0, owners, pack, 0)

    keeps = [
        pltpu.make_async_copy(outgoing[member].at[whole_me], arrived[member].at[whole_me], keep_sems.at[member])
        for member in range(members)
    ]

    def dispatch(member):
        each(peers, lambda d: scale_copy(member, d).start())
        each(peers, lambda d: grad_copy(member, d).start())
        keeps[member].start()

    def add_up(member):
        each(peers, lambda d: scale_copy(member, d).wait())
        each(peers, lambda d: grad_copy(member, d).wait())
        keeps[member].wait()
        per = cap * 8

        def decode(source, carry):
            code = arrived[member][source].astype(jnp.int32).astype(jnp.float32)[:per]
            decoded[pl.ds(pl.multiple_of(source * per, per), per), :] = code * jnp.abs(code) * scale_in[member, source]
            return carry

        lax.fori_loop(0, peers, decode, 0, unroll=2)
        held = out_ref.shape[0] // 8
        total = peers * cap
        pick = (lax.broadcasted_iota(jnp.int32, (held, total), 0) == homes_ref[pl.ds(member, 1), :]).astype(jnp.float32).astype(jnp.bfloat16)
        pick = jnp.concatenate([pick, pick], axis=1)
        for i in range(8):
            part = dot(pick, jnp.concatenate(halves(decoded[pl.ds(i, total, stride=8), :]), axis=0))
            mine = pl.ds(i, held, stride=8)
            out_ref[mine, :] = part if member == 0 else out_ref[mine, :] + part

    for member in range(members):
        first_half(member)
        each(owners, lambda d: model_copy(2 * member + 1, d).wait())
        if member == members - 1:
            for done in range(members - 1):
                dispatch(done)
        second_half(member)
    dispatch(members - 1)
    for member in range(members):
        add_up(member)


def per_device(
    velocity, density, tile_home, footprints, source_cell, source_wave, receivers, observed,
    pressure_old, pressure_now, adjoint_next, adjoint_now,
):
    owners = lax.axis_size("own")
    cores = lax.axis_size("shot")
    me = lax.axis_index("own")
    my_core = lax.axis_index("shot")
    held = velocity.shape[0]
    members, foot = footprints.shape[2:]
    cap = foot // owners
    nx, ny, nz = pressure_now.shape[-3:]
    home = lookup(tile_home, footprints)
    slots = jnp.sum((home[..., None, :] < home[..., :, None]).astype(jnp.int32), axis=-1)
    wanted = me * cap + jnp.arange(cap, dtype=jnp.int32)
    row_all = jnp.sum(
        jnp.where(slots[..., None, :] == wanted[:, None], home[..., None, :] - me * held, 0), axis=-1
    )
    row_all = row_all.transpose(2, 0, 1, 3)
    row_mine = lax.dynamic_index_in_dim(row_all, my_core, 2, keepdims=False)
    my_slots = lax.dynamic_index_in_dim(
        lax.dynamic_index_in_dim(slots, me, 0, keepdims=False), my_core, 0, keepdims=False
    )
    every = jnp.arange(foot, dtype=jnp.int32)
    my_spots = jnp.sum(jnp.where(my_slots[:, None, :] == every[:, None], every, 0), axis=-1)
    vmem = pl.BlockSpec(memory_space=pltpu.VMEM)
    smem = pl.BlockSpec(memory_space=pltpu.SMEM)
    hbm = pl.BlockSpec(memory_space=pl.ANY)
    field = pltpu.VMEM((nx, ny, nz), jnp.float32)
    stored = pltpu.VMEM((members, nx, ny, nz), jnp.bfloat16)
    table = pltpu.VMEM((held, 16, nz), jnp.bfloat16)
    model = pltpu.VMEM((owners, cap, 16, nz), jnp.bfloat16)
    peers = owners * cores
    grads = pltpu.VMEM((peers, (cap * 8 + 15) // 16 * 16, nz), jnp.int16)
    zband, yband = depth_bands(nz), line_bands(ny)
    count = receivers.shape[-1]
    dma = pltpu.SemaphoreType.DMA
    gradient = pl.pallas_call(
        shots_kernel,
        out_shape=jax.ShapeDtypeStruct((held * 8, nz), jnp.float32),
        in_specs=[smem] * 6 + [vmem] * 3 + [hbm] * 8,
        out_specs=vmem,
        scratch_shapes=[pltpu.VMEM((foot, 16, nz), jnp.bfloat16)] * (2 * members) + [model] * (2 * members) + [grads] * (2 * members) + [
            table, table, pltpu.VMEM(zband.shape, jnp.bfloat16), pltpu.VMEM(yband.shape, jnp.bfloat16),
            stored, stored, stored, stored,
            field, field, pltpu.VMEM((nx, ny + 8, nz), jnp.float32)] + [field] * 13 + [
            pltpu.VMEM((foot, 2, 8, nz), jnp.float32), pltpu.VMEM((2, count, nz), jnp.float32),
            pltpu.VMEM((peers * cap * 8, nz), jnp.float32), pltpu.VMEM((members, 1, nz), jnp.float32), pltpu.VMEM((members, peers, 1, nz), jnp.float32),
            dma((8,)), dma((members,)), dma((2 * members, owners)), dma((2 * members, owners)),
            dma((members, peers)), dma((members, peers)), dma((members, peers)), dma((members, peers)),
        ],
        compiler_params=pltpu.CompilerParams(collective_id=0, has_side_effects=True, vmem_limit_bytes=56 * 1024 * 1024),
        cost_estimate=pl.CostEstimate(flops=200_000_000, bytes_accessed=6_000_000, transcendentals=0),
    )(
        row_mine.reshape(-1), my_slots, my_spots, source_cell, receivers, source_wave, observed, receivers, row_all.reshape(members, -1),
        velocity.reshape(held, 16, nz), density.reshape(held, 16, nz), zband, yband,
        pressure_old, pressure_now, adjoint_next, adjoint_now,
    )
    gradient = gradient * (2.0 * COURANT * COURANT)
    return gradient.reshape(held, 4 // cores, 4, nz)


def solution(mesh):
    whole = P(("grp", "own"), None, None, None)
    fields = P(("grp", "own"), "shot", None, None, None, None)
    in_specs = (
        whole, whole, P("grp"), P("grp", None, None, None),
        P(("grp", "own"), "shot", None),
        P(("grp", "own"), "shot", None, None),
        P(("grp", "own"), "shot", None, None),
        P(("grp", "own"), "shot", None, None, None),
        fields, fields, fields, fields,
    )
    return jax.shard_map(
        per_device, mesh=mesh, in_specs=in_specs,
        out_specs=P(("grp", "own"), "shot", None, None), check_vma=False,
    )
```

```python
import functools

import jax
import jax.numpy as jnp
import numpy as np
from jax import lax
from jax.experimental import pallas as pl
from jax.experimental.pallas import tpu as pltpu
from jax.sharding import PartitionSpec as P

COURANT = 0.09
LEAD = 1225.0 / 1024.0
RATIOS = (1.0, -1.0 / 15.0, 1.0 / 125.0, -1.0 / 1715.0)
BAND = 105.0
GROUP = 8
LANE_BITS = 7
CODES = 32760.0
SMALL = 1e-30
MESH = pl.DeviceIdType.MESH


def difference_matrices(length):
    grad = np.zeros((length, length), np.float32)
    div = np.zeros((length, length), np.float32)
    for i in range(length):
        for m, ratio in enumerate(RATIOS, start=1):
            if i + m < length:
                grad[i, i + m] += BAND * ratio
            if i + 1 - m >= 0:
                grad[i, i + 1 - m] -= BAND * ratio
            if i + m - 1 < length:
                div[i, i + m - 1] += BAND * ratio
            if i - m >= 0:
                div[i, i - m] -= BAND * ratio
    return grad, div


def depth_bands(depth):
    grad, div = difference_matrices(depth)
    return jnp.asarray(np.stack([np.concatenate([a.T, a.T], axis=0) for a in (grad, div)]), jnp.bfloat16)


def line_bands(length):
    return jnp.asarray(np.stack([np.kron(np.eye(GROUP, dtype=np.float32), a) for a in difference_matrices(length)]), jnp.bfloat16)


def taps(at, low):
    total = None
    for m, ratio in enumerate(RATIOS, start=1):
        up, down = (at(m), at(1 - m)) if low else (at(m - 1), at(-m))
        if up is None and down is None:
            continue
        diff = up - down if up is not None and down is not None else (up if down is None else -down)
        term = diff if m == 1 else ratio * diff
        total = term if total is None else total + term
    return total


def halves(value):
    high = value.astype(jnp.bfloat16)
    return high, (value - high.astype(jnp.float32)).astype(jnp.bfloat16)


def dot(a, b):
    return jnp.dot(a, b, preferred_element_type=jnp.float32)


def leave(source, target, sems):
    pieces = sems.shape[0]
    step = source.shape[0] // pieces
    copies = [
        pltpu.make_async_copy(source.at[pl.ds(i * step, step)], target.at[pl.ds(i * step, step)], sems.at[i])
        for i in range(pieces)
    ]
    for copy in copies:
        copy.start()
    for copy in copies:
        copy.wait()


def pass_on(source, target, held, in_sems, out_sems):
    pieces = in_sems.shape[0]
    step = source.shape[0] // pieces
    part = lambda ref, i: ref.at[pl.ds(i * step, step)]
    arrive = [pltpu.make_async_copy(part(source, i), part(held, i), in_sems.at[i]) for i in range(pieces)]
    depart = [pltpu.make_async_copy(part(held, i), part(target, i), out_sems.at[i]) for i in range(pieces)]
    for copy in arrive:
        copy.start()
    for i in range(pieces):
        arrive[i].wait()
        depart[i].start()
    for copy in depart:
        copy.wait()


def shots_kernel(
    foot_ref, source_ref, cells_ref, wave_ref, obs_ref, lanes_ref, home_ref,
    vel_hbm, rho_hbm, zband_hbm, yband_hbm, old_hbm, now_hbm, next_hbm, adj_hbm,
    out_hbm, *rest,
):
    members, foot = foot_ref.shape[2:]
    models, rest = rest[: 2 * members], rest[2 * members :]
    leaving, rest = rest[: 2 * members], rest[2 * members :]
    outgoing, rest = rest[:members], rest[members:]
    arrived, rest = rest[:members], rest[members:]
    (
        vel_tab, rho_tab, zband, yband, old_ref, now_ref, next_ref, adj_ref,
        rho, vel, buoy, hx, hy, hz, sum_p, sum_q, image_one, adj_one, second, third, image_two, mixed, wide_p, wide_q, tiles,
        misfit, decoded, scale_out, scale_in, out_ref, homes_ref, book, rows_ref, lists_ref, table_sems, out_sems,
        load_sems, keep_sems, model_send, model_recv, grad_send, grad_recv, scale_send, scale_recv,
    ) = rest
    owners, cap = leaving[0].shape[:2]
    cores = lax.axis_size("shot")
    nx, ny, nz = now_ref.shape[1:]
    grid_y = ny // 4
    tiles_y = ny // 8
    rows = GROUP * ny
    me = lax.axis_index("own")
    whole_me = me * cores + lax.axis_index("shot")
    peers = owners * cores
    lane = lax.broadcasted_iota(jnp.int32, (1, nz), 1)

    loads = [
        pltpu.make_async_copy(src, dst, load_sems.at[i])
        for i, (src, dst) in enumerate((
            (rho_hbm, rho_tab), (vel_hbm, vel_tab), (zband_hbm, zband), (yband_hbm, yband),
            (now_hbm.at[0, 0], now_ref), (adj_hbm.at[0, 0], adj_ref), (old_hbm.at[0, 0], old_ref), (next_hbm.at[0, 0], next_ref),
        ))
    ]
    for load in loads:
        load.start()
    barrier = pltpu.get_barrier_semaphore()

    def device(peer):
        return {"own": peer // cores, "shot": peer % cores}

    def greet(d, carry):
        pl.semaphore_signal(barrier, inc=1, device_id=device((whole_me + d) % peers), device_id_type=MESH)
        return carry

    lax.fori_loop(1, peers, greet, 0)

    def model_copy(phase, d):
        peer = (me + d) % owners
        return pltpu.make_async_remote_copy(
            src_ref=leaving[phase].at[peer], dst_ref=models[phase].at[pl.ds(me * cap, cap)],
            send_sem=model_send.at[phase, d], recv_sem=model_recv.at[phase, d],
            device_id={"own": peer}, device_id_type=MESH,
        )

    def grad_copy(member, d):
        peer = (whole_me + d) % peers
        return pltpu.make_async_remote_copy(
            src_ref=outgoing[member].at[peer], dst_ref=arrived[member].at[whole_me],
            send_sem=grad_send.at[member, d], recv_sem=grad_recv.at[member, d],
            device_id=device(peer), device_id_type=MESH,
        )

    def scale_copy(member, d):
        peer = (whole_me + d) % peers
        return pltpu.make_async_remote_copy(
            src_ref=scale_out.at[member], dst_ref=scale_in.at[member, whole_me],
            send_sem=scale_send.at[member, d], recv_sem=scale_recv.at[member, d],
            device_id=device(peer), device_id_type=MESH,
        )

    def each(count, act):
        def body(d, carry):
            act(d)
            return carry

        lax.fori_loop(1, count, body, 0)

    held = vel_tab.shape[0]
    count_tiles = home_ref.shape[0] * nz
    side = int(round(count_tiles ** 0.5))
    edge = int(round(foot ** 0.5))
    bits = lambda size: size.bit_length() - 1
    iota = lambda shape, axis: lax.broadcasted_iota(jnp.int32, shape, axis)
    narrow = lambda value: value.astype(jnp.float32).astype(jnp.bfloat16)
    across = lambda a, b: lax.dot_general(a, b, (((1,), (1,)), ((), ())), preferred_element_type=jnp.float32)
    blocks = home_ref.shape[0]

    def locate():
        home = home_ref[...]
        high, low = lax.shift_right_logical(home, LANE_BITS), home & (nz - 1)
        hit, full, own = [], [], []
        mine = lax.shift_right_logical(me * held, LANE_BITS)
        for i in range(blocks):
            tile = i * nz + iota((1, nz), 1)
            where = lax.shift_right_logical(tile, bits(side)), tile & (side - 1)
            hit.append(narrow(low[i : i + 1] == iota((nz, nz), 0)))
            high_row = high[i : i + 1]
            full.append(narrow(jnp.concatenate([jnp.where(high_row == iota((blocks, nz), 0), w, 0) for w in where], axis=0)))
            own.append(narrow(jnp.concatenate([jnp.broadcast_to(jnp.where(high_row == mine, w, 0), (nz, nz)) for w in where], axis=0)))
        hit, full, own = (jnp.concatenate(parts, axis=1) for parts in (hit, full, own))
        return across(full, hit).astype(jnp.int32), across(hit, own).astype(jnp.int32)

    def inside(dx, dy):
        return (dx >= 0) & (dx < edge) & (dy >= 0) & (dy < edge)

    def first_of(owner, core, member):
        first = foot_ref[owner, core, member, 0]
        return lax.shift_right_logical(first, bits(side)), first & (side - 1)

    total = peers * cap
    share = bits(held)
    spot_x, spot_y = iota((nz, nz), 0), iota((nz, nz), 1)
    same = lax.shift_right_logical(spot_x, share) == lax.shift_right_logical(spot_y, share)
    positions, own_positions = locate()
    book[...] = jnp.zeros_like(book)
    in_share = lax.shift_right_logical(iota((nz, total), 0), share) == me % (nz >> share)
    before = narrow(same & (spot_y < spot_x))
    for member in range(members):
        first = jnp.zeros((1, total), jnp.int32)
        shot_of = lax.shift_right_logical(iota((1, total), 1), bits(cap))
        for peer in range(peers):
            first = jnp.where(shot_of == peer, foot_ref[peer // cores, peer % cores, member, 0], first)
        dx = own_positions[:, :nz] - lax.shift_right_logical(first, bits(side))
        dy = own_positions[:, nz:] - (first & (side - 1))
        chosen = inside(dx, dy) & in_share
        order = dot(before, narrow(chosen)).astype(jnp.int32)
        chosen = chosen & (order == (iota((1, total), 1) & (cap - 1)))
        local = jnp.where(chosen, iota((nz, total), 0) & (held - 1), 0)
        homes = jnp.clip(jnp.sum(local, axis=0, keepdims=True), 0, held - 1)
        homes_ref[pl.ds(member, 1), :] = homes
        book[pl.ds(member, 1), :] = homes
    rows_copy = pltpu.make_async_copy(book.at[pl.ds(0, 8)], rows_ref, table_sems.at[0])
    lists_copy = pltpu.make_async_copy(book.at[pl.ds(8, book.shape[0] - 8)], lists_ref, table_sems.at[1])
    rows_copy.start()

    def list_tiles():
        after = narrow(same & (spot_x < spot_y))
        keys, values = [], []
        cell = iota((blocks, nz), 0) * nz + iota((blocks, nz), 1)
        owner = lax.shift_right_logical(cell, share)
        for member in range(members):
            at_x, at_y = first_of(me, lax.axis_index("shot"), member)
            dx, dy = positions[:blocks] - at_x, positions[blocks:] - at_y
            chosen = inside(dx, dy)
            order = dot(narrow(chosen), after).astype(jnp.int32)
            slot = owner * cap + order
            key, value = [], []
            for i in range(blocks):
                row = lambda field: field[i : i + 1]
                valid = row(chosen.astype(jnp.int32)) == 1
                small = iota((8, nz), 0)
                key.append(narrow(jnp.concatenate([
                    jnp.where(valid & (row(dx) == small), 1, 0),
                    jnp.where(valid & (row(owner) == iota((owners, nz), 0)), 1, 0),
                ], axis=0)))
                value.append(narrow(jnp.concatenate([
                    jnp.where(row(dy) == small, row(slot), 0),
                    jnp.where(row(order) == small, row(dx) * edge + row(dy), 0),
                ], axis=0)))
            keys.append(jnp.concatenate(key, axis=1))
            values.append(jnp.concatenate(value, axis=1))
        values.append(jnp.zeros((nz - 16 * members, blocks * nz), jnp.bfloat16))
        found = across(jnp.concatenate(keys, axis=0), jnp.concatenate(values, axis=0)).astype(jnp.int32)
        book[pl.ds(8, found.shape[0]), :] = jnp.clip(found, 0, foot - 1)
        lists_copy.start()

    def slot_at(member, kx, ky):
        return lists_ref[member * (8 + owners) + kx, member * 16 + ky]

    def spot_at(member, owner, j):
        return lists_ref[member * (8 + owners) + 8 + owner, member * 16 + 8 + j]

    def collect(table, member, peer, out):
        for j in range(cap):
            tile = table[rows_ref[member, (peer * cores + lax.axis_index("shot")) * cap + j]]
            if len(out.shape) == 4:
                out[peer, j] = tile
            else:
                out[peer * cap + j] = tile

    rows_copy.wait()
    loads[0].wait()
    for phase in range(2 * members):
        member, table = phase // 2, (rho_tab, vel_tab)[phase % 2]
        if phase == 1:
            loads[1].wait()
        if phase == 0:
            each(owners, lambda d: collect(table, member, (me + d) % owners, leaving[phase]))
            pl.semaphore_wait(barrier, peers - 1)
            each(owners, lambda d: model_copy(phase, d).start())
            list_tiles()
        else:
            def send(d):
                collect(table, member, (me + d) % owners, leaving[phase])
                model_copy(phase, d).start()

            each(owners, send)
        collect(table, member, me, models[phase])

    def unpack(member, arrival, field):
        def body(kx, carry):
            for ky in range(grid_y):
                slot = slot_at(member, kx, ky)
                tile = arrival[slot].astype(jnp.float32)
                for i in range(4):
                    field[kx * 4 + i, pl.ds(ky * 4, 4), :] = tile[4 * i : 4 * i + 4]
            return carry

        lax.fori_loop(0, nx // 4, body, 0, unroll=2)

    def divergence(value, half, transposed):
        high, low = halves(half * value)
        if transposed:
            return dot(jnp.concatenate([yband[1], yband[1]], axis=1), jnp.concatenate([high, low], axis=0))
        return dot(jnp.concatenate([high, low], axis=1), zband[1])

    def planes(ref, g, *lead):
        return ref[(*lead, pl.ds(pl.multiple_of(g * GROUP, GROUP), GROUP))].reshape(rows, nz)

    def lines(first, second_block, first_half, second_half, exact):
        pair = lambda a, b: jnp.concatenate([a, b], axis=1)
        stack = lambda a, b: jnp.concatenate([a, b], axis=0)
        if exact:
            grad_z = dot(stack(first, second_block), zband[0, :nz])
            grad_y = dot(yband[0], pair(first, second_block))
        else:
            (high_a, low_a), (high_b, low_b) = halves(first), halves(second_block)
            grad_z = dot(stack(pair(high_a, low_a), pair(high_b, low_b)), zband[0])
            grad_y = dot(pair(yband[0], yband[0]), stack(pair(high_a, high_b), pair(low_a, low_b)))
        (hy_a, hz_a), (hy_b, hz_b) = first_half, second_half
        div_z = divergence(grad_z, stack(hz_a, hz_b), False)
        div_y = divergence(grad_y, pair(hy_a, hy_b), True)
        return div_z[:rows] + div_y[:, :nz], div_z[rows:] + div_y[:, nz:]

    def cut(g):
        return planes(hy, g), planes(hz, g)

    def put(ref, g, block):
        ref[pl.ds(pl.multiple_of(g * GROUP, GROUP), GROUP)] = block.reshape(GROUP, ny, nz)

    def columns(jobs):
        def body(ty, peak):
            start = pl.multiple_of(ty * 8, 8)
            here = pl.ds(start, 8)
            for load, rest_sum, finish in jobs:
                values, fluxes = {}, {}

                def value_at(x):
                    if x < 0 or x >= nx:
                        return None
                    if x not in values:
                        values[x] = load(x, here)
                    return values[x]

                def flux_at(x):
                    if x < 0 or x >= nx:
                        return None
                    if x not in fluxes:
                        fluxes[x] = hx[x, here, :] * taps(lambda shift: value_at(x + shift), True)
                    return fluxes[x]

                for x in range(nx):
                    total = rest_sum[x, here, :] + taps(lambda shift: flux_at(x + shift), False)
                    size = finish(x, ty, here, value_at(x), total)
                    if size is not None:
                        peak = jnp.maximum(peak, size)
            return peak

        return lax.fori_loop(0, tiles_y, body, jnp.zeros((8, nz), jnp.float32))

    def single(field):
        def body(pair_index, carry):
            g = pair_index * 2
            one, two = lines(planes(field, g), planes(field, g + 1), cut(g), cut(g + 1), False)
            put(sum_p, g, one)
            put(sum_p, g + 1, two)
            return carry

        lax.fori_loop(0, nx // GROUP // 2, body, 0, unroll=True)

    def source_term(member, step, base, shape):
        local = lax.broadcasted_iota(jnp.int32, shape, 0) * nz + lax.broadcasted_iota(jnp.int32, shape, 1)
        return jnp.where(local == source_ref[0, 0, member] - base, wave_ref[0, 0, member, step], 0.0)

    def first_half(member):
        each(owners, lambda d: model_copy(2 * member, d).wait())
        unpack(member, models[2 * member], rho)

        def prepare(x, carry):
            value = (0.5 * LEAD * LEAD) / rho[x]
            buoy[x, pl.ds(0, ny), :] = value
            buoy[x, pl.ds(ny, 1), :] = value[ny - 1 :]
            return carry

        lax.fori_loop(0, nx, prepare, 0, unroll=4)

        def between(x, carry):
            here = buoy[x, pl.ds(0, ny), :]
            hx[x] = here + buoy[jnp.minimum(x + 1, nx - 1), pl.ds(0, ny), :]
            hy[x] = (here + buoy[x, pl.ds(1, ny), :]) * (1.0 / (BAND * BAND))
            shifted = jnp.where(lane == nz - 1, here, pltpu.roll(here, nz - 1, 1))
            hz[x] = (here + shifted) * (1.0 / (BAND * BAND))
            return carry

        lax.fori_loop(0, nx, between, 0, unroll=8)
        if member == 0:
            for load in loads[2:6]:
                load.wait()

        def both(g, carry):
            first, other = planes(now_ref, g, member), planes(adj_ref, g, member)
            put(wide_p, g, first.astype(jnp.float32))
            put(wide_q, g, other.astype(jnp.float32))
            one, two = lines(first, other, cut(g), cut(g), True)
            put(sum_p, g, one)
            put(sum_q, g, two)
            return carry

        lax.fori_loop(0, nx // GROUP, both, 0, unroll=True)

        def keep_p(x, ty, here, value, total):
            image_one[x, here, :] = total

        def keep_q(x, ty, here, value, total):
            adj_one[x, here, :] = total

        columns((
            (lambda x, here: wide_p[x, here, :], sum_p, keep_p),
            (lambda x, here: wide_q[x, here, :], sum_q, keep_q),
        ))

    def second_half(member):
        unpack(member, models[2 * member + 1], vel)
        if member == 0:
            for load in loads[6:]:
                load.wait()
        coupling, weight = vel, rho

        def advance(x, carry):
            velocity, density = vel[x], rho[x]
            scale = (COURANT * velocity) * (COURANT * velocity) * density
            coupling[x] = scale
            weight[x] = velocity * density
            wide = lambda ref: ref[member, x].astype(jnp.float32)
            second[x] = 2.0 * wide_p[x] - wide(old_ref) + scale * image_one[x] + source_term(member, 0, x * (ny * nz), (ny, nz))
            adj_one[x] = 2.0 * wide_q[x] - wide(next_ref) + scale * adj_one[x]
            return carry

        lax.fori_loop(0, nx, advance, 0, unroll=2)
        single(second)

        def finish_two(x, ty, here, value, total):
            image_two[x, here, :] = total
            third[x, here, :] = 2.0 * value - wide_p[x, here, :] + coupling[x, here, :] * total + source_term(member, 1, (x * ny + ty * 8) * nz, (8, nz))

        columns(((lambda x, here: second[x, here, :], sum_p, finish_two),))
        count = cells_ref.shape[-1]

        def receive(step, carry):
            for sub in range(16):
                n = step * 16 + sub
                line = lax.shift_right_logical(cells_ref[0, 0, member, n], LANE_BITS)
                spot = pl.ds(lax.bitwise_and(line, ny - 1), 1)
                x = lax.shift_right_logical(line, ny.bit_length() - 1)
                misfit[0, pl.ds(n, 1), :] = third[x, spot, :]
                misfit[1, pl.ds(n, 1), :] = second[x, spot, :]
            return carry

        lax.fori_loop(0, count // 16, receive, 0)
        upright = lambda row: jnp.broadcast_to(row, (nz, count)).T
        cells = lanes_ref[0, 0, pl.ds(member, 1), :]
        pick_z = upright((cells & (nz - 1)).astype(jnp.float32)) == lax.broadcasted_iota(jnp.int32, (count, nz), 1).astype(jnp.float32)
        amounts = [
            jnp.where(pick_z, misfit[step] - upright(obs_ref[0, 0, member, pl.ds(1 - step, 1), :]), 0.0) for step in range(2)
        ]
        amounts = jnp.concatenate(halves(jnp.concatenate(amounts, axis=1)), axis=0)
        line_of = lax.shift_right_logical(cells, LANE_BITS)

        def deliver(g, carry):
            pick = (lax.broadcasted_iota(jnp.int32, (rows, count), 0) + g * rows == line_of).astype(jnp.float32).astype(jnp.bfloat16)
            added = dot(jnp.concatenate([pick, pick], axis=1), amounts)
            put(adj_one, g, planes(adj_one, g) + added[:, :nz])
            put(mixed, g, added[:, nz:] - planes(wide_q, g))
            return carry

        lax.fori_loop(0, nx // GROUP, deliver, 0, unroll=True)
        single(adj_one)

        def finish_four(x, ty, here, value, total):
            q0 = 2.0 * value + mixed[x, here, :] + coupling[x, here, :] * total
            result = weight[x, here, :] * (value * image_two[x, here, :] + q0 * image_one[x, here, :])
            size = jnp.abs(result)
            root = result * lax.rsqrt(jnp.maximum(size, SMALL))
            for half in range(2):
                spot = (x // 4) * grid_y + ty * 2 + half
                tiles[spot, (x % 4) // 2, pl.ds((x % 2) * 4, 4), :] = root[4 * half : 4 * half + 4]
            return size

        peak = columns(((lambda x, here: adj_one[x, here, :], sum_p, finish_four),))
        top = jnp.maximum(jnp.max(peak, axis=(0, 1), keepdims=True), SMALL)
        factor = jnp.broadcast_to(CODES * lax.rsqrt(top), (8, nz))
        scale = jnp.broadcast_to(top * (2.0 * COURANT * COURANT / (CODES * CODES)), (1, nz))
        scale_out[member] = scale
        scale_in[member, whole_me] = scale

        def pack(owner, carry):
            for core in range(cores):
                parts = []
                for j in range(0, cap):
                    parts.append(jnp.round(tiles[spot_at(member, owner, j), core] * factor))
                if cap % 2:
                    parts.append(jnp.zeros((8, nz), jnp.float32))
                for j in range(0, len(parts), 2):
                    code = jnp.concatenate(parts[j : j + 2], axis=0).astype(jnp.int32).astype(jnp.int16)
                    outgoing[member][owner * cores + core, pl.ds(8 * j, 16), :] = code
            return carry

        lax.fori_loop(0, owners, pack, 0)

    keeps = [
        pltpu.make_async_copy(outgoing[member].at[whole_me], arrived[member].at[whole_me], keep_sems.at[member])
        for member in range(members)
    ]

    def dispatch(member):
        each(peers, lambda d: scale_copy(member, d).start())
        each(peers, lambda d: grad_copy(member, d).start())
        keeps[member].start()

    def add_up(member):
        each(peers, lambda d: scale_copy(member, d).wait())
        each(peers, lambda d: grad_copy(member, d).wait())
        keeps[member].wait()
        per = cap * 8

        def decode(source, carry):
            code = arrived[member][source].astype(jnp.int32).astype(jnp.float32)[:per]
            decoded[pl.ds(pl.multiple_of(source * per, per), per), :] = code * jnp.abs(code) * scale_in[member, source]
            return carry

        lax.fori_loop(0, peers, decode, 0, unroll=2)
        pick = (lax.broadcasted_iota(jnp.int32, (held, total), 0) == homes_ref[pl.ds(member, 1), :]).astype(jnp.float32).astype(jnp.bfloat16)
        pick = jnp.concatenate([pick, pick], axis=1)
        for i in range(8):
            part = dot(pick, jnp.concatenate(halves(decoded[pl.ds(i, total, stride=8), :]), axis=0))
            mine = pl.ds(i, held, stride=8)
            out_ref[mine, :] = part if member == 0 else out_ref[mine, :] + part

    lists_copy.wait()
    for member in range(members):
        first_half(member)
        each(owners, lambda d: model_copy(2 * member + 1, d).wait())
        if member == members - 1:
            for done in range(members - 1):
                dispatch(done)
        second_half(member)
    dispatch(members - 1)
    for member in range(members):
        add_up(member)
    leave(out_ref, out_hbm, out_sems)


def per_device(
    velocity, density, tile_home, footprints, source_cell, source_wave, receivers, observed,
    pressure_old, pressure_now, adjoint_next, adjoint_now,
):
    owners = lax.axis_size("own")
    cores = lax.axis_size("shot")
    held = velocity.shape[0]
    members, foot = footprints.shape[2:]
    cap = foot // owners
    nx, ny, nz = pressure_now.shape[-3:]
    vmem = pl.BlockSpec(memory_space=pltpu.VMEM)
    smem = pl.BlockSpec(memory_space=pltpu.SMEM)
    hbm = pl.BlockSpec(memory_space=pl.ANY)
    field = pltpu.VMEM((nx, ny, nz), jnp.float32)
    stored = pltpu.VMEM((members, nx, ny, nz), jnp.bfloat16)
    table = pltpu.VMEM((held, 16, nz), jnp.bfloat16)
    model = pltpu.VMEM((owners, cap, 16, nz), jnp.bfloat16)
    peers = owners * cores
    grads = pltpu.VMEM((peers, (cap * 8 + 15) // 16 * 16, nz), jnp.int16)
    zband, yband = depth_bands(nz), line_bands(ny)
    count = receivers.shape[-1]
    lists = members * (8 + owners)
    dma = pltpu.SemaphoreType.DMA
    gradient = pl.pallas_call(
        shots_kernel,
        out_shape=jax.ShapeDtypeStruct((held * 8, nz), jnp.float32),
        in_specs=[smem] * 4 + [vmem] * 3 + [hbm] * 8,
        out_specs=hbm,
        scratch_shapes=[pltpu.VMEM((foot, 16, nz), jnp.bfloat16)] * (2 * members) + [model] * (2 * members) + [grads] * (2 * members) + [
            table, table, pltpu.VMEM(zband.shape, jnp.bfloat16), pltpu.VMEM(yband.shape, jnp.bfloat16),
            stored, stored, stored, stored,
            field, field, pltpu.VMEM((nx, ny + 8, nz), jnp.float32)] + [field] * 13 + [
            pltpu.VMEM((foot, 2, 8, nz), jnp.float32), pltpu.VMEM((2, count, nz), jnp.float32),
            pltpu.VMEM((peers * cap * 8, nz), jnp.float32), pltpu.VMEM((members, 1, nz), jnp.float32), pltpu.VMEM((members, peers, 1, nz), jnp.float32),
            pltpu.VMEM((held * 8, nz), jnp.float32), pltpu.VMEM((members, peers * cap), jnp.int32),
            pltpu.VMEM((8 + lists, nz), jnp.int32), pltpu.SMEM((8, nz), jnp.int32), pltpu.SMEM((lists, nz), jnp.int32), dma((2,)), dma((8,)),
            dma((8,)), dma((members,)), dma((2 * members, owners)), dma((2 * members, owners)),
            dma((members, peers)), dma((members, peers)), dma((members, peers)), dma((members, peers)),
        ],
        compiler_params=pltpu.CompilerParams(collective_id=0, has_side_effects=True, vmem_limit_bytes=56 * 1024 * 1024),
        cost_estimate=pl.CostEstimate(flops=200_000_000, bytes_accessed=6_000_000, transcendentals=0),
    )(
        footprints, source_cell, receivers, source_wave, observed, receivers, tile_home.reshape(-1, nz),
        velocity.reshape(held, 16, nz), density.reshape(held, 16, nz), zband, yband,
        pressure_old, pressure_now, adjoint_next, adjoint_now,
    )
    gradient = pl.pallas_call(
        pass_on,
        out_shape=jax.ShapeDtypeStruct(gradient.shape, jnp.float32),
        in_specs=[hbm], out_specs=hbm,
        scratch_shapes=[pltpu.VMEM(gradient.shape, jnp.float32), dma((8,)), dma((8,))],
        compiler_params=pltpu.CompilerParams(vmem_limit_bytes=56 * 1024 * 1024),
    )(gradient)
    return gradient.reshape(held, 4 // cores, 4, nz)


def solution(mesh):
    whole = P(("grp", "own"), None, None, None)
    fields = P(("grp", "own"), "shot", None, None, None, None)
    in_specs = (
        whole, whole, P("grp"), P("grp", None, None, None),
        P(("grp", "own"), "shot", None),
        P(("grp", "own"), "shot", None, None),
        P(("grp", "own"), "shot", None, None),
        P(("grp", "own"), "shot", None, None, None),
        fields, fields, fields, fields,
    )
    return jax.shard_map(
        per_device, mesh=mesh, in_specs=in_specs,
        out_specs=P(("grp", "own"), "shot", None, None), check_vma=False,
    )
```

```python
import functools

import jax
import jax.numpy as jnp
import numpy as np
from jax import lax
from jax.experimental import pallas as pl
from jax.experimental.pallas import tpu as pltpu
from jax.sharding import PartitionSpec as P

COURANT = 0.09
LEAD = 1225.0 / 1024.0
RATIOS = (1.0, -1.0 / 15.0, 1.0 / 125.0, -1.0 / 1715.0)
BAND = 105.0
GROUP = 8
LANE_BITS = 7
CODES = 32760.0
SMALL = 1e-30
MESH = pl.DeviceIdType.MESH


def difference_matrices(length):
    grad = np.zeros((length, length), np.float32)
    div = np.zeros((length, length), np.float32)
    for i in range(length):
        for m, ratio in enumerate(RATIOS, start=1):
            if i + m < length:
                grad[i, i + m] += BAND * ratio
            if i + 1 - m >= 0:
                grad[i, i + 1 - m] -= BAND * ratio
            if i + m - 1 < length:
                div[i, i + m - 1] += BAND * ratio
            if i - m >= 0:
                div[i, i - m] -= BAND * ratio
    return grad, div


def depth_bands(depth):
    grad, div = difference_matrices(depth)
    return jnp.asarray(np.stack([np.concatenate([a.T, a.T], axis=0) for a in (grad, div)]), jnp.bfloat16)


def line_bands(length):
    return jnp.asarray(np.stack([np.kron(np.eye(GROUP, dtype=np.float32), a) for a in difference_matrices(length)]), jnp.bfloat16)


def taps(at, low):
    total = None
    for m, ratio in enumerate(RATIOS, start=1):
        up, down = (at(m), at(1 - m)) if low else (at(m - 1), at(-m))
        if up is None and down is None:
            continue
        diff = up - down if up is not None and down is not None else (up if down is None else -down)
        term = diff if m == 1 else ratio * diff
        total = term if total is None else total + term
    return total


def halves(value):
    high = value.astype(jnp.bfloat16)
    return high, (value - high.astype(jnp.float32)).astype(jnp.bfloat16)


def dot(a, b):
    return jnp.dot(a, b, preferred_element_type=jnp.float32)


def leave(source, target, sems):
    pieces = sems.shape[0]
    step = source.shape[0] // pieces
    copies = [
        pltpu.make_async_copy(source.at[pl.ds(i * step, step)], target.at[pl.ds(i * step, step)], sems.at[i])
        for i in range(pieces)
    ]
    for copy in copies:
        copy.start()
    for copy in copies:
        copy.wait()


def pass_on(source, target, held, in_sems, out_sems):
    pieces = in_sems.shape[0]
    step = source.shape[0] // pieces
    part = lambda ref, i: ref.at[pl.ds(i * step, step)]
    arrive = [pltpu.make_async_copy(part(source, i), part(held, i), in_sems.at[i]) for i in range(pieces)]
    depart = [pltpu.make_async_copy(part(held, i), part(target, i), out_sems.at[i]) for i in range(pieces)]
    for copy in arrive:
        copy.start()
    for i in range(pieces):
        arrive[i].wait()
        depart[i].start()
    for copy in depart:
        copy.wait()


def shots_kernel(
    home_hbm, foot_hbm, source_hbm, cells_hbm, wave_hbm, obs_hbm,
    vel_hbm, rho_hbm, zband_hbm, yband_hbm, old_hbm, now_hbm, next_hbm, adj_hbm,
    out_hbm, *rest,
):
    members, foot = foot_hbm.shape[2:]
    models, rest = rest[: 2 * members], rest[2 * members :]
    leaving, rest = rest[: 2 * members], rest[2 * members :]
    outgoing, rest = rest[:members], rest[members:]
    arrived, rest = rest[:members], rest[members:]
    (
        vel_tab, rho_tab, zband, yband, old_ref, now_ref, next_ref, adj_ref,
        rho, vel, buoy, hx, hy, hz, sum_p, sum_q, image_one, adj_one, second, third, image_two, mixed, wide_p, wide_q, tiles,
        misfit, decoded, scale_out, scale_in, out_ref, homes_ref, book, rows_ref, lists_ref, table_sems, out_sems,
        home_ref, foot_ref, source_ref, cells_ref, wave_ref, obs_ref, lanes_ref, picks, upright_obs, pick_z, lead_p, lead_q,
        load_sems, keep_sems, model_send, model_recv, grad_send, grad_recv, scale_send, scale_recv,
    ) = rest
    owners, cap = leaving[0].shape[:2]
    cores = lax.axis_size("shot")
    nx, ny, nz = now_ref.shape[1:]
    grid_y = ny // 4
    tiles_y = ny // 8
    rows = GROUP * ny
    me = lax.axis_index("own")
    whole_me = me * cores + lax.axis_index("shot")
    peers = owners * cores
    lane = lax.broadcasted_iota(jnp.int32, (1, nz), 1)

    loads = [
        pltpu.make_async_copy(src, dst, load_sems.at[i])
        for i, (src, dst) in enumerate((
            (home_hbm, home_ref), (foot_hbm, foot_ref), (rho_hbm, rho_tab), (vel_hbm, vel_tab), (zband_hbm, zband), (yband_hbm, yband),
            (now_hbm.at[0, 0], now_ref), (adj_hbm.at[0, 0], adj_ref), (old_hbm.at[0, 0], old_ref), (next_hbm.at[0, 0], next_ref),
            (cells_hbm, lanes_ref), (obs_hbm, obs_ref), (cells_hbm, cells_ref), (source_hbm, source_ref), (wave_hbm, wave_ref),
        ))
    ]
    for load in loads:
        load.start()
    barrier = pltpu.get_barrier_semaphore()

    def device(peer):
        return {"own": peer // cores, "shot": peer % cores}

    def greet(d, carry):
        pl.semaphore_signal(barrier, inc=1, device_id=device((whole_me + d) % peers), device_id_type=MESH)
        return carry

    lax.fori_loop(1, peers, greet, 0)

    def model_copy(phase, d):
        peer = (me + d) % owners
        return pltpu.make_async_remote_copy(
            src_ref=leaving[phase].at[peer], dst_ref=models[phase].at[pl.ds(me * cap, cap)],
            send_sem=model_send.at[phase, d], recv_sem=model_recv.at[phase, d],
            device_id={"own": peer}, device_id_type=MESH,
        )

    def grad_copy(member, d):
        peer = (whole_me + d) % peers
        return pltpu.make_async_remote_copy(
            src_ref=outgoing[member].at[peer], dst_ref=arrived[member].at[whole_me],
            send_sem=grad_send.at[member, d], recv_sem=grad_recv.at[member, d],
            device_id=device(peer), device_id_type=MESH,
        )

    def scale_copy(member, d):
        peer = (whole_me + d) % peers
        return pltpu.make_async_remote_copy(
            src_ref=scale_out.at[member], dst_ref=scale_in.at[member, whole_me],
            send_sem=scale_send.at[member, d], recv_sem=scale_recv.at[member, d],
            device_id=device(peer), device_id_type=MESH,
        )

    def each(count, act):
        def body(d, carry):
            act(d)
            return carry

        lax.fori_loop(1, count, body, 0)

    held = vel_tab.shape[0]
    count_tiles = home_ref.shape[0] * nz
    side = int(round(count_tiles ** 0.5))
    edge = int(round(foot ** 0.5))
    bits = lambda size: size.bit_length() - 1
    iota = lambda shape, axis: lax.broadcasted_iota(jnp.int32, shape, axis)
    narrow = lambda value: value.astype(jnp.float32).astype(jnp.bfloat16)
    across = lambda a, b: lax.dot_general(a, b, (((1,), (1,)), ((), ())), preferred_element_type=jnp.float32)
    blocks = home_ref.shape[0]

    def locate():
        home = home_ref[...]
        high, low = lax.shift_right_logical(home, LANE_BITS), home & (nz - 1)
        hit, full, own = [], [], []
        mine = lax.shift_right_logical(me * held, LANE_BITS)
        for i in range(blocks):
            tile = i * nz + iota((1, nz), 1)
            where = lax.shift_right_logical(tile, bits(side)), tile & (side - 1)
            hit.append(narrow(low[i : i + 1] == iota((nz, nz), 0)))
            high_row = high[i : i + 1]
            full.append(narrow(jnp.concatenate([jnp.where(high_row == iota((blocks, nz), 0), w, 0) for w in where], axis=0)))
            own.append(narrow(jnp.concatenate([jnp.broadcast_to(jnp.where(high_row == mine, w, 0), (nz, nz)) for w in where], axis=0)))
        hit, full, own = (jnp.concatenate(parts, axis=1) for parts in (hit, full, own))
        return across(full, hit).astype(jnp.int32), across(hit, own).astype(jnp.int32)

    def inside(dx, dy):
        return (dx >= 0) & (dx < edge) & (dy >= 0) & (dy < edge)

    def first_of(owner, core, member):
        first = foot_ref[owner, core, member, 0]
        return lax.shift_right_logical(first, bits(side)), first & (side - 1)

    total = peers * cap
    share = bits(held)
    spot_x, spot_y = iota((nz, nz), 0), iota((nz, nz), 1)
    same = lax.shift_right_logical(spot_x, share) == lax.shift_right_logical(spot_y, share)
    for load in loads[:2]:
        load.wait()
    positions, own_positions = locate()
    book[...] = jnp.zeros_like(book)
    in_share = lax.shift_right_logical(iota((nz, total), 0), share) == me % (nz >> share)
    before = narrow(same & (spot_y < spot_x))
    for member in range(members):
        first = jnp.zeros((1, total), jnp.int32)
        shot_of = lax.shift_right_logical(iota((1, total), 1), bits(cap))
        for peer in range(peers):
            first = jnp.where(shot_of == peer, foot_ref[peer // cores, peer % cores, member, 0], first)
        dx = own_positions[:, :nz] - lax.shift_right_logical(first, bits(side))
        dy = own_positions[:, nz:] - (first & (side - 1))
        chosen = inside(dx, dy) & in_share
        order = dot(before, narrow(chosen)).astype(jnp.int32)
        chosen = chosen & (order == (iota((1, total), 1) & (cap - 1)))
        local = jnp.where(chosen, iota((nz, total), 0) & (held - 1), 0)
        homes = jnp.clip(jnp.sum(local, axis=0, keepdims=True), 0, held - 1)
        homes_ref[pl.ds(member, 1), :] = homes
        book[pl.ds(member, 1), :] = homes
    rows_copy = pltpu.make_async_copy(book.at[pl.ds(0, 8)], rows_ref, table_sems.at[0])
    lists_copy = pltpu.make_async_copy(book.at[pl.ds(8, book.shape[0] - 8)], lists_ref, table_sems.at[1])
    rows_copy.start()

    def list_tiles():
        after = narrow(same & (spot_x < spot_y))
        keys, values = [], []
        cell = iota((blocks, nz), 0) * nz + iota((blocks, nz), 1)
        owner = lax.shift_right_logical(cell, share)
        for member in range(members):
            at_x, at_y = first_of(me, lax.axis_index("shot"), member)
            dx, dy = positions[:blocks] - at_x, positions[blocks:] - at_y
            chosen = inside(dx, dy)
            order = dot(narrow(chosen), after).astype(jnp.int32)
            slot = owner * cap + order
            key, value = [], []
            for i in range(blocks):
                row = lambda field: field[i : i + 1]
                valid = row(chosen.astype(jnp.int32)) == 1
                small = iota((8, nz), 0)
                key.append(narrow(jnp.concatenate([
                    jnp.where(valid & (row(dx) == small), 1, 0),
                    jnp.where(valid & (row(owner) == iota((owners, nz), 0)), 1, 0),
                ], axis=0)))
                value.append(narrow(jnp.concatenate([
                    jnp.where(row(dy) == small, row(slot), 0),
                    jnp.where(row(order) == small, row(dx) * edge + row(dy), 0),
                ], axis=0)))
            keys.append(jnp.concatenate(key, axis=1))
            values.append(jnp.concatenate(value, axis=1))
        values.append(jnp.zeros((nz - 16 * members, blocks * nz), jnp.bfloat16))
        found = across(jnp.concatenate(keys, axis=0), jnp.concatenate(values, axis=0)).astype(jnp.int32)
        book[pl.ds(8, found.shape[0]), :] = jnp.clip(found, 0, foot - 1)
        lists_copy.start()

    def slot_at(member, kx, ky):
        return lists_ref[member * (8 + owners) + kx, member * 16 + ky]

    def spot_at(member, owner, j):
        return lists_ref[member * (8 + owners) + 8 + owner, member * 16 + 8 + j]

    def collect(table, member, peer, out):
        for j in range(cap):
            tile = table[rows_ref[member, (peer * cores + lax.axis_index("shot")) * cap + j]]
            if len(out.shape) == 4:
                out[peer, j] = tile
            else:
                out[peer * cap + j] = tile

    rows_copy.wait()
    loads[2].wait()
    for phase in range(2 * members):
        member, table = phase // 2, (rho_tab, vel_tab)[phase % 2]
        if phase == 1:
            loads[3].wait()
        if phase == 0:
            each(owners, lambda d: collect(table, member, (me + d) % owners, leaving[phase]))
            pl.semaphore_wait(barrier, peers - 1)
            each(owners, lambda d: model_copy(phase, d).start())
            list_tiles()
        else:
            def send(d):
                collect(table, member, (me + d) % owners, leaving[phase])
                model_copy(phase, d).start()

            each(owners, send)
        collect(table, member, me, models[phase])

    def unpack(member, arrival, field):
        def body(kx, carry):
            for ky in range(grid_y):
                slot = slot_at(member, kx, ky)
                tile = arrival[slot].astype(jnp.float32)
                for i in range(4):
                    field[kx * 4 + i, pl.ds(ky * 4, 4), :] = tile[4 * i : 4 * i + 4]
            return carry

        lax.fori_loop(0, nx // 4, body, 0, unroll=2)

    def divergence(value, half, transposed):
        high, low = halves(half * value)
        if transposed:
            return dot(jnp.concatenate([yband[1], yband[1]], axis=1), jnp.concatenate([high, low], axis=0))
        return dot(jnp.concatenate([high, low], axis=1), zband[1])

    def planes(ref, g, *lead):
        return ref[(*lead, pl.ds(pl.multiple_of(g * GROUP, GROUP), GROUP))].reshape(rows, nz)

    def lines(first, second_block, first_half, second_half, exact):
        pair = lambda a, b: jnp.concatenate([a, b], axis=1)
        stack = lambda a, b: jnp.concatenate([a, b], axis=0)
        if exact:
            grad_z = dot(stack(first, second_block), zband[0, :nz])
            grad_y = dot(yband[0], pair(first, second_block))
        else:
            (high_a, low_a), (high_b, low_b) = halves(first), halves(second_block)
            grad_z = dot(stack(pair(high_a, low_a), pair(high_b, low_b)), zband[0])
            grad_y = dot(pair(yband[0], yband[0]), stack(pair(high_a, high_b), pair(low_a, low_b)))
        (hy_a, hz_a), (hy_b, hz_b) = first_half, second_half
        div_z = divergence(grad_z, stack(hz_a, hz_b), False)
        div_y = divergence(grad_y, pair(hy_a, hy_b), True)
        return div_z[:rows] + div_y[:, :nz], div_z[rows:] + div_y[:, nz:]

    def cut(g):
        return planes(hy, g), planes(hz, g)

    def put(ref, g, block):
        ref[pl.ds(pl.multiple_of(g * GROUP, GROUP), GROUP)] = block.reshape(GROUP, ny, nz)

    def columns(jobs):
        def body(ty, peak):
            start = pl.multiple_of(ty * 8, 8)
            here = pl.ds(start, 8)
            for load, rest_sum, finish in jobs:
                values, fluxes = {}, {}

                def value_at(x):
                    if x < 0 or x >= nx:
                        return None
                    if x not in values:
                        values[x] = load(x, here)
                    return values[x]

                def flux_at(x):
                    if x < 0 or x >= nx:
                        return None
                    if x not in fluxes:
                        fluxes[x] = hx[x, here, :] * taps(lambda shift: value_at(x + shift), True)
                    return fluxes[x]

                for x in range(nx):
                    total = rest_sum[x, here, :] + taps(lambda shift: flux_at(x + shift), False)
                    size = finish(x, ty, here, value_at(x), total)
                    if size is not None:
                        peak = jnp.maximum(peak, size)
            return peak

        return lax.fori_loop(0, tiles_y, body, jnp.zeros((8, nz), jnp.float32))

    def single(field):
        def body(pair_index, carry):
            g = pair_index * 2
            one, two = lines(planes(field, g), planes(field, g + 1), cut(g), cut(g + 1), False)
            put(sum_p, g, one)
            put(sum_p, g + 1, two)
            return carry

        lax.fori_loop(0, nx // GROUP // 2, body, 0, unroll=True)

    def source_term(member, step, base, shape):
        local = lax.broadcasted_iota(jnp.int32, shape, 0) * nz + lax.broadcasted_iota(jnp.int32, shape, 1)
        return jnp.where(local == source_ref[0, 0, member] - base, wave_ref[0, 0, member, step], 0.0)

    def first_half(member):
        each(owners, lambda d: model_copy(2 * member, d).wait())
        unpack(member, models[2 * member], rho)

        def prepare(x, carry):
            value = (0.5 * LEAD * LEAD) / rho[x]
            buoy[x, pl.ds(0, ny), :] = value
            buoy[x, pl.ds(ny, 1), :] = value[ny - 1 :]
            return carry

        lax.fori_loop(0, nx, prepare, 0, unroll=4)

        def between(x, carry):
            here = buoy[x, pl.ds(0, ny), :]
            hx[x] = here + buoy[jnp.minimum(x + 1, nx - 1), pl.ds(0, ny), :]
            hy[x] = (here + buoy[x, pl.ds(1, ny), :]) * (1.0 / (BAND * BAND))
            shifted = jnp.where(lane == nz - 1, here, pltpu.roll(here, nz - 1, 1))
            hz[x] = (here + shifted) * (1.0 / (BAND * BAND))
            return carry

        lax.fori_loop(0, nx, between, 0, unroll=8)
        if member == 0:
            for load in loads[4:]:
                load.wait()

        count = cells_ref.shape[-1]
        upright = lambda row: jnp.broadcast_to(row, (nz, count)).T
        cells = lanes_ref[0, 0, pl.ds(member, 1), :]
        pick_z[...] = (upright((cells & (nz - 1)).astype(jnp.float32)) == iota((count, nz), 1).astype(jnp.float32)).astype(jnp.float32)
        for step in range(2):
            upright_obs[step] = upright(obs_ref[0, 0, member, pl.ds(1 - step, 1), :])
        line_of = lax.shift_right_logical(cells, LANE_BITS)

        def both(g, carry):
            part = pl.ds(pl.multiple_of(g * rows, rows), rows)
            picks[part, :] = narrow(iota((rows, count), 0) + g * rows == line_of)
            first, other = planes(now_ref, g, member), planes(adj_ref, g, member)
            wide, wide_other = first.astype(jnp.float32), other.astype(jnp.float32)
            put(wide_p, g, wide)
            put(wide_q, g, wide_other)
            put(lead_p, g, 2.0 * wide - planes(old_ref, g, member).astype(jnp.float32))
            put(lead_q, g, 2.0 * wide_other - planes(next_ref, g, member).astype(jnp.float32))
            one, two = lines(first, other, cut(g), cut(g), True)
            put(sum_p, g, one)
            put(sum_q, g, two)
            return carry

        lax.fori_loop(0, nx // GROUP, both, 0, unroll=True)

        def keep_p(x, ty, here, value, total):
            image_one[x, here, :] = total

        def keep_q(x, ty, here, value, total):
            adj_one[x, here, :] = total

        columns((
            (lambda x, here: wide_p[x, here, :], sum_p, keep_p),
            (lambda x, here: wide_q[x, here, :], sum_q, keep_q),
        ))

    def second_half(member):
        unpack(member, models[2 * member + 1], vel)
        coupling, weight = vel, rho

        def advance(x, carry):
            velocity, density = vel[x], rho[x]
            scale = (COURANT * velocity) * (COURANT * velocity) * density
            coupling[x] = scale
            weight[x] = velocity * density
            second[x] = lead_p[x] + scale * image_one[x] + source_term(member, 0, x * (ny * nz), (ny, nz))
            adj_one[x] = lead_q[x] + scale * adj_one[x]
            return carry

        lax.fori_loop(0, nx, advance, 0, unroll=4)
        single(second)

        def finish_two(x, ty, here, value, total):
            image_two[x, here, :] = total
            third[x, here, :] = 2.0 * value - wide_p[x, here, :] + coupling[x, here, :] * total + source_term(member, 1, (x * ny + ty * 8) * nz, (8, nz))

        columns(((lambda x, here: second[x, here, :], sum_p, finish_two),))
        count = cells_ref.shape[-1]

        def receive(step, carry):
            for sub in range(16):
                n = step * 16 + sub
                line = lax.shift_right_logical(cells_ref[0, 0, member, n], LANE_BITS)
                spot = pl.ds(lax.bitwise_and(line, ny - 1), 1)
                x = lax.shift_right_logical(line, ny.bit_length() - 1)
                misfit[0, pl.ds(n, 1), :] = third[x, spot, :]
                misfit[1, pl.ds(n, 1), :] = second[x, spot, :]
            return carry

        lax.fori_loop(0, count // 16, receive, 0)
        amounts = [
            jnp.where(pick_z[...] > 0.5, misfit[step] - upright_obs[step], 0.0) for step in range(2)
        ]
        amounts = jnp.concatenate(halves(jnp.concatenate(amounts, axis=1)), axis=0)

        def deliver(g, carry):
            pick = picks[pl.ds(pl.multiple_of(g * rows, rows), rows), :]
            added = dot(jnp.concatenate([pick, pick], axis=1), amounts)
            put(adj_one, g, planes(adj_one, g) + added[:, :nz])
            put(mixed, g, added[:, nz:] - planes(wide_q, g))
            return carry

        lax.fori_loop(0, nx // GROUP, deliver, 0, unroll=True)
        single(adj_one)

        def finish_four(x, ty, here, value, total):
            q0 = 2.0 * value + mixed[x, here, :] + coupling[x, here, :] * total
            result = weight[x, here, :] * (value * image_two[x, here, :] + q0 * image_one[x, here, :])
            size = jnp.abs(result)
            root = result * lax.rsqrt(jnp.maximum(size, SMALL))
            for half in range(2):
                spot = (x // 4) * grid_y + ty * 2 + half
                tiles[spot, (x % 4) // 2, pl.ds((x % 2) * 4, 4), :] = root[4 * half : 4 * half + 4]
            return size

        peak = columns(((lambda x, here: adj_one[x, here, :], sum_p, finish_four),))
        top = jnp.maximum(jnp.max(peak, axis=(0, 1), keepdims=True), SMALL)
        factor = jnp.broadcast_to(CODES * lax.rsqrt(top), (8, nz))
        scale = jnp.broadcast_to(top * (2.0 * COURANT * COURANT / (CODES * CODES)), (1, nz))
        scale_out[member] = scale
        scale_in[member, whole_me] = scale

        def pack(owner, carry):
            for core in range(cores):
                parts = []
                for j in range(0, cap):
                    parts.append(jnp.round(tiles[spot_at(member, owner, j), core] * factor))
                if cap % 2:
                    parts.append(jnp.zeros((8, nz), jnp.float32))
                for j in range(0, len(parts), 2):
                    code = jnp.concatenate(parts[j : j + 2], axis=0).astype(jnp.int32).astype(jnp.int16)
                    outgoing[member][owner * cores + core, pl.ds(8 * j, 16), :] = code
            return carry

        lax.fori_loop(0, owners, pack, 0)

    keeps = [
        pltpu.make_async_copy(outgoing[member].at[whole_me], arrived[member].at[whole_me], keep_sems.at[member])
        for member in range(members)
    ]

    def dispatch(member):
        each(peers, lambda d: scale_copy(member, d).start())
        each(peers, lambda d: grad_copy(member, d).start())
        keeps[member].start()

    def add_up(member):
        per = cap * 8

        def decode(source):
            code = arrived[member][source].astype(jnp.int32).astype(jnp.float32)[:per]
            decoded[pl.ds(pl.multiple_of(source * per, per), per), :] = code * jnp.abs(code) * scale_in[member, source]

        keeps[member].wait()
        decode(whole_me)

        def accept(d):
            scale_copy(member, d).wait()
            grad_copy(member, d).wait()
            decode((whole_me + peers - d) % peers)

        each(peers, accept)
        pick = (lax.broadcasted_iota(jnp.int32, (held, total), 0) == homes_ref[pl.ds(member, 1), :]).astype(jnp.float32).astype(jnp.bfloat16)
        pick = jnp.concatenate([pick, pick], axis=1)
        for i in range(8):
            part = dot(pick, jnp.concatenate(halves(decoded[pl.ds(i, total, stride=8), :]), axis=0))
            mine = pl.ds(i, held, stride=8)
            out_ref[mine, :] = part if member == 0 else out_ref[mine, :] + part

    lists_copy.wait()
    for member in range(members):
        first_half(member)
        if member == members - 1:
            for done in range(members - 1):
                dispatch(done)
        each(owners, lambda d: model_copy(2 * member + 1, d).wait())
        second_half(member)
    dispatch(members - 1)
    for member in range(members):
        add_up(member)
    leave(out_ref, out_hbm, out_sems)


def per_device(
    velocity, density, tile_home, footprints, source_cell, source_wave, receivers, observed,
    pressure_old, pressure_now, adjoint_next, adjoint_now,
):
    owners = lax.axis_size("own")
    cores = lax.axis_size("shot")
    held = velocity.shape[0]
    members, foot = footprints.shape[2:]
    cap = foot // owners
    nx, ny, nz = pressure_now.shape[-3:]
    home = tile_home.reshape(-1, nz)
    hbm = pl.BlockSpec(memory_space=pl.ANY)
    field = pltpu.VMEM((nx, ny, nz), jnp.float32)
    stored = pltpu.VMEM((members, nx, ny, nz), jnp.bfloat16)
    table = pltpu.VMEM((held, 16, nz), jnp.bfloat16)
    model = pltpu.VMEM((owners, cap, 16, nz), jnp.bfloat16)
    peers = owners * cores
    grads = pltpu.VMEM((peers, (cap * 8 + 15) // 16 * 16, nz), jnp.int16)
    zband, yband = depth_bands(nz), line_bands(ny)
    count = receivers.shape[-1]
    lists = members * (8 + owners)
    dma = pltpu.SemaphoreType.DMA
    gradient = pl.pallas_call(
        shots_kernel,
        out_shape=jax.ShapeDtypeStruct((held * 8, nz), jnp.float32),
        in_specs=[hbm] * 14,
        out_specs=hbm,
        scratch_shapes=[pltpu.VMEM((foot, 16, nz), jnp.bfloat16)] * (2 * members) + [model] * (2 * members) + [grads] * (2 * members) + [
            table, table, pltpu.VMEM(zband.shape, jnp.bfloat16), pltpu.VMEM(yband.shape, jnp.bfloat16),
            stored, stored, stored, stored,
            field, field, pltpu.VMEM((nx, ny + 8, nz), jnp.float32)] + [field] * 13 + [
            pltpu.VMEM((foot, 2, 8, nz), jnp.float32), pltpu.VMEM((2, count, nz), jnp.float32),
            pltpu.VMEM((peers * cap * 8, nz), jnp.float32), pltpu.VMEM((members, 1, nz), jnp.float32), pltpu.VMEM((members, peers, 1, nz), jnp.float32),
            pltpu.VMEM((held * 8, nz), jnp.float32), pltpu.VMEM((members, peers * cap), jnp.int32),
            pltpu.VMEM((8 + lists, nz), jnp.int32), pltpu.SMEM((8, nz), jnp.int32), pltpu.SMEM((lists, nz), jnp.int32), dma((2,)), dma((8,)),
            pltpu.VMEM(home.shape, jnp.int32), pltpu.SMEM(footprints.shape, jnp.int32), pltpu.SMEM(source_cell.shape, jnp.int32),
            pltpu.SMEM(receivers.shape, jnp.int32), pltpu.SMEM(source_wave.shape, jnp.float32),
            pltpu.VMEM(observed.shape, jnp.float32), pltpu.VMEM(receivers.shape, jnp.int32),
            pltpu.VMEM((nx * ny, count), jnp.bfloat16), pltpu.VMEM((2, count, nz), jnp.float32), pltpu.VMEM((count, nz), jnp.float32), field, field,
            dma((15,)), dma((members,)), dma((2 * members, owners)), dma((2 * members, owners)),
            dma((members, peers)), dma((members, peers)), dma((members, peers)), dma((members, peers)),
        ],
        compiler_params=pltpu.CompilerParams(collective_id=0, has_side_effects=True, vmem_limit_bytes=56 * 1024 * 1024),
        cost_estimate=pl.CostEstimate(flops=200_000_000, bytes_accessed=6_000_000, transcendentals=0),
    )(
        home, footprints, source_cell, receivers, source_wave, observed,
        velocity.reshape(held, 16, nz), density.reshape(held, 16, nz), zband, yband,
        pressure_old, pressure_now, adjoint_next, adjoint_now,
    )
    gradient = pl.pallas_call(
        pass_on,
        out_shape=jax.ShapeDtypeStruct(gradient.shape, jnp.float32),
        in_specs=[hbm], out_specs=hbm,
        scratch_shapes=[pltpu.VMEM(gradient.shape, jnp.float32), dma((8,)), dma((8,))],
        compiler_params=pltpu.CompilerParams(vmem_limit_bytes=56 * 1024 * 1024),
    )(gradient)
    return gradient.reshape(held, 4 // cores, 4, nz)


def solution(mesh):
    whole = P(("grp", "own"), None, None, None)
    fields = P(("grp", "own"), "shot", None, None, None, None)
    in_specs = (
        whole, whole, P("grp"), P("grp", None, None, None),
        P(("grp", "own"), "shot", None),
        P(("grp", "own"), "shot", None, None),
        P(("grp", "own"), "shot", None, None),
        P(("grp", "own"), "shot", None, None, None),
        fields, fields, fields, fields,
    )
    return jax.shard_map(
        per_device, mesh=mesh, in_specs=in_specs,
        out_specs=P(("grp", "own"), "shot", None, None), check_vma=False,
    )
```

```python
import functools

import jax
import jax.numpy as jnp
import numpy as np
from jax import lax
from jax.experimental import pallas as pl
from jax.experimental.pallas import tpu as pltpu
from jax.sharding import PartitionSpec as P

COURANT = 0.09
LEAD = 1225.0 / 1024.0
RATIOS = (1.0, -1.0 / 15.0, 1.0 / 125.0, -1.0 / 1715.0)
BAND = 105.0
GROUP = 8
LANE_BITS = 7
CODES = 32760.0
SMALL = 1e-30
MESH = pl.DeviceIdType.MESH


def difference_matrices(length):
    grad = np.zeros((length, length), np.float32)
    div = np.zeros((length, length), np.float32)
    for i in range(length):
        for m, ratio in enumerate(RATIOS, start=1):
            if i + m < length:
                grad[i, i + m] += BAND * ratio
            if i + 1 - m >= 0:
                grad[i, i + 1 - m] -= BAND * ratio
            if i + m - 1 < length:
                div[i, i + m - 1] += BAND * ratio
            if i - m >= 0:
                div[i, i - m] -= BAND * ratio
    return grad, div


def depth_bands(depth):
    grad, div = difference_matrices(depth)
    return jnp.asarray(np.stack([np.concatenate([a.T, a.T], axis=0) for a in (grad, div)]), jnp.bfloat16)


def line_bands(length):
    return jnp.asarray(np.stack([np.kron(np.eye(GROUP, dtype=np.float32), a) for a in difference_matrices(length)]), jnp.bfloat16)


def taps(at, low):
    total = None
    for m, ratio in enumerate(RATIOS, start=1):
        up, down = (at(m), at(1 - m)) if low else (at(m - 1), at(-m))
        if up is None and down is None:
            continue
        diff = up - down if up is not None and down is not None else (up if down is None else -down)
        term = diff if m == 1 else ratio * diff
        total = term if total is None else total + term
    return total


def halves(value):
    high = value.astype(jnp.bfloat16)
    return high, (value - high.astype(jnp.float32)).astype(jnp.bfloat16)


def dot(a, b):
    return jnp.dot(a, b, preferred_element_type=jnp.float32)


def shots_kernel(
    home_hbm, foot_hbm, source_hbm, cells_hbm, wave_hbm, obs_hbm,
    vel_hbm, rho_hbm, zband_hbm, yband_hbm, old_hbm, now_hbm, next_hbm, adj_hbm,
    out_ref, *rest,
):
    members, foot = foot_hbm.shape[2:]
    models, rest = rest[: 2 * members], rest[2 * members :]
    leaving, rest = rest[: 2 * members], rest[2 * members :]
    outgoing, rest = rest[:members], rest[members:]
    arrived, rest = rest[:members], rest[members:]
    (
        vel_tab, rho_tab, zband, yband, old_ref, now_ref, next_ref, adj_ref,
        rho, vel, buoy, hx, hy, hz, sum_p, sum_q, image_one, adj_one, second, third, image_two, mixed, wide_p, wide_q, tiles,
        misfit, decoded, scale_out, scale_in, homes_ref, book, rows_ref, lists_ref, table_sems,
        home_ref, foot_ref, source_ref, cells_ref, wave_ref, obs_ref, lanes_ref, picks, upright_obs, pick_z, lead_p, lead_q,
        load_sems, keep_sems, model_send, model_recv, grad_send, grad_recv, scale_send, scale_recv,
    ) = rest
    owners, cap = leaving[0].shape[:2]
    cores = lax.axis_size("shot")
    nx, ny, nz = now_ref.shape[1:]
    grid_y = ny // 4
    tiles_y = ny // 8
    rows = GROUP * ny
    me = lax.axis_index("own")
    whole_me = me * cores + lax.axis_index("shot")
    peers = owners * cores
    lane = lax.broadcasted_iota(jnp.int32, (1, nz), 1)

    loads = [
        pltpu.make_async_copy(src, dst, load_sems.at[i])
        for i, (src, dst) in enumerate((
            (home_hbm, home_ref), (foot_hbm, foot_ref), (rho_hbm, rho_tab), (vel_hbm, vel_tab), (zband_hbm, zband), (yband_hbm, yband),
            (now_hbm.at[0, 0], now_ref), (adj_hbm.at[0, 0], adj_ref), (old_hbm.at[0, 0], old_ref), (next_hbm.at[0, 0], next_ref),
            (cells_hbm, lanes_ref), (obs_hbm, obs_ref), (cells_hbm, cells_ref), (source_hbm, source_ref), (wave_hbm, wave_ref),
        ))
    ]
    for load in loads:
        load.start()
    barrier = pltpu.get_barrier_semaphore()

    def device(peer):
        return {"own": peer // cores, "shot": peer % cores}

    def greet(d, carry):
        pl.semaphore_signal(barrier, inc=1, device_id=device((whole_me + d) % peers), device_id_type=MESH)
        return carry

    lax.fori_loop(1, peers, greet, 0)

    def model_copy(phase, d):
        peer = (me + d) % owners
        return pltpu.make_async_remote_copy(
            src_ref=leaving[phase].at[peer], dst_ref=models[phase].at[pl.ds(me * cap, cap)],
            send_sem=model_send.at[phase, d], recv_sem=model_recv.at[phase, d],
            device_id={"own": peer}, device_id_type=MESH,
        )

    def grad_copy(member, d):
        peer = (whole_me + d) % peers
        return pltpu.make_async_remote_copy(
            src_ref=outgoing[member].at[peer], dst_ref=arrived[member].at[whole_me],
            send_sem=grad_send.at[member, d], recv_sem=grad_recv.at[member, d],
            device_id=device(peer), device_id_type=MESH,
        )

    def scale_copy(member, d):
        peer = (whole_me + d) % peers
        return pltpu.make_async_remote_copy(
            src_ref=scale_out.at[member], dst_ref=scale_in.at[member, whole_me],
            send_sem=scale_send.at[member, d], recv_sem=scale_recv.at[member, d],
            device_id=device(peer), device_id_type=MESH,
        )

    def each(count, act):
        def body(d, carry):
            act(d)
            return carry

        lax.fori_loop(1, count, body, 0)

    held = vel_tab.shape[0]
    count_tiles = home_ref.shape[0] * nz
    side = int(round(count_tiles ** 0.5))
    edge = int(round(foot ** 0.5))
    bits = lambda size: size.bit_length() - 1
    iota = lambda shape, axis: lax.broadcasted_iota(jnp.int32, shape, axis)
    narrow = lambda value: value.astype(jnp.float32).astype(jnp.bfloat16)
    across = lambda a, b: lax.dot_general(a, b, (((1,), (1,)), ((), ())), preferred_element_type=jnp.float32)
    blocks = home_ref.shape[0]

    def locate():
        home = home_ref[...]
        high, low = lax.shift_right_logical(home, LANE_BITS), home & (nz - 1)
        hit, full, own = [], [], []
        mine = lax.shift_right_logical(me * held, LANE_BITS)
        for i in range(blocks):
            tile = i * nz + iota((1, nz), 1)
            where = lax.shift_right_logical(tile, bits(side)), tile & (side - 1)
            hit.append(narrow(low[i : i + 1] == iota((nz, nz), 0)))
            high_row = high[i : i + 1]
            full.append(narrow(jnp.concatenate([jnp.where(high_row == iota((blocks, nz), 0), w, 0) for w in where], axis=0)))
            own.append(narrow(jnp.concatenate([jnp.broadcast_to(jnp.where(high_row == mine, w, 0), (nz, nz)) for w in where], axis=0)))
        hit, full, own = (jnp.concatenate(parts, axis=1) for parts in (hit, full, own))
        return across(full, hit).astype(jnp.int32), across(hit, own).astype(jnp.int32)

    def inside(dx, dy):
        return (dx >= 0) & (dx < edge) & (dy >= 0) & (dy < edge)

    def first_of(owner, core, member):
        first = foot_ref[owner, core, member, 0]
        return lax.shift_right_logical(first, bits(side)), first & (side - 1)

    total = peers * cap
    share = bits(held)
    spot_x, spot_y = iota((nz, nz), 0), iota((nz, nz), 1)
    same = lax.shift_right_logical(spot_x, share) == lax.shift_right_logical(spot_y, share)
    for load in loads[:2]:
        load.wait()
    positions, own_positions = locate()
    book[...] = jnp.zeros_like(book)
    in_share = lax.shift_right_logical(iota((nz, total), 0), share) == me % (nz >> share)
    before = narrow(same & (spot_y < spot_x))
    for member in range(members):
        first = jnp.zeros((1, total), jnp.int32)
        shot_of = lax.shift_right_logical(iota((1, total), 1), bits(cap))
        for peer in range(peers):
            first = jnp.where(shot_of == peer, foot_ref[peer // cores, peer % cores, member, 0], first)
        dx = own_positions[:, :nz] - lax.shift_right_logical(first, bits(side))
        dy = own_positions[:, nz:] - (first & (side - 1))
        chosen = inside(dx, dy) & in_share
        order = dot(before, narrow(chosen)).astype(jnp.int32)
        chosen = chosen & (order == (iota((1, total), 1) & (cap - 1)))
        local = jnp.where(chosen, iota((nz, total), 0) & (held - 1), 0)
        homes = jnp.clip(jnp.sum(local, axis=0, keepdims=True), 0, held - 1)
        homes_ref[pl.ds(member, 1), :] = homes
        book[pl.ds(member, 1), :] = homes
    rows_copy = pltpu.make_async_copy(book.at[pl.ds(0, 8)], rows_ref, table_sems.at[0])
    lists_copy = pltpu.make_async_copy(book.at[pl.ds(8, book.shape[0] - 8)], lists_ref, table_sems.at[1])
    rows_copy.start()

    def list_tiles():
        after = narrow(same & (spot_x < spot_y))
        keys, values = [], []
        cell = iota((blocks, nz), 0) * nz + iota((blocks, nz), 1)
        owner = lax.shift_right_logical(cell, share)
        for member in range(members):
            at_x, at_y = first_of(me, lax.axis_index("shot"), member)
            dx, dy = positions[:blocks] - at_x, positions[blocks:] - at_y
            chosen = inside(dx, dy)
            order = dot(narrow(chosen), after).astype(jnp.int32)
            slot = owner * cap + order
            key, value = [], []
            for i in range(blocks):
                row = lambda field: field[i : i + 1]
                valid = row(chosen.astype(jnp.int32)) == 1
                small = iota((8, nz), 0)
                key.append(narrow(jnp.concatenate([
                    jnp.where(valid & (row(dx) == small), 1, 0),
                    jnp.where(valid & (row(owner) == iota((owners, nz), 0)), 1, 0),
                ], axis=0)))
                value.append(narrow(jnp.concatenate([
                    jnp.where(row(dy) == small, row(slot), 0),
                    jnp.where(row(order) == small, row(dx) * edge + row(dy), 0),
                ], axis=0)))
            keys.append(jnp.concatenate(key, axis=1))
            values.append(jnp.concatenate(value, axis=1))
        values.append(jnp.zeros((nz - 16 * members, blocks * nz), jnp.bfloat16))
        found = across(jnp.concatenate(keys, axis=0), jnp.concatenate(values, axis=0)).astype(jnp.int32)
        book[pl.ds(8, found.shape[0]), :] = jnp.clip(found, 0, foot - 1)
        lists_copy.start()

    def slot_at(member, kx, ky):
        return lists_ref[member * (8 + owners) + kx, member * 16 + ky]

    def spot_at(member, owner, j):
        return lists_ref[member * (8 + owners) + 8 + owner, member * 16 + 8 + j]

    def collect(table, member, peer, out):
        for j in range(cap):
            tile = table[rows_ref[member, (peer * cores + lax.axis_index("shot")) * cap + j]]
            if len(out.shape) == 4:
                out[peer, j] = tile
            else:
                out[peer * cap + j] = tile

    rows_copy.wait()
    loads[2].wait()
    for phase in range(2 * members):
        member, table = phase // 2, (rho_tab, vel_tab)[phase % 2]
        if phase == 1:
            loads[3].wait()
        if phase == 0:
            each(owners, lambda d: collect(table, member, (me + d) % owners, leaving[phase]))
            pl.semaphore_wait(barrier, peers - 1)
            each(owners, lambda d: model_copy(phase, d).start())
            list_tiles()
        else:
            def send(d):
                collect(table, member, (me + d) % owners, leaving[phase])
                model_copy(phase, d).start()

            each(owners, send)
        collect(table, member, me, models[phase])

    def unpack(member, arrival, field):
        def body(kx, carry):
            for ky in range(grid_y):
                slot = slot_at(member, kx, ky)
                tile = arrival[slot].astype(jnp.float32)
                for i in range(4):
                    field[kx * 4 + i, pl.ds(ky * 4, 4), :] = tile[4 * i : 4 * i + 4]
            return carry

        lax.fori_loop(0, nx // 4, body, 0, unroll=2)

    def divergence(value, half, transposed):
        high, low = halves(half * value)
        if transposed:
            return dot(jnp.concatenate([yband[1], yband[1]], axis=1), jnp.concatenate([high, low], axis=0))
        return dot(jnp.concatenate([high, low], axis=1), zband[1])

    def planes(ref, g, *lead):
        return ref[(*lead, pl.ds(pl.multiple_of(g * GROUP, GROUP), GROUP))].reshape(rows, nz)

    def lines(first, second_block, first_half, second_half, exact):
        pair = lambda a, b: jnp.concatenate([a, b], axis=1)
        stack = lambda a, b: jnp.concatenate([a, b], axis=0)
        if exact:
            grad_z = dot(stack(first, second_block), zband[0, :nz])
            grad_y = dot(yband[0], pair(first, second_block))
        else:
            (high_a, low_a), (high_b, low_b) = halves(first), halves(second_block)
            grad_z = dot(stack(pair(high_a, low_a), pair(high_b, low_b)), zband[0])
            grad_y = dot(pair(yband[0], yband[0]), stack(pair(high_a, high_b), pair(low_a, low_b)))
        (hy_a, hz_a), (hy_b, hz_b) = first_half, second_half
        div_z = divergence(grad_z, stack(hz_a, hz_b), False)
        div_y = divergence(grad_y, pair(hy_a, hy_b), True)
        return div_z[:rows] + div_y[:, :nz], div_z[rows:] + div_y[:, nz:]

    def cut(g):
        return planes(hy, g), planes(hz, g)

    def put(ref, g, block):
        ref[pl.ds(pl.multiple_of(g * GROUP, GROUP), GROUP)] = block.reshape(GROUP, ny, nz)

    def columns(jobs):
        def body(ty, peak):
            start = pl.multiple_of(ty * 8, 8)
            here = pl.ds(start, 8)
            for load, rest_sum, finish in jobs:
                values, fluxes = {}, {}

                def value_at(x):
                    if x < 0 or x >= nx:
                        return None
                    if x not in values:
                        values[x] = load(x, here)
                    return values[x]

                def flux_at(x):
                    if x < 0 or x >= nx:
                        return None
                    if x not in fluxes:
                        fluxes[x] = hx[x, here, :] * taps(lambda shift: value_at(x + shift), True)
                    return fluxes[x]

                for x in range(nx):
                    total = rest_sum[x, here, :] + taps(lambda shift: flux_at(x + shift), False)
                    size = finish(x, ty, here, value_at(x), total)
                    if size is not None:
                        peak = jnp.maximum(peak, size)
            return peak

        return lax.fori_loop(0, tiles_y, body, jnp.zeros((8, nz), jnp.float32))

    def single(field):
        def body(pair_index, carry):
            g = pair_index * 2
            one, two = lines(planes(field, g), planes(field, g + 1), cut(g), cut(g + 1), False)
            put(sum_p, g, one)
            put(sum_p, g + 1, two)
            return carry

        lax.fori_loop(0, nx // GROUP // 2, body, 0, unroll=True)

    def source_term(member, step, base, shape):
        local = lax.broadcasted_iota(jnp.int32, shape, 0) * nz + lax.broadcasted_iota(jnp.int32, shape, 1)
        return jnp.where(local == source_ref[0, 0, member] - base, wave_ref[0, 0, member, step], 0.0)

    def first_half(member):
        each(owners, lambda d: model_copy(2 * member, d).wait())
        unpack(member, models[2 * member], rho)

        def prepare(x, carry):
            value = (0.5 * LEAD * LEAD) / rho[x]
            buoy[x, pl.ds(0, ny), :] = value
            buoy[x, pl.ds(ny, 1), :] = value[ny - 1 :]
            return carry

        lax.fori_loop(0, nx, prepare, 0, unroll=4)

        def between(x, carry):
            here = buoy[x, pl.ds(0, ny), :]
            hx[x] = here + buoy[jnp.minimum(x + 1, nx - 1), pl.ds(0, ny), :]
            hy[x] = (here + buoy[x, pl.ds(1, ny), :]) * (1.0 / (BAND * BAND))
            shifted = jnp.where(lane == nz - 1, here, pltpu.roll(here, nz - 1, 1))
            hz[x] = (here + shifted) * (1.0 / (BAND * BAND))
            return carry

        lax.fori_loop(0, nx, between, 0, unroll=8)
        if member == 0:
            for load in loads[4:]:
                load.wait()

        count = cells_ref.shape[-1]
        upright = lambda row: jnp.broadcast_to(row, (nz, count)).T
        cells = lanes_ref[0, 0, pl.ds(member, 1), :]
        pick_z[...] = (upright((cells & (nz - 1)).astype(jnp.float32)) == iota((count, nz), 1).astype(jnp.float32)).astype(jnp.float32)
        for step in range(2):
            upright_obs[step] = upright(obs_ref[0, 0, member, pl.ds(1 - step, 1), :])
        line_of = lax.shift_right_logical(cells, LANE_BITS)

        def both(g, carry):
            part = pl.ds(pl.multiple_of(g * rows, rows), rows)
            picks[part, :] = narrow(iota((rows, count), 0) + g * rows == line_of)
            first, other = planes(now_ref, g, member), planes(adj_ref, g, member)
            wide, wide_other = first.astype(jnp.float32), other.astype(jnp.float32)
            put(wide_p, g, wide)
            put(wide_q, g, wide_other)
            put(lead_p, g, 2.0 * wide - planes(old_ref, g, member).astype(jnp.float32))
            put(lead_q, g, 2.0 * wide_other - planes(next_ref, g, member).astype(jnp.float32))
            one, two = lines(first, other, cut(g), cut(g), True)
            put(sum_p, g, one)
            put(sum_q, g, two)
            return carry

        lax.fori_loop(0, nx // GROUP, both, 0, unroll=True)

        def keep_p(x, ty, here, value, total):
            image_one[x, here, :] = total

        def keep_q(x, ty, here, value, total):
            adj_one[x, here, :] = total

        columns((
            (lambda x, here: wide_p[x, here, :], sum_p, keep_p),
            (lambda x, here: wide_q[x, here, :], sum_q, keep_q),
        ))

    def second_half(member):
        unpack(member, models[2 * member + 1], vel)
        coupling, weight = vel, rho

        def advance(x, carry):
            velocity, density = vel[x], rho[x]
            scale = (COURANT * velocity) * (COURANT * velocity) * density
            coupling[x] = scale
            weight[x] = velocity * density
            second[x] = lead_p[x] + scale * image_one[x] + source_term(member, 0, x * (ny * nz), (ny, nz))
            adj_one[x] = lead_q[x] + scale * adj_one[x]
            return carry

        lax.fori_loop(0, nx, advance, 0, unroll=4)
        single(second)

        def finish_two(x, ty, here, value, total):
            image_two[x, here, :] = total
            third[x, here, :] = 2.0 * value - wide_p[x, here, :] + coupling[x, here, :] * total + source_term(member, 1, (x * ny + ty * 8) * nz, (8, nz))

        columns(((lambda x, here: second[x, here, :], sum_p, finish_two),))
        count = cells_ref.shape[-1]

        def receive(step, carry):
            for sub in range(16):
                n = step * 16 + sub
                line = lax.shift_right_logical(cells_ref[0, 0, member, n], LANE_BITS)
                spot = pl.ds(lax.bitwise_and(line, ny - 1), 1)
                x = lax.shift_right_logical(line, ny.bit_length() - 1)
                misfit[0, pl.ds(n, 1), :] = third[x, spot, :]
                misfit[1, pl.ds(n, 1), :] = second[x, spot, :]
            return carry

        lax.fori_loop(0, count // 16, receive, 0)
        amounts = [
            jnp.where(pick_z[...] > 0.5, misfit[step] - upright_obs[step], 0.0) for step in range(2)
        ]
        amounts = jnp.concatenate(halves(jnp.concatenate(amounts, axis=1)), axis=0)

        def deliver(g, carry):
            pick = picks[pl.ds(pl.multiple_of(g * rows, rows), rows), :]
            added = dot(jnp.concatenate([pick, pick], axis=1), amounts)
            put(adj_one, g, planes(adj_one, g) + added[:, :nz])
            put(mixed, g, added[:, nz:] - planes(wide_q, g))
            return carry

        lax.fori_loop(0, nx // GROUP, deliver, 0, unroll=True)
        single(adj_one)

        def finish_four(x, ty, here, value, total):
            q0 = 2.0 * value + mixed[x, here, :] + coupling[x, here, :] * total
            result = weight[x, here, :] * (value * image_two[x, here, :] + q0 * image_one[x, here, :])
            size = jnp.abs(result)
            root = result * lax.rsqrt(jnp.maximum(size, SMALL))
            for half in range(2):
                spot = (x // 4) * grid_y + ty * 2 + half
                tiles[spot, (x % 4) // 2, pl.ds((x % 2) * 4, 4), :] = root[4 * half : 4 * half + 4]
            return size

        peak = columns(((lambda x, here: adj_one[x, here, :], sum_p, finish_four),))
        top = jnp.maximum(jnp.max(peak, axis=(0, 1), keepdims=True), SMALL)
        factor = jnp.broadcast_to(CODES * lax.rsqrt(top), (8, nz))
        scale = jnp.broadcast_to(top * (2.0 * COURANT * COURANT / (CODES * CODES)), (1, nz))
        scale_out[member] = scale
        scale_in[member, whole_me] = scale

        def pack(owner, carry):
            for core in range(cores):
                parts = []
                for j in range(0, cap):
                    parts.append(jnp.round(tiles[spot_at(member, owner, j), core] * factor))
                if cap % 2:
                    parts.append(jnp.zeros((8, nz), jnp.float32))
                for j in range(0, len(parts), 2):
                    code = jnp.concatenate(parts[j : j + 2], axis=0).astype(jnp.int32).astype(jnp.int16)
                    outgoing[member][owner * cores + core, pl.ds(8 * j, 16), :] = code
            return carry

        lax.fori_loop(0, owners, pack, 0)

    keeps = [
        pltpu.make_async_copy(outgoing[member].at[whole_me], arrived[member].at[whole_me], keep_sems.at[member])
        for member in range(members)
    ]

    def dispatch(member):
        each(peers, lambda d: scale_copy(member, d).start())
        each(peers, lambda d: grad_copy(member, d).start())
        keeps[member].start()

    def add_up(member):
        per = cap * 8

        def decode(source):
            code = arrived[member][source].astype(jnp.int32).astype(jnp.float32)[:per]
            decoded[pl.ds(pl.multiple_of(source * per, per), per), :] = code * jnp.abs(code) * scale_in[member, source]

        keeps[member].wait()
        decode(whole_me)

        def accept(d):
            scale_copy(member, d).wait()
            grad_copy(member, d).wait()
            decode((whole_me + peers - d) % peers)

        each(peers, accept)
        pick = (lax.broadcasted_iota(jnp.int32, (held, total), 0) == homes_ref[pl.ds(member, 1), :]).astype(jnp.float32).astype(jnp.bfloat16)
        pick = jnp.concatenate([pick, pick], axis=1)
        for i in range(8):
            part = dot(pick, jnp.concatenate(halves(decoded[pl.ds(i, total, stride=8), :]), axis=0))
            mine = pl.ds(i, held, stride=8)
            out_ref[mine, :] = part if member == 0 else out_ref[mine, :] + part

    lists_copy.wait()
    for member in range(members):
        first_half(member)
        if member == members - 1:
            for done in range(members - 1):
                dispatch(done)
        each(owners, lambda d: model_copy(2 * member + 1, d).wait())
        second_half(member)
    dispatch(members - 1)
    for member in range(members):
        add_up(member)


def per_device(
    velocity, density, tile_home, footprints, source_cell, source_wave, receivers, observed,
    pressure_old, pressure_now, adjoint_next, adjoint_now,
):
    owners = lax.axis_size("own")
    cores = lax.axis_size("shot")
    held = velocity.shape[0]
    members, foot = footprints.shape[2:]
    cap = foot // owners
    nx, ny, nz = pressure_now.shape[-3:]
    home = tile_home.reshape(-1, nz)
    hbm = pl.BlockSpec(memory_space=pltpu.HBM)
    field = pltpu.VMEM((nx, ny, nz), jnp.float32)
    stored = pltpu.VMEM((members, nx, ny, nz), jnp.bfloat16)
    table = pltpu.VMEM((held, 16, nz), jnp.bfloat16)
    model = pltpu.VMEM((owners, cap, 16, nz), jnp.bfloat16)
    peers = owners * cores
    grads = pltpu.VMEM((peers, (cap * 8 + 15) // 16 * 16, nz), jnp.int16)
    zband, yband = depth_bands(nz), line_bands(ny)
    count = receivers.shape[-1]
    lists = members * (8 + owners)
    dma = pltpu.SemaphoreType.DMA
    gradient = pl.pallas_call(
        shots_kernel,
        out_shape=jax.ShapeDtypeStruct((held * 8, nz), jnp.float32),
        in_specs=[hbm] * 14,
        out_specs=pl.BlockSpec(memory_space=pltpu.VMEM),
        scratch_shapes=[pltpu.VMEM((foot, 16, nz), jnp.bfloat16)] * (2 * members) + [model] * (2 * members) + [grads] * (2 * members) + [
            table, table, pltpu.VMEM(zband.shape, jnp.bfloat16), pltpu.VMEM(yband.shape, jnp.bfloat16),
            stored, stored, stored, stored,
            field, field, pltpu.VMEM((nx, ny + 8, nz), jnp.float32)] + [field] * 13 + [
            pltpu.VMEM((foot, 2, 8, nz), jnp.float32), pltpu.VMEM((2, count, nz), jnp.float32),
            pltpu.VMEM((peers * cap * 8, nz), jnp.float32), pltpu.VMEM((members, 1, nz), jnp.float32), pltpu.VMEM((members, peers, 1, nz), jnp.float32),
            pltpu.VMEM((members, peers * cap), jnp.int32),
            pltpu.VMEM((8 + lists, nz), jnp.int32), pltpu.SMEM((8, nz), jnp.int32), pltpu.SMEM((lists, nz), jnp.int32), dma((2,)),
            pltpu.VMEM(home.shape, jnp.int32), pltpu.SMEM(footprints.shape, jnp.int32), pltpu.SMEM(source_cell.shape, jnp.int32),
            pltpu.SMEM(receivers.shape, jnp.int32), pltpu.SMEM(source_wave.shape, jnp.float32),
            pltpu.VMEM(observed.shape, jnp.float32), pltpu.VMEM(receivers.shape, jnp.int32),
            pltpu.VMEM((nx * ny, count), jnp.bfloat16), pltpu.VMEM((2, count, nz), jnp.float32), pltpu.VMEM((count, nz), jnp.float32), field, field,
            dma((15,)), dma((members,)), dma((2 * members, owners)), dma((2 * members, owners)),
            dma((members, peers)), dma((members, peers)), dma((members, peers)), dma((members, peers)),
        ],
        compiler_params=pltpu.CompilerParams(collective_id=0, has_side_effects=True, vmem_limit_bytes=40 * 1024 * 1024),
        cost_estimate=pl.CostEstimate(flops=200_000_000, bytes_accessed=6_000_000, transcendentals=0),
    )(*(pltpu.with_memory_space_constraint(operand, pltpu.HBM) for operand in (
        home, footprints, source_cell, receivers, source_wave, observed,
        velocity.reshape(held, 16, nz), density.reshape(held, 16, nz), zband, yband,
        pressure_old, pressure_now, adjoint_next, adjoint_now,
    )))
    return gradient.reshape(held, 4 // cores, 4, nz)


def solution(mesh):
    whole = P(("grp", "own"), None, None, None)
    fields = P(("grp", "own"), "shot", None, None, None, None)
    in_specs = (
        whole, whole, P("grp"), P("grp", None, None, None),
        P(("grp", "own"), "shot", None),
        P(("grp", "own"), "shot", None, None),
        P(("grp", "own"), "shot", None, None),
        P(("grp", "own"), "shot", None, None, None),
        fields, fields, fields, fields,
    )
    return jax.shard_map(
        per_device, mesh=mesh, in_specs=in_specs,
        out_specs=P(("grp", "own"), "shot", None, None), check_vma=False,
    )
```

```python
import functools

import jax
import jax.numpy as jnp
import numpy as np
from jax import lax
from jax.experimental import pallas as pl
from jax.experimental.pallas import tpu as pltpu
from jax.sharding import PartitionSpec as P

COURANT = 0.09
LEAD = 1225.0 / 1024.0
RATIOS = (1.0, -1.0 / 15.0, 1.0 / 125.0, -1.0 / 1715.0)
BAND = 105.0
GROUP = 8
LANE_BITS = 7
CODES = 32760.0
SMALL = 1e-30
MESH = pl.DeviceIdType.MESH


def difference_matrices(length):
    grad = np.zeros((length, length), np.float32)
    div = np.zeros((length, length), np.float32)
    for i in range(length):
        for m, ratio in enumerate(RATIOS, start=1):
            if i + m < length:
                grad[i, i + m] += BAND * ratio
            if i + 1 - m >= 0:
                grad[i, i + 1 - m] -= BAND * ratio
            if i + m - 1 < length:
                div[i, i + m - 1] += BAND * ratio
            if i - m >= 0:
                div[i, i - m] -= BAND * ratio
    return grad, div


def depth_bands(depth):
    grad, div = difference_matrices(depth)
    return jnp.asarray(np.stack([np.concatenate([a.T, a.T], axis=0) for a in (grad, div)]), jnp.bfloat16)


def line_bands(length):
    return jnp.asarray(np.stack([np.kron(np.eye(GROUP, dtype=np.float32), a) for a in difference_matrices(length)]), jnp.bfloat16)


def taps(at, low):
    total = None
    for m, ratio in enumerate(RATIOS, start=1):
        up, down = (at(m), at(1 - m)) if low else (at(m - 1), at(-m))
        if up is None and down is None:
            continue
        diff = up - down if up is not None and down is not None else (up if down is None else -down)
        term = diff if m == 1 else ratio * diff
        total = term if total is None else total + term
    return total


def halves(value):
    high = value.astype(jnp.bfloat16)
    return high, (value - high.astype(jnp.float32)).astype(jnp.bfloat16)


def dot(a, b):
    return jnp.dot(a, b, preferred_element_type=jnp.float32)


def shots_kernel(
    home_hbm, foot_hbm, source_hbm, cells_hbm, wave_hbm, obs_hbm,
    vel_hbm, rho_hbm, zband_hbm, yband_hbm, old_hbm, now_hbm, next_hbm, adj_hbm,
    out_ref, *rest,
):
    members, foot = foot_hbm.shape[2:]
    models, rest = rest[: 2 * members], rest[2 * members :]
    leaving, rest = rest[: 2 * members], rest[2 * members :]
    outgoing, rest = rest[:members], rest[members:]
    arrived, rest = rest[:members], rest[members:]
    (
        vel_tab, rho_tab, zband, yband, old_ref, now_ref, next_ref, adj_ref,
        rho, vel, buoy, hx, hy, hz, sum_p, sum_q, image_one, adj_one, second, third, image_two, mixed, wide_p, wide_q, tiles,
        misfit, decoded, scale_out, scale_in, homes_ref, book, rows_ref, lists_ref, table_sems,
        home_ref, foot_ref, source_ref, cells_ref, wave_ref, obs_ref, lanes_ref, picks, upright_obs, pick_z, lead_p, lead_q,
        load_sems, keep_sems, model_send, model_recv, grad_send, grad_recv, scale_send, scale_recv,
    ) = rest
    owners, cap = leaving[0].shape[:2]
    cores = lax.axis_size("shot")
    nx, ny, nz = now_ref.shape[1:]
    grid_y = ny // 4
    tiles_y = ny // 8
    rows = GROUP * ny
    me = lax.axis_index("own")
    whole_me = me * cores + lax.axis_index("shot")
    peers = owners * cores
    lane = lax.broadcasted_iota(jnp.int32, (1, nz), 1)

    loads = [
        pltpu.make_async_copy(src, dst, load_sems.at[i])
        for i, (src, dst) in enumerate((
            (home_hbm, home_ref), (foot_hbm, foot_ref), (rho_hbm, rho_tab), (vel_hbm, vel_tab), (zband_hbm, zband), (yband_hbm, yband),
            (now_hbm.at[0, 0], now_ref), (adj_hbm.at[0, 0], adj_ref), (old_hbm.at[0, 0], old_ref), (next_hbm.at[0, 0], next_ref),
            (cells_hbm, lanes_ref), (obs_hbm, obs_ref), (cells_hbm, cells_ref), (source_hbm, source_ref), (wave_hbm, wave_ref),
        ))
    ]
    for load in loads:
        load.start()
    barrier = pltpu.get_barrier_semaphore()

    def device(peer):
        return {"own": peer // cores, "shot": peer % cores}

    def greet(d, carry):
        pl.semaphore_signal(barrier, inc=1, device_id=device((whole_me + d) % peers), device_id_type=MESH)
        return carry

    lax.fori_loop(1, peers, greet, 0)

    def model_copy(phase, d):
        peer = (me + d) % owners
        return pltpu.make_async_remote_copy(
            src_ref=leaving[phase].at[peer], dst_ref=models[phase].at[pl.ds(me * cap, cap)],
            send_sem=model_send.at[phase, d], recv_sem=model_recv.at[phase, d],
            device_id={"own": peer}, device_id_type=MESH,
        )

    def grad_copy(member, d):
        peer = (whole_me + d) % peers
        return pltpu.make_async_remote_copy(
            src_ref=outgoing[member].at[peer], dst_ref=arrived[member].at[whole_me],
            send_sem=grad_send.at[member, d], recv_sem=grad_recv.at[member, d],
            device_id=device(peer), device_id_type=MESH,
        )

    def scale_copy(member, d):
        peer = (whole_me + d) % peers
        return pltpu.make_async_remote_copy(
            src_ref=scale_out.at[member], dst_ref=scale_in.at[member, whole_me],
            send_sem=scale_send.at[member, d], recv_sem=scale_recv.at[member, d],
            device_id=device(peer), device_id_type=MESH,
        )

    def each(count, act):
        def body(d, carry):
            act(d)
            return carry

        lax.fori_loop(1, count, body, 0)

    held = vel_tab.shape[0]
    count_tiles = home_ref.shape[0] * nz
    side = int(round(count_tiles ** 0.5))
    edge = int(round(foot ** 0.5))
    bits = lambda size: size.bit_length() - 1
    iota = lambda shape, axis: lax.broadcasted_iota(jnp.int32, shape, axis)
    narrow = lambda value: value.astype(jnp.float32).astype(jnp.bfloat16)
    across = lambda a, b: lax.dot_general(a, b, (((1,), (1,)), ((), ())), preferred_element_type=jnp.float32)
    blocks = home_ref.shape[0]

    def locate():
        home = home_ref[...]
        high, low = lax.shift_right_logical(home, LANE_BITS), home & (nz - 1)
        hit, full, own = [], [], []
        mine = lax.shift_right_logical(me * held, LANE_BITS)
        for i in range(blocks):
            tile = i * nz + iota((1, nz), 1)
            where = lax.shift_right_logical(tile, bits(side)), tile & (side - 1)
            hit.append(narrow(low[i : i + 1] == iota((nz, nz), 0)))
            high_row = high[i : i + 1]
            full.append(narrow(jnp.concatenate([jnp.where(high_row == iota((blocks, nz), 0), w, 0) for w in where], axis=0)))
            own.append(narrow(jnp.concatenate([jnp.broadcast_to(jnp.where(high_row == mine, w, 0), (nz, nz)) for w in where], axis=0)))
        hit, full, own = (jnp.concatenate(parts, axis=1) for parts in (hit, full, own))
        return across(full, hit).astype(jnp.int32), across(hit, own).astype(jnp.int32)

    def inside(dx, dy):
        return (dx >= 0) & (dx < edge) & (dy >= 0) & (dy < edge)

    def first_of(owner, core, member):
        first = foot_ref[owner, core, member, 0]
        return lax.shift_right_logical(first, bits(side)), first & (side - 1)

    total = peers * cap
    share = bits(held)
    spot_x, spot_y = iota((nz, nz), 0), iota((nz, nz), 1)
    same = lax.shift_right_logical(spot_x, share) == lax.shift_right_logical(spot_y, share)
    for load in loads[:2]:
        load.wait()
    positions, own_positions = locate()
    book[...] = jnp.zeros_like(book)
    in_share = lax.shift_right_logical(iota((nz, total), 0), share) == me % (nz >> share)
    before = narrow(same & (spot_y < spot_x))
    for member in range(members):
        first = jnp.zeros((1, total), jnp.int32)
        shot_of = lax.shift_right_logical(iota((1, total), 1), bits(cap))
        for peer in range(peers):
            first = jnp.where(shot_of == peer, foot_ref[peer // cores, peer % cores, member, 0], first)
        dx = own_positions[:, :nz] - lax.shift_right_logical(first, bits(side))
        dy = own_positions[:, nz:] - (first & (side - 1))
        chosen = inside(dx, dy) & in_share
        order = dot(before, narrow(chosen)).astype(jnp.int32)
        chosen = chosen & (order == (iota((1, total), 1) & (cap - 1)))
        local = jnp.where(chosen, iota((nz, total), 0) & (held - 1), 0)
        homes = jnp.clip(jnp.sum(local, axis=0, keepdims=True), 0, held - 1)
        homes_ref[pl.ds(member, 1), :] = homes
        book[pl.ds(member, 1), :] = homes
    rows_copy = pltpu.make_async_copy(book.at[pl.ds(0, 8)], rows_ref, table_sems.at[0])
    lists_copy = pltpu.make_async_copy(book.at[pl.ds(8, book.shape[0] - 8)], lists_ref, table_sems.at[1])
    rows_copy.start()

    def list_tiles():
        after = narrow(same & (spot_x < spot_y))
        keys, values = [], []
        cell = iota((blocks, nz), 0) * nz + iota((blocks, nz), 1)
        owner = lax.shift_right_logical(cell, share)
        for member in range(members):
            at_x, at_y = first_of(me, lax.axis_index("shot"), member)
            dx, dy = positions[:blocks] - at_x, positions[blocks:] - at_y
            chosen = inside(dx, dy)
            order = dot(narrow(chosen), after).astype(jnp.int32)
            slot = owner * cap + order
            key, value = [], []
            for i in range(blocks):
                row = lambda field: field[i : i + 1]
                valid = row(chosen.astype(jnp.int32)) == 1
                small = iota((8, nz), 0)
                key.append(narrow(jnp.concatenate([
                    jnp.where(valid & (row(dx) == small), 1, 0),
                    jnp.where(valid & (row(owner) == iota((owners, nz), 0)), 1, 0),
                ], axis=0)))
                value.append(narrow(jnp.concatenate([
                    jnp.where(row(dy) == small, row(slot), 0),
                    jnp.where(row(order) == small, row(dx) * edge + row(dy), 0),
                ], axis=0)))
            keys.append(jnp.concatenate(key, axis=1))
            values.append(jnp.concatenate(value, axis=1))
        values.append(jnp.zeros((nz - 16 * members, blocks * nz), jnp.bfloat16))
        found = across(jnp.concatenate(keys, axis=0), jnp.concatenate(values, axis=0)).astype(jnp.int32)
        book[pl.ds(8, found.shape[0]), :] = jnp.clip(found, 0, foot - 1)
        lists_copy.start()

    def slot_at(member, kx, ky):
        return lists_ref[member * (8 + owners) + kx, member * 16 + ky]

    def spot_at(member, owner, j):
        return lists_ref[member * (8 + owners) + 8 + owner, member * 16 + 8 + j]

    def collect(table, member, peer, out):
        for j in range(cap):
            tile = table[rows_ref[member, (peer * cores + lax.axis_index("shot")) * cap + j]]
            if len(out.shape) == 4:
                out[peer, j] = tile
            else:
                out[peer * cap + j] = tile

    rows_copy.wait()
    loads[2].wait()
    for phase in range(2 * members):
        member, table = phase // 2, (rho_tab, vel_tab)[phase % 2]
        if phase == 1:
            loads[3].wait()
        if phase == 0:
            each(owners, lambda d: collect(table, member, (me + d) % owners, leaving[phase]))
            pl.semaphore_wait(barrier, peers - 1)
            each(owners, lambda d: model_copy(phase, d).start())
            list_tiles()
        else:
            def send(d):
                collect(table, member, (me + d) % owners, leaving[phase])
                model_copy(phase, d).start()

            each(owners, send)
        collect(table, member, me, models[phase])

    def unpack(member, arrival, field):
        def body(kx, carry):
            for ky in range(grid_y):
                slot = slot_at(member, kx, ky)
                tile = arrival[slot].astype(jnp.float32)
                for i in range(4):
                    field[kx * 4 + i, pl.ds(ky * 4, 4), :] = tile[4 * i : 4 * i + 4]
            return carry

        lax.fori_loop(0, nx // 4, body, 0, unroll=2)

    def divergence(value, half, transposed):
        high, low = halves(half * value)
        if transposed:
            return dot(jnp.concatenate([yband[1], yband[1]], axis=1), jnp.concatenate([high, low], axis=0))
        return dot(jnp.concatenate([high, low], axis=1), zband[1])

    def planes(ref, g, *lead):
        return ref[(*lead, pl.ds(pl.multiple_of(g * GROUP, GROUP), GROUP))].reshape(rows, nz)

    def lines(first, second_block, first_half, second_half, exact):
        pair = lambda a, b: jnp.concatenate([a, b], axis=1)
        stack = lambda a, b: jnp.concatenate([a, b], axis=0)
        if exact:
            grad_z = dot(stack(first, second_block), zband[0, :nz])
            grad_y = dot(yband[0], pair(first, second_block))
        else:
            (high_a, low_a), (high_b, low_b) = halves(first), halves(second_block)
            grad_z = dot(stack(pair(high_a, low_a), pair(high_b, low_b)), zband[0])
            grad_y = dot(pair(yband[0], yband[0]), stack(pair(high_a, high_b), pair(low_a, low_b)))
        (hy_a, hz_a), (hy_b, hz_b) = first_half, second_half
        div_z = divergence(grad_z, stack(hz_a, hz_b), False)
        div_y = divergence(grad_y, pair(hy_a, hy_b), True)
        return div_z[:rows] + div_y[:, :nz], div_z[rows:] + div_y[:, nz:]

    def cut(g):
        return planes(hy, g), planes(hz, g)

    def put(ref, g, block):
        ref[pl.ds(pl.multiple_of(g * GROUP, GROUP), GROUP)] = block.reshape(GROUP, ny, nz)

    def columns(jobs):
        def body(ty, peak):
            start = pl.multiple_of(ty * 8, 8)
            here = pl.ds(start, 8)
            for load, rest_sum, finish in jobs:
                values, fluxes = {}, {}

                def value_at(x):
                    if x < 0 or x >= nx:
                        return None
                    if x not in values:
                        values[x] = load(x, here)
                    return values[x]

                def flux_at(x):
                    if x < 0 or x >= nx:
                        return None
                    if x not in fluxes:
                        fluxes[x] = hx[x, here, :] * taps(lambda shift: value_at(x + shift), True)
                    return fluxes[x]

                for x in range(nx):
                    total = rest_sum[x, here, :] + taps(lambda shift: flux_at(x + shift), False)
                    size = finish(x, ty, here, value_at(x), total)
                    if size is not None:
                        peak = jnp.maximum(peak, size)
            return peak

        return lax.fori_loop(0, tiles_y, body, jnp.zeros((8, nz), jnp.float32))

    def single(field):
        def body(pair_index, carry):
            g = pair_index * 2
            one, two = lines(planes(field, g), planes(field, g + 1), cut(g), cut(g + 1), False)
            put(sum_p, g, one)
            put(sum_p, g + 1, two)
            return carry

        lax.fori_loop(0, nx // GROUP // 2, body, 0, unroll=True)

    def source_term(member, step, base, shape):
        local = lax.broadcasted_iota(jnp.int32, shape, 0) * nz + lax.broadcasted_iota(jnp.int32, shape, 1)
        return jnp.where(local == source_ref[0, 0, member] - base, wave_ref[0, 0, member, step], 0.0)

    def first_half(member):
        each(owners, lambda d: model_copy(2 * member, d).wait())
        unpack(member, models[2 * member], rho)

        def prepare(x, carry):
            value = (0.5 * LEAD * LEAD) / rho[x]
            buoy[x, pl.ds(0, ny), :] = value
            buoy[x, pl.ds(ny, 1), :] = value[ny - 1 :]
            return carry

        lax.fori_loop(0, nx, prepare, 0, unroll=4)

        def between(x, carry):
            here = buoy[x, pl.ds(0, ny), :]
            hx[x] = here + buoy[jnp.minimum(x + 1, nx - 1), pl.ds(0, ny), :]
            hy[x] = (here + buoy[x, pl.ds(1, ny), :]) * (1.0 / (BAND * BAND))
            shifted = jnp.where(lane == nz - 1, here, pltpu.roll(here, nz - 1, 1))
            hz[x] = (here + shifted) * (1.0 / (BAND * BAND))
            return carry

        lax.fori_loop(0, nx, between, 0, unroll=8)
        if member == 0:
            for load in loads[4:]:
                load.wait()

        count = cells_ref.shape[-1]
        upright = lambda row: jnp.broadcast_to(row, (nz, count)).T
        cells = lanes_ref[0, 0, pl.ds(member, 1), :]
        pick_z[...] = (upright((cells & (nz - 1)).astype(jnp.float32)) == iota((count, nz), 1).astype(jnp.float32)).astype(jnp.float32)
        for step in range(2):
            upright_obs[step] = upright(obs_ref[0, 0, member, pl.ds(1 - step, 1), :])
        line_of = lax.shift_right_logical(cells, LANE_BITS)

        def both(g, carry):
            part = pl.ds(pl.multiple_of(g * rows, rows), rows)
            picks[part, :] = narrow(iota((rows, count), 0) + g * rows == line_of)
            first, other = planes(now_ref, g, member), planes(adj_ref, g, member)
            wide, wide_other = first.astype(jnp.float32), other.astype(jnp.float32)
            put(wide_p, g, wide)
            put(wide_q, g, wide_other)
            put(lead_p, g, 2.0 * wide - planes(old_ref, g, member).astype(jnp.float32))
            put(lead_q, g, 2.0 * wide_other - planes(next_ref, g, member).astype(jnp.float32))
            one, two = lines(first, other, cut(g), cut(g), True)
            put(sum_p, g, one)
            put(sum_q, g, two)
            return carry

        lax.fori_loop(0, nx // GROUP, both, 0, unroll=True)

        def keep_p(x, ty, here, value, total):
            image_one[x, here, :] = total

        def keep_q(x, ty, here, value, total):
            adj_one[x, here, :] = total

        columns((
            (lambda x, here: wide_p[x, here, :], sum_p, keep_p),
            (lambda x, here: wide_q[x, here, :], sum_q, keep_q),
        ))

    def second_half(member):
        unpack(member, models[2 * member + 1], vel)
        coupling, weight = vel, rho

        def advance(x, carry):
            velocity, density = vel[x], rho[x]
            scale = (COURANT * velocity) * (COURANT * velocity) * density
            coupling[x] = scale
            weight[x] = velocity * density
            second[x] = lead_p[x] + scale * image_one[x] + source_term(member, 0, x * (ny * nz), (ny, nz))
            adj_one[x] = lead_q[x] + scale * adj_one[x]
            return carry

        lax.fori_loop(0, nx, advance, 0, unroll=4)
        single(second)

        def finish_two(x, ty, here, value, total):
            image_two[x, here, :] = total
            third[x, here, :] = 2.0 * value - wide_p[x, here, :] + coupling[x, here, :] * total + source_term(member, 1, (x * ny + ty * 8) * nz, (8, nz))

        columns(((lambda x, here: second[x, here, :], sum_p, finish_two),))
        count = cells_ref.shape[-1]

        def receive(step, carry):
            for sub in range(16):
                n = step * 16 + sub
                line = lax.shift_right_logical(cells_ref[0, 0, member, n], LANE_BITS)
                spot = pl.ds(lax.bitwise_and(line, ny - 1), 1)
                x = lax.shift_right_logical(line, ny.bit_length() - 1)
                misfit[0, pl.ds(n, 1), :] = third[x, spot, :]
                misfit[1, pl.ds(n, 1), :] = second[x, spot, :]
            return carry

        lax.fori_loop(0, count // 16, receive, 0)
        amounts = [
            jnp.where(pick_z[...] > 0.5, misfit[step] - upright_obs[step], 0.0) for step in range(2)
        ]
        amounts = jnp.concatenate(halves(jnp.concatenate(amounts, axis=1)), axis=0)

        def deliver(g, carry):
            pick = picks[pl.ds(pl.multiple_of(g * rows, rows), rows), :]
            added = dot(jnp.concatenate([pick, pick], axis=1), amounts)
            put(adj_one, g, planes(adj_one, g) + added[:, :nz])
            put(mixed, g, added[:, nz:] - planes(wide_q, g))
            return carry

        lax.fori_loop(0, nx // GROUP, deliver, 0, unroll=True)
        single(adj_one)

        def finish_four(x, ty, here, value, total):
            q0 = 2.0 * value + mixed[x, here, :] + coupling[x, here, :] * total
            result = weight[x, here, :] * (value * image_two[x, here, :] + q0 * image_one[x, here, :])
            size = jnp.abs(result)
            root = result * lax.rsqrt(jnp.maximum(size, SMALL))
            for half in range(2):
                spot = (x // 4) * grid_y + ty * 2 + half
                tiles[spot, (x % 4) // 2, pl.ds((x % 2) * 4, 4), :] = root[4 * half : 4 * half + 4]
            return size

        peak = columns(((lambda x, here: adj_one[x, here, :], sum_p, finish_four),))
        top = jnp.maximum(jnp.max(peak, axis=(0, 1), keepdims=True), SMALL)
        factor = jnp.broadcast_to(CODES * lax.rsqrt(top), (8, nz))
        scale = jnp.broadcast_to(top * (2.0 * COURANT * COURANT / (CODES * CODES)), (1, nz))
        scale_out[member] = scale
        scale_in[member, whole_me] = scale

        def pack(owner, carry):
            for core in range(cores):
                parts = []
                for j in range(0, cap):
                    parts.append(jnp.round(tiles[spot_at(member, owner, j), core] * factor))
                if cap % 2:
                    parts.append(jnp.zeros((8, nz), jnp.float32))
                for j in range(0, len(parts), 2):
                    code = jnp.concatenate(parts[j : j + 2], axis=0).astype(jnp.int32).astype(jnp.int16)
                    outgoing[member][owner * cores + core, pl.ds(8 * j, 16), :] = code
            return carry

        lax.fori_loop(0, owners, pack, 0)

    keeps = [
        pltpu.make_async_copy(outgoing[member].at[whole_me], arrived[member].at[whole_me], keep_sems.at[member])
        for member in range(members)
    ]

    def dispatch(member):
        each(peers, lambda d: scale_copy(member, d).start())
        each(peers, lambda d: grad_copy(member, d).start())
        keeps[member].start()

    def add_up(member):
        per = cap * 8

        def decode(source):
            code = arrived[member][source].astype(jnp.int32).astype(jnp.float32)[:per]
            decoded[pl.ds(pl.multiple_of(source * per, per), per), :] = code * jnp.abs(code) * scale_in[member, source]

        keeps[member].wait()
        decode(whole_me)

        def accept(d):
            scale_copy(member, d).wait()
            grad_copy(member, d).wait()
            decode((whole_me + peers - d) % peers)

        each(peers, accept)
        pick = (lax.broadcasted_iota(jnp.int32, (held, total), 0) == homes_ref[pl.ds(member, 1), :]).astype(jnp.float32).astype(jnp.bfloat16)
        pick = jnp.concatenate([pick, pick], axis=1)
        for i in range(0, 8, 2):
            value = jnp.concatenate([decoded[pl.ds(i + k, total, stride=8), :] for k in range(2)], axis=1)
            part = dot(pick, jnp.concatenate(halves(value), axis=0))
            for k in range(2):
                mine, half = pl.ds(i + k, held, stride=8), part[:, k * nz : (k + 1) * nz]
                out_ref[mine, :] = half if member == 0 else out_ref[mine, :] + half

    lists_copy.wait()
    for member in range(members):
        first_half(member)
        if member == members - 1:
            for done in range(members - 1):
                dispatch(done)
        each(owners, lambda d: model_copy(2 * member + 1, d).wait())
        second_half(member)
    dispatch(members - 1)
    for member in range(members):
        add_up(member)


def per_device(
    velocity, density, tile_home, footprints, source_cell, source_wave, receivers, observed,
    pressure_old, pressure_now, adjoint_next, adjoint_now,
):
    owners = lax.axis_size("own")
    cores = lax.axis_size("shot")
    held = velocity.shape[0]
    members, foot = footprints.shape[2:]
    cap = foot // owners
    nx, ny, nz = pressure_now.shape[-3:]
    home = tile_home.reshape(-1, nz)
    hbm = pl.BlockSpec(memory_space=pltpu.HBM)
    field = pltpu.VMEM((nx, ny, nz), jnp.float32)
    stored = pltpu.VMEM((members, nx, ny, nz), jnp.bfloat16)
    table = pltpu.VMEM((held, 16, nz), jnp.bfloat16)
    model = pltpu.VMEM((owners, cap, 16, nz), jnp.bfloat16)
    peers = owners * cores
    grads = pltpu.VMEM((peers, (cap * 8 + 15) // 16 * 16, nz), jnp.int16)
    zband, yband = depth_bands(nz), line_bands(ny)
    count = receivers.shape[-1]
    lists = members * (8 + owners)
    dma = pltpu.SemaphoreType.DMA
    gradient = pl.pallas_call(
        shots_kernel,
        out_shape=jax.ShapeDtypeStruct((held * 8, nz), jnp.float32),
        in_specs=[hbm] * 14,
        out_specs=pl.BlockSpec(memory_space=pltpu.VMEM),
        scratch_shapes=[pltpu.VMEM((foot, 16, nz), jnp.bfloat16)] * (2 * members) + [model] * (2 * members) + [grads] * (2 * members) + [
            table, table, pltpu.VMEM(zband.shape, jnp.bfloat16), pltpu.VMEM(yband.shape, jnp.bfloat16),
            stored, stored, stored, stored,
            field, field, pltpu.VMEM((nx, ny + 8, nz), jnp.float32)] + [field] * 13 + [
            pltpu.VMEM((foot, 2, 8, nz), jnp.float32), pltpu.VMEM((2, count, nz), jnp.float32),
            pltpu.VMEM((peers * cap * 8, nz), jnp.float32), pltpu.VMEM((members, 1, nz), jnp.float32), pltpu.VMEM((members, peers, 1, nz), jnp.float32),
            pltpu.VMEM((members, peers * cap), jnp.int32),
            pltpu.VMEM((8 + lists, nz), jnp.int32), pltpu.SMEM((8, nz), jnp.int32), pltpu.SMEM((lists, nz), jnp.int32), dma((2,)),
            pltpu.VMEM(home.shape, jnp.int32), pltpu.SMEM(footprints.shape, jnp.int32), pltpu.SMEM(source_cell.shape, jnp.int32),
            pltpu.SMEM(receivers.shape, jnp.int32), pltpu.SMEM(source_wave.shape, jnp.float32),
            pltpu.VMEM(observed.shape, jnp.float32), pltpu.VMEM(receivers.shape, jnp.int32),
            pltpu.VMEM((nx * ny, count), jnp.bfloat16), pltpu.VMEM((2, count, nz), jnp.float32), pltpu.VMEM((count, nz), jnp.float32), field, field,
            dma((15,)), dma((members,)), dma((2 * members, owners)), dma((2 * members, owners)),
            dma((members, peers)), dma((members, peers)), dma((members, peers)), dma((members, peers)),
        ],
        compiler_params=pltpu.CompilerParams(collective_id=0, has_side_effects=True, vmem_limit_bytes=40 * 1024 * 1024),
        cost_estimate=pl.CostEstimate(flops=200_000_000, bytes_accessed=6_000_000, transcendentals=0),
    )(*(pltpu.with_memory_space_constraint(operand, pltpu.HBM) for operand in (
        home, footprints, source_cell, receivers, source_wave, observed,
        velocity.reshape(held, 16, nz), density.reshape(held, 16, nz), zband, yband,
        pressure_old, pressure_now, adjoint_next, adjoint_now,
    )))
    return gradient.reshape(held, 4 // cores, 4, nz)


def solution(mesh):
    whole = P(("grp", "own"), None, None, None)
    fields = P(("grp", "own"), "shot", None, None, None, None)
    in_specs = (
        whole, whole, P("grp"), P("grp", None, None, None),
        P(("grp", "own"), "shot", None),
        P(("grp", "own"), "shot", None, None),
        P(("grp", "own"), "shot", None, None),
        P(("grp", "own"), "shot", None, None, None),
        fields, fields, fields, fields,
    )
    return jax.shard_map(
        per_device, mesh=mesh, in_specs=in_specs,
        out_specs=P(("grp", "own"), "shot", None, None), check_vma=False,
    )
```

```python
import functools

import jax
import jax.numpy as jnp
import numpy as np
from jax import lax
from jax.experimental import pallas as pl
from jax.experimental.pallas import tpu as pltpu
from jax.sharding import PartitionSpec as P

COURANT = 0.09
LEAD = 1225.0 / 1024.0
RATIOS = (1.0, -1.0 / 15.0, 1.0 / 125.0, -1.0 / 1715.0)
BAND = 105.0
GROUP = 8
LANE_BITS = 7
CODES = 32760.0
SMALL = 1e-30
MESH = pl.DeviceIdType.MESH


def difference_matrices(length):
    grad = np.zeros((length, length), np.float32)
    div = np.zeros((length, length), np.float32)
    for i in range(length):
        for m, ratio in enumerate(RATIOS, start=1):
            if i + m < length:
                grad[i, i + m] += BAND * ratio
            if i + 1 - m >= 0:
                grad[i, i + 1 - m] -= BAND * ratio
            if i + m - 1 < length:
                div[i, i + m - 1] += BAND * ratio
            if i - m >= 0:
                div[i, i - m] -= BAND * ratio
    return grad, div


def depth_bands(depth):
    grad, div = difference_matrices(depth)
    return jnp.asarray(np.stack([np.concatenate([a.T, a.T], axis=0) for a in (grad, div)]), jnp.bfloat16)


def line_bands(length):
    return jnp.asarray(np.stack([np.kron(np.eye(GROUP, dtype=np.float32), a) for a in difference_matrices(length)]), jnp.bfloat16)


def taps(at, low):
    total = None
    for m, ratio in enumerate(RATIOS, start=1):
        up, down = (at(m), at(1 - m)) if low else (at(m - 1), at(-m))
        if up is None and down is None:
            continue
        diff = up - down if up is not None and down is not None else (up if down is None else -down)
        term = diff if m == 1 else ratio * diff
        total = term if total is None else total + term
    return total


def halves(value):
    high = value.astype(jnp.bfloat16)
    return high, (value - high.astype(jnp.float32)).astype(jnp.bfloat16)


def dot(a, b):
    return jnp.dot(a, b, preferred_element_type=jnp.float32)


def shots_kernel(
    home_hbm, foot_hbm, source_hbm, cells_hbm, wave_hbm, obs_hbm,
    vel_hbm, rho_hbm, zband_hbm, yband_hbm, old_hbm, now_hbm, next_hbm, adj_hbm,
    out_ref, *rest,
):
    members, foot = foot_hbm.shape[2:]
    models, rest = rest[: 2 * members], rest[2 * members :]
    leaving, rest = rest[: 2 * members], rest[2 * members :]
    outgoing, rest = rest[:members], rest[members:]
    arrived, rest = rest[:members], rest[members:]
    (
        vel_tab, rho_tab, zband, yband, old_ref, now_ref, next_ref, adj_ref,
        rho, vel, buoy, hx, hy, hz, sum_p, sum_q, image_one, adj_one, second, third, image_two, mixed, wide_p, wide_q, tiles,
        misfit, decoded, scale_out, scale_in, homes_ref, book, rows_ref, lists_ref, table_sems,
        home_ref, foot_ref, source_ref, cells_ref, wave_ref, obs_ref, lanes_ref, picks, upright_obs, pick_z, lead_p, lead_q,
        load_sems, keep_sems, model_send, model_recv, grad_send, grad_recv, scale_send, scale_recv,
    ) = rest
    owners, cap = leaving[0].shape[:2]
    cores = lax.axis_size("shot")
    nx, ny, nz = now_ref.shape[1:]
    grid_y = ny // 4
    tiles_y = ny // 8
    rows = GROUP * ny
    me = lax.axis_index("own")
    whole_me = me * cores + lax.axis_index("shot")
    peers = owners * cores
    lane = lax.broadcasted_iota(jnp.int32, (1, nz), 1)

    loads = [
        pltpu.make_async_copy(src, dst, load_sems.at[i])
        for i, (src, dst) in enumerate((
            (home_hbm, home_ref), (foot_hbm, foot_ref), (rho_hbm, rho_tab), (vel_hbm, vel_tab), (zband_hbm, zband), (yband_hbm, yband),
            (now_hbm.at[0, 0], now_ref), (adj_hbm.at[0, 0], adj_ref), (old_hbm.at[0, 0], old_ref), (next_hbm.at[0, 0], next_ref),
            (cells_hbm, lanes_ref), (obs_hbm, obs_ref), (cells_hbm, cells_ref), (source_hbm, source_ref), (wave_hbm, wave_ref),
        ))
    ]
    for load in loads:
        load.start()
    barrier = pltpu.get_barrier_semaphore()

    def device(peer):
        return {"own": peer // cores, "shot": peer % cores}

    def greet(d, carry):
        pl.semaphore_signal(barrier, inc=1, device_id=device((whole_me + d) % peers), device_id_type=MESH)
        return carry

    lax.fori_loop(1, peers, greet, 0)

    def model_copy(phase, d):
        peer = (me + d) % owners
        return pltpu.make_async_remote_copy(
            src_ref=leaving[phase].at[peer], dst_ref=models[phase].at[pl.ds(me * cap, cap)],
            send_sem=model_send.at[phase, d], recv_sem=model_recv.at[phase, d],
            device_id={"own": peer}, device_id_type=MESH,
        )

    def grad_copy(member, d):
        peer = (whole_me + d) % peers
        return pltpu.make_async_remote_copy(
            src_ref=outgoing[member].at[peer], dst_ref=arrived[member].at[whole_me],
            send_sem=grad_send.at[member, d], recv_sem=grad_recv.at[member, d],
            device_id=device(peer), device_id_type=MESH,
        )

    def scale_copy(member, d):
        peer = (whole_me + d) % peers
        return pltpu.make_async_remote_copy(
            src_ref=scale_out.at[member], dst_ref=scale_in.at[member, whole_me],
            send_sem=scale_send.at[member, d], recv_sem=scale_recv.at[member, d],
            device_id=device(peer), device_id_type=MESH,
        )

    def each(count, act):
        def body(d, carry):
            act(d)
            return carry

        lax.fori_loop(1, count, body, 0)

    held = vel_tab.shape[0]
    count_tiles = home_ref.shape[0] * nz
    side = int(round(count_tiles ** 0.5))
    edge = int(round(foot ** 0.5))
    bits = lambda size: size.bit_length() - 1
    iota = lambda shape, axis: lax.broadcasted_iota(jnp.int32, shape, axis)
    narrow = lambda value: value.astype(jnp.float32).astype(jnp.bfloat16)
    across = lambda a, b: lax.dot_general(a, b, (((1,), (1,)), ((), ())), preferred_element_type=jnp.float32)
    blocks = home_ref.shape[0]

    def locate():
        home = home_ref[...]
        high, low = lax.shift_right_logical(home, LANE_BITS), home & (nz - 1)
        hit, full, own = [], [], []
        mine = lax.shift_right_logical(me * held, LANE_BITS)
        for i in range(blocks):
            tile = i * nz + iota((1, nz), 1)
            where = lax.shift_right_logical(tile, bits(side)), tile & (side - 1)
            hit.append(narrow(low[i : i + 1] == iota((nz, nz), 0)))
            high_row = high[i : i + 1]
            full.append(narrow(jnp.concatenate([jnp.where(high_row == iota((blocks, nz), 0), w, 0) for w in where], axis=0)))
            own.append(narrow(jnp.concatenate([jnp.broadcast_to(jnp.where(high_row == mine, w, 0), (nz, nz)) for w in where], axis=0)))
        hit, full, own = (jnp.concatenate(parts, axis=1) for parts in (hit, full, own))
        return across(full, hit).astype(jnp.int32), across(hit, own).astype(jnp.int32)

    def inside(dx, dy):
        return (dx >= 0) & (dx < edge) & (dy >= 0) & (dy < edge)

    def first_of(owner, core, member):
        first = foot_ref[owner, core, member, 0]
        return lax.shift_right_logical(first, bits(side)), first & (side - 1)

    total = peers * cap
    share = bits(held)
    spot_x, spot_y = iota((nz, nz), 0), iota((nz, nz), 1)
    same = lax.shift_right_logical(spot_x, share) == lax.shift_right_logical(spot_y, share)
    for load in loads[:2]:
        load.wait()
    positions, own_positions = locate()
    book[...] = jnp.zeros_like(book)
    in_share = lax.shift_right_logical(iota((nz, total), 0), share) == me % (nz >> share)
    before = narrow(same & (spot_y < spot_x))
    for member in range(members):
        first = jnp.zeros((1, total), jnp.int32)
        shot_of = lax.shift_right_logical(iota((1, total), 1), bits(cap))
        for peer in range(peers):
            first = jnp.where(shot_of == peer, foot_ref[peer // cores, peer % cores, member, 0], first)
        dx = own_positions[:, :nz] - lax.shift_right_logical(first, bits(side))
        dy = own_positions[:, nz:] - (first & (side - 1))
        chosen = inside(dx, dy) & in_share
        order = dot(before, narrow(chosen)).astype(jnp.int32)
        chosen = chosen & (order == (iota((1, total), 1) & (cap - 1)))
        local = jnp.where(chosen, iota((nz, total), 0) & (held - 1), 0)
        homes = jnp.clip(jnp.sum(local, axis=0, keepdims=True), 0, held - 1)
        homes_ref[pl.ds(member, 1), :] = homes
        book[pl.ds(member, 1), :] = homes
    rows_copy = pltpu.make_async_copy(book.at[pl.ds(0, 8)], rows_ref, table_sems.at[0])
    lists_copy = pltpu.make_async_copy(book.at[pl.ds(8, book.shape[0] - 8)], lists_ref, table_sems.at[1])
    rows_copy.start()

    def list_tiles():
        after = narrow(same & (spot_x < spot_y))
        keys, values = [], []
        cell = iota((blocks, nz), 0) * nz + iota((blocks, nz), 1)
        owner = lax.shift_right_logical(cell, share)
        for member in range(members):
            at_x, at_y = first_of(me, lax.axis_index("shot"), member)
            dx, dy = positions[:blocks] - at_x, positions[blocks:] - at_y
            chosen = inside(dx, dy)
            order = dot(narrow(chosen), after).astype(jnp.int32)
            slot = owner * cap + order
            key, value = [], []
            for i in range(blocks):
                row = lambda field: field[i : i + 1]
                valid = row(chosen.astype(jnp.int32)) == 1
                small = iota((8, nz), 0)
                key.append(narrow(jnp.concatenate([
                    jnp.where(valid & (row(dx) == small), 1, 0),
                    jnp.where(valid & (row(owner) == iota((owners, nz), 0)), 1, 0),
                ], axis=0)))
                value.append(narrow(jnp.concatenate([
                    jnp.where(row(dy) == small, row(slot), 0),
                    jnp.where(row(order) == small, row(dx) * edge + row(dy), 0),
                ], axis=0)))
            keys.append(jnp.concatenate(key, axis=1))
            values.append(jnp.concatenate(value, axis=1))
        values.append(jnp.zeros((nz - 16 * members, blocks * nz), jnp.bfloat16))
        found = across(jnp.concatenate(keys, axis=0), jnp.concatenate(values, axis=0)).astype(jnp.int32)
        book[pl.ds(8, found.shape[0]), :] = jnp.clip(found, 0, foot - 1)
        lists_copy.start()

    def slot_at(member, kx, ky):
        return lists_ref[member * (8 + owners) + kx, member * 16 + ky]

    def spot_at(member, owner, j):
        return lists_ref[member * (8 + owners) + 8 + owner, member * 16 + 8 + j]

    def collect(table, member, peer, out):
        for j in range(cap):
            tile = table[rows_ref[member, (peer * cores + lax.axis_index("shot")) * cap + j]]
            if len(out.shape) == 4:
                out[peer, j] = tile
            else:
                out[peer * cap + j] = tile

    pl.semaphore_wait(barrier, peers - 1)
    rows_copy.wait()
    loads[2].wait()
    for phase in range(2 * members):
        member, table = phase // 2, (rho_tab, vel_tab)[phase % 2]
        if phase == 1:
            loads[3].wait()

        def send(d):
            collect(table, member, (me + d) % owners, leaving[phase])
            model_copy(phase, d).start()

        each(owners, send)
        if phase == 0:
            list_tiles()
        collect(table, member, me, models[phase])

    def unpack(member, arrival, field):
        def body(kx, carry):
            for ky in range(grid_y):
                slot = slot_at(member, kx, ky)
                tile = arrival[slot].astype(jnp.float32)
                for i in range(4):
                    field[kx * 4 + i, pl.ds(ky * 4, 4), :] = tile[4 * i : 4 * i + 4]
            return carry

        lax.fori_loop(0, nx // 4, body, 0, unroll=2)

    def divergence(value, half, transposed):
        high, low = halves(half * value)
        if transposed:
            return dot(jnp.concatenate([yband[1], yband[1]], axis=1), jnp.concatenate([high, low], axis=0))
        return dot(jnp.concatenate([high, low], axis=1), zband[1])

    def planes(ref, g, *lead):
        return ref[(*lead, pl.ds(pl.multiple_of(g * GROUP, GROUP), GROUP))].reshape(rows, nz)

    def lines(first, second_block, first_half, second_half, exact):
        pair = lambda a, b: jnp.concatenate([a, b], axis=1)
        stack = lambda a, b: jnp.concatenate([a, b], axis=0)
        if exact:
            grad_z = dot(stack(first, second_block), zband[0, :nz])
            grad_y = dot(yband[0], pair(first, second_block))
        else:
            (high_a, low_a), (high_b, low_b) = halves(first), halves(second_block)
            grad_z = dot(stack(pair(high_a, low_a), pair(high_b, low_b)), zband[0])
            grad_y = dot(pair(yband[0], yband[0]), stack(pair(high_a, high_b), pair(low_a, low_b)))
        (hy_a, hz_a), (hy_b, hz_b) = first_half, second_half
        div_z = divergence(grad_z, stack(hz_a, hz_b), False)
        div_y = divergence(grad_y, pair(hy_a, hy_b), True)
        return div_z[:rows] + div_y[:, :nz], div_z[rows:] + div_y[:, nz:]

    def cut(g):
        return planes(hy, g), planes(hz, g)

    def put(ref, g, block):
        ref[pl.ds(pl.multiple_of(g * GROUP, GROUP), GROUP)] = block.reshape(GROUP, ny, nz)

    def columns(jobs):
        def body(ty, peak):
            start = pl.multiple_of(ty * 8, 8)
            here = pl.ds(start, 8)
            for load, rest_sum, finish in jobs:
                values, fluxes = {}, {}

                def value_at(x):
                    if x < 0 or x >= nx:
                        return None
                    if x not in values:
                        values[x] = load(x, here)
                    return values[x]

                def flux_at(x):
                    if x < 0 or x >= nx:
                        return None
                    if x not in fluxes:
                        fluxes[x] = hx[x, here, :] * taps(lambda shift: value_at(x + shift), True)
                    return fluxes[x]

                for x in range(nx):
                    total = rest_sum[x, here, :] + taps(lambda shift: flux_at(x + shift), False)
                    size = finish(x, ty, here, value_at(x), total)
                    if size is not None:
                        peak = jnp.maximum(peak, size)
            return peak

        return lax.fori_loop(0, tiles_y, body, jnp.zeros((8, nz), jnp.float32))

    def single(field):
        def body(pair_index, carry):
            g = pair_index * 2
            one, two = lines(planes(field, g), planes(field, g + 1), cut(g), cut(g + 1), False)
            put(sum_p, g, one)
            put(sum_p, g + 1, two)
            return carry

        lax.fori_loop(0, nx // GROUP // 2, body, 0, unroll=True)

    def source_term(member, step, base, shape):
        local = lax.broadcasted_iota(jnp.int32, shape, 0) * nz + lax.broadcasted_iota(jnp.int32, shape, 1)
        return jnp.where(local == source_ref[0, 0, member] - base, wave_ref[0, 0, member, step], 0.0)

    def first_half(member):
        each(owners, lambda d: model_copy(2 * member, d).wait())
        unpack(member, models[2 * member], rho)

        def prepare(x, carry):
            value = (0.5 * LEAD * LEAD) / rho[x]
            buoy[x, pl.ds(0, ny), :] = value
            buoy[x, pl.ds(ny, 1), :] = value[ny - 1 :]
            return carry

        lax.fori_loop(0, nx, prepare, 0, unroll=4)

        def between(x, carry):
            here = buoy[x, pl.ds(0, ny), :]
            hx[x] = here + buoy[jnp.minimum(x + 1, nx - 1), pl.ds(0, ny), :]
            hy[x] = (here + buoy[x, pl.ds(1, ny), :]) * (1.0 / (BAND * BAND))
            shifted = jnp.where(lane == nz - 1, here, pltpu.roll(here, nz - 1, 1))
            hz[x] = (here + shifted) * (1.0 / (BAND * BAND))
            return carry

        lax.fori_loop(0, nx, between, 0, unroll=8)
        if member == 0:
            for load in loads[4:]:
                load.wait()

        count = cells_ref.shape[-1]
        upright = lambda row: jnp.broadcast_to(row, (nz, count)).T
        cells = lanes_ref[0, 0, pl.ds(member, 1), :]
        pick_z[...] = (upright((cells & (nz - 1)).astype(jnp.float32)) == iota((count, nz), 1).astype(jnp.float32)).astype(jnp.float32)
        for step in range(2):
            upright_obs[step] = upright(obs_ref[0, 0, member, pl.ds(1 - step, 1), :])
        line_of = lax.shift_right_logical(cells, LANE_BITS)

        def both(g, carry):
            part = pl.ds(pl.multiple_of(g * rows, rows), rows)
            picks[part, :] = narrow(iota((rows, count), 0) + g * rows == line_of)
            first, other = planes(now_ref, g, member), planes(adj_ref, g, member)
            wide, wide_other = first.astype(jnp.float32), other.astype(jnp.float32)
            put(wide_p, g, wide)
            put(wide_q, g, wide_other)
            put(lead_p, g, 2.0 * wide - planes(old_ref, g, member).astype(jnp.float32))
            put(lead_q, g, 2.0 * wide_other - planes(next_ref, g, member).astype(jnp.float32))
            one, two = lines(first, other, cut(g), cut(g), True)
            put(sum_p, g, one)
            put(sum_q, g, two)
            return carry

        lax.fori_loop(0, nx // GROUP, both, 0, unroll=True)

        def keep_p(x, ty, here, value, total):
            image_one[x, here, :] = total

        def keep_q(x, ty, here, value, total):
            adj_one[x, here, :] = total

        columns((
            (lambda x, here: wide_p[x, here, :], sum_p, keep_p),
            (lambda x, here: wide_q[x, here, :], sum_q, keep_q),
        ))

    def second_half(member):
        unpack(member, models[2 * member + 1], vel)
        coupling, weight = vel, rho

        def advance(x, carry):
            velocity, density = vel[x], rho[x]
            scale = (COURANT * velocity) * (COURANT * velocity) * density
            coupling[x] = scale
            weight[x] = velocity * density
            second[x] = lead_p[x] + scale * image_one[x] + source_term(member, 0, x * (ny * nz), (ny, nz))
            adj_one[x] = lead_q[x] + scale * adj_one[x]
            return carry

        lax.fori_loop(0, nx, advance, 0, unroll=4)
        single(second)

        def finish_two(x, ty, here, value, total):
            image_two[x, here, :] = total
            third[x, here, :] = 2.0 * value - wide_p[x, here, :] + coupling[x, here, :] * total + source_term(member, 1, (x * ny + ty * 8) * nz, (8, nz))

        columns(((lambda x, here: second[x, here, :], sum_p, finish_two),))
        count = cells_ref.shape[-1]

        def receive(step, carry):
            for sub in range(16):
                n = step * 16 + sub
                line = lax.shift_right_logical(cells_ref[0, 0, member, n], LANE_BITS)
                spot = pl.ds(lax.bitwise_and(line, ny - 1), 1)
                x = lax.shift_right_logical(line, ny.bit_length() - 1)
                misfit[0, pl.ds(n, 1), :] = third[x, spot, :]
                misfit[1, pl.ds(n, 1), :] = second[x, spot, :]
            return carry

        lax.fori_loop(0, count // 16, receive, 0)
        amounts = [
            jnp.where(pick_z[...] > 0.5, misfit[step] - upright_obs[step], 0.0) for step in range(2)
        ]
        amounts = jnp.concatenate(halves(jnp.concatenate(amounts, axis=1)), axis=0)

        def deliver(g, carry):
            pick = picks[pl.ds(pl.multiple_of(g * rows, rows), rows), :]
            added = dot(jnp.concatenate([pick, pick], axis=1), amounts)
            put(adj_one, g, planes(adj_one, g) + added[:, :nz])
            put(mixed, g, added[:, nz:] - planes(wide_q, g))
            return carry

        lax.fori_loop(0, nx // GROUP, deliver, 0, unroll=True)
        single(adj_one)

        def finish_four(x, ty, here, value, total):
            q0 = 2.0 * value + mixed[x, here, :] + coupling[x, here, :] * total
            result = weight[x, here, :] * (value * image_two[x, here, :] + q0 * image_one[x, here, :])
            size = jnp.abs(result)
            root = result * lax.rsqrt(jnp.maximum(size, SMALL))
            for half in range(2):
                spot = (x // 4) * grid_y + ty * 2 + half
                tiles[spot, (x % 4) // 2, pl.ds((x % 2) * 4, 4), :] = root[4 * half : 4 * half + 4]
            return size

        peak = columns(((lambda x, here: adj_one[x, here, :], sum_p, finish_four),))
        top = jnp.maximum(jnp.max(peak, axis=(0, 1), keepdims=True), SMALL)
        factor = jnp.broadcast_to(CODES * lax.rsqrt(top), (8, nz))
        scale = jnp.broadcast_to(top * (2.0 * COURANT * COURANT / (CODES * CODES)), (1, nz))
        scale_out[member] = scale
        scale_in[member, whole_me] = scale

        def pack(owner, carry):
            for core in range(cores):
                parts = []
                for j in range(0, cap):
                    parts.append(jnp.round(tiles[spot_at(member, owner, j), core] * factor))
                if cap % 2:
                    parts.append(jnp.zeros((8, nz), jnp.float32))
                for j in range(0, len(parts), 2):
                    code = jnp.concatenate(parts[j : j + 2], axis=0).astype(jnp.int32).astype(jnp.int16)
                    outgoing[member][owner * cores + core, pl.ds(8 * j, 16), :] = code
            return carry

        lax.fori_loop(0, owners, pack, 0)

    keeps = [
        pltpu.make_async_copy(outgoing[member].at[whole_me], arrived[member].at[whole_me], keep_sems.at[member])
        for member in range(members)
    ]

    def dispatch(member):
        each(peers, lambda d: scale_copy(member, d).start())
        each(peers, lambda d: grad_copy(member, d).start())
        keeps[member].start()

    def add_up(member):
        per = cap * 8

        def decode(source):
            code = arrived[member][source].astype(jnp.int32).astype(jnp.float32)[:per]
            decoded[pl.ds(pl.multiple_of(source * per, per), per), :] = code * jnp.abs(code) * scale_in[member, source]

        keeps[member].wait()
        decode(whole_me)

        def accept(d):
            scale_copy(member, d).wait()
            grad_copy(member, d).wait()
            decode((whole_me + peers - d) % peers)

        each(peers, accept)
        pick = (lax.broadcasted_iota(jnp.int32, (held, total), 0) == homes_ref[pl.ds(member, 1), :]).astype(jnp.float32).astype(jnp.bfloat16)
        pick = jnp.concatenate([pick, pick], axis=1)
        for i in range(8):
            part = dot(pick, jnp.concatenate(halves(decoded[pl.ds(i, total, stride=8), :]), axis=0))
            mine = pl.ds(i, held, stride=8)
            out_ref[mine, :] = part if member == 0 else out_ref[mine, :] + part

    lists_copy.wait()
    for member in range(members):
        first_half(member)
        if member == members - 1:
            for done in range(members - 1):
                dispatch(done)
        each(owners, lambda d: model_copy(2 * member + 1, d).wait())
        second_half(member)
    dispatch(members - 1)
    for member in range(members):
        add_up(member)


def per_device(
    velocity, density, tile_home, footprints, source_cell, source_wave, receivers, observed,
    pressure_old, pressure_now, adjoint_next, adjoint_now,
):
    owners = lax.axis_size("own")
    cores = lax.axis_size("shot")
    held = velocity.shape[0]
    members, foot = footprints.shape[2:]
    cap = foot // owners
    nx, ny, nz = pressure_now.shape[-3:]
    home = tile_home.reshape(-1, nz)
    hbm = pl.BlockSpec(memory_space=pltpu.HBM)
    field = pltpu.VMEM((nx, ny, nz), jnp.float32)
    stored = pltpu.VMEM((members, nx, ny, nz), jnp.bfloat16)
    table = pltpu.VMEM((held, 16, nz), jnp.bfloat16)
    model = pltpu.VMEM((owners, cap, 16, nz), jnp.bfloat16)
    peers = owners * cores
    grads = pltpu.VMEM((peers, (cap * 8 + 15) // 16 * 16, nz), jnp.int16)
    zband, yband = depth_bands(nz), line_bands(ny)
    count = receivers.shape[-1]
    lists = members * (8 + owners)
    dma = pltpu.SemaphoreType.DMA
    gradient = pl.pallas_call(
        shots_kernel,
        out_shape=jax.ShapeDtypeStruct((held * 8, nz), jnp.float32),
        in_specs=[hbm] * 14,
        out_specs=pl.BlockSpec(memory_space=pltpu.VMEM),
        scratch_shapes=[pltpu.VMEM((foot, 16, nz), jnp.bfloat16)] * (2 * members) + [model] * (2 * members) + [grads] * (2 * members) + [
            table, table, pltpu.VMEM(zband.shape, jnp.bfloat16), pltpu.VMEM(yband.shape, jnp.bfloat16),
            stored, stored, stored, stored,
            field, field, pltpu.VMEM((nx, ny + 8, nz), jnp.float32)] + [field] * 13 + [
            pltpu.VMEM((foot, 2, 8, nz), jnp.float32), pltpu.VMEM((2, count, nz), jnp.float32),
            pltpu.VMEM((peers * cap * 8, nz), jnp.float32), pltpu.VMEM((members, 1, nz), jnp.float32), pltpu.VMEM((members, peers, 1, nz), jnp.float32),
            pltpu.VMEM((members, peers * cap), jnp.int32),
            pltpu.VMEM((8 + lists, nz), jnp.int32), pltpu.SMEM((8, nz), jnp.int32), pltpu.SMEM((lists, nz), jnp.int32), dma((2,)),
            pltpu.VMEM(home.shape, jnp.int32), pltpu.SMEM(footprints.shape, jnp.int32), pltpu.SMEM(source_cell.shape, jnp.int32),
            pltpu.SMEM(receivers.shape, jnp.int32), pltpu.SMEM(source_wave.shape, jnp.float32),
            pltpu.VMEM(observed.shape, jnp.float32), pltpu.VMEM(receivers.shape, jnp.int32),
            pltpu.VMEM((nx * ny, count), jnp.bfloat16), pltpu.VMEM((2, count, nz), jnp.float32), pltpu.VMEM((count, nz), jnp.float32), field, field,
            dma((15,)), dma((members,)), dma((2 * members, owners)), dma((2 * members, owners)),
            dma((members, peers)), dma((members, peers)), dma((members, peers)), dma((members, peers)),
        ],
        compiler_params=pltpu.CompilerParams(collective_id=0, has_side_effects=True, vmem_limit_bytes=40 * 1024 * 1024),
        cost_estimate=pl.CostEstimate(flops=200_000_000, bytes_accessed=6_000_000, transcendentals=0),
    )(*(pltpu.with_memory_space_constraint(operand, pltpu.HBM) for operand in (
        home, footprints, source_cell, receivers, source_wave, observed,
        velocity.reshape(held, 16, nz), density.reshape(held, 16, nz), zband, yband,
        pressure_old, pressure_now, adjoint_next, adjoint_now,
    )))
    return gradient.reshape(held, 4 // cores, 4, nz)


def solution(mesh):
    whole = P(("grp", "own"), None, None, None)
    fields = P(("grp", "own"), "shot", None, None, None, None)
    in_specs = (
        whole, whole, P("grp"), P("grp", None, None, None),
        P(("grp", "own"), "shot", None),
        P(("grp", "own"), "shot", None, None),
        P(("grp", "own"), "shot", None, None),
        P(("grp", "own"), "shot", None, None, None),
        fields, fields, fields, fields,
    )
    return jax.shard_map(
        per_device, mesh=mesh, in_specs=in_specs,
        out_specs=P(("grp", "own"), "shot", None, None), check_vma=False,
    )
```
